32 devices in a mesh: band: 8 (over z, y), lev: 4 (over x, core).
Axes of the slice: x: 2, y: 2, z: 4, core: 2. Of those that a mesh axis runs over, the one named last changes fastest.
Arguments:
- grid_adjoint: float32 [1024, 64, 2048], P('band', 'lev'), may hold values from -6 to 6
- trajectory: float32 [1024, 64, 2048], P('band', 'lev'), may hold values from -3 to 3
- legendre_north: float32 [512, 512, 512], P(('band', 'lev')), may hold values from -0.25 to 0.25
- slot_wavenumber: int32 [512], replicated, may hold values from 0 to 511, each once
- spectral_state: float32 [512, 512, 2, 64], P(('band', 'lev')), may hold values from -6 to 6
- to_modes: float32 [64, 64], replicated, may hold values from -0.75 to 0.75
- from_modes: float32 [64, 64], replicated, may hold values from -0.75 to 0.75
- rates: float32 [64], replicated, may hold values from 0.1 to 10
Outputs:
- spectral_out: float32 [512, 512, 2, 64], P(('band', 'lev'))
- grid_out: float32 [1024, 64, 2048], P('band', 'lev')
The draws below stay inside these ranges and needn't reach their ends.
Inputs may be any that keep to these rules, and one draw needn't show every extreme that they name: `slot_wavenumber`: each wavenumber stands in exactly one slot.
All inputs are finite; a program needn't handle non-finite values.
Results may differ from the reference program's by a relative error of at most 0.000067.
Values sent between devices are 32-bit elements; how exact they have to be, the bound alone decides.
A program may use at most 192 MiB of HBM per device.

```python
import math
import jax
import jax.numpy as jnp
from jax import lax

M = 512
LAT = 1024
LON = 2048
L = 64
LH = 512


def level_of(key, dims, shards, low, largest):
    factor_of = 1.0
    for axis_at, blocks in shards:
        draws = jax.random.uniform(jax.random.fold_in(jax.random.fold_in(key, 6), axis_at), (blocks,), jnp.float32, low / len(shards), largest / len(shards))
        factor_of = factor_of * jnp.repeat(jnp.exp(draws), dims[axis_at] // blocks).reshape((-1,) + (1,) * (len(dims) - 1 - axis_at))
    return factor_of


def scatter_about(rng, dims, deviation, reach, split=(), kind=jnp.bfloat16):
    entries = jax.random.normal(rng, dims, jnp.float32) * deviation
    if len(split) > 0:
        entries = level_of(rng, dims, split, -0.22, 0.18) * entries
    return jnp.clip(entries, min=-reach, max=reach).astype(kind)


def setup_inputs(seed: int = 0) -> dict:
    key_of = jax.random.split(jax.random.key(seed), 9)
    grid_adjoint = scatter_about(key_of[0], (LAT, L, LON), 1.0, 6.0, ((0, 8), (1, 4)), jnp.float32)
    trajectory = scatter_about(key_of[1], (LAT, L, LON), 0.5, 3.0, ((0, 8), (1, 4)), jnp.float32)
    legendre_north = scatter_about(key_of[2], (M, M, LH), LH ** -0.5, 0.25, ((0, 32),), jnp.float32)
    slot_wavenumber = jax.random.permutation(key_of[3], M).astype(jnp.int32)
    spectral_state = scatter_about(key_of[4], (M, M, 2, L), 1.0, 6.0, ((0, 32),), jnp.float32)
    to_modes = scatter_about(key_of[5], (L, L), L ** -0.5, 0.75, (), jnp.float32)
    from_modes = scatter_about(key_of[6], (L, L), L ** -0.5, 0.75, (), jnp.float32)
    rates = jnp.clip(jnp.exp(jax.random.uniform(key_of[7], (L,), jnp.float32, math.log(0.1), math.log(10.0))), 0.1, 10.0)
    return dict(grid_adjoint=grid_adjoint, trajectory=trajectory, legendre_north=legendre_north, slot_wavenumber=slot_wavenumber, spectral_state=spectral_state, to_modes=to_modes, from_modes=from_modes, rates=rates)


def wave_table():
    column = jnp.arange(LON, dtype=jnp.int32)
    number = jnp.arange(M, dtype=jnp.int32)
    phase = (column[:, None] * number[None, :]) % LON
    angles = phase.astype(jnp.float32) * (2.0 * jnp.pi / LON)
    scale = jnp.float32(LON) ** -0.5
    return jnp.concatenate([jnp.cos(angles), -jnp.sin(angles)], axis=1) * scale


def unfold(north):
    depth = north.shape[0]
    parity = jnp.where(jnp.arange(depth) % 2 == 0, 1.0, -1.0).astype(jnp.float32)
    return jnp.concatenate([north, parity[:, None] * north[:, ::-1]], axis=1)


def reference(grid_adjoint, trajectory, legendre_north, slot_wavenumber, spectral_state, to_modes, from_modes, rates):
    highest = lax.Precision.HIGHEST
    table = wave_table()
    forced = grid_adjoint * (1.0 + trajectory)
    fourier = jnp.dot(forced.reshape(LAT * L, LON), table, precision=highest, preferred_element_type=jnp.float32)
    fourier = fourier.reshape(LAT, L, 2, M)
    slotted = jnp.take(fourier, slot_wavenumber, axis=3)
    columns = jnp.transpose(slotted, (3, 0, 1, 2))

    def analyse(pair):
        north, column_data = pair
        whole = unfold(north)
        return jnp.einsum('kt,tlc->kcl', whole, column_data, precision=highest)

    analysed = lax.map(analyse, (legendre_north, columns))
    depth_index = jnp.arange(M, dtype=jnp.int32)
    valid = (depth_index[None, :] < M - slot_wavenumber[:, None]).astype(jnp.float32)
    total = (analysed + spectral_state) * valid[:, :, None, None]
    degree = (slot_wavenumber[:, None] + depth_index[None, :]).astype(jnp.float32)
    helm = degree * (degree + 1.0) / (M * (M - 1.0))
    modes = jnp.einsum('skcl,pl->skcp', total, to_modes, precision=highest)
    scaled = modes / (1.0 + helm[:, :, None, None] * rates)
    spectral_out = jnp.einsum('skcp,lp->skcl', scaled, from_modes, precision=highest)

    def synthesise(pair):
        north, coeffs = pair
        whole = unfold(north)
        return jnp.einsum('kt,kcl->tlc', whole, coeffs, precision=highest)

    synthesised = lax.map(synthesise, (legendre_north, spectral_out))
    inverse = jnp.zeros((M,), jnp.int32).at[slot_wavenumber].set(jnp.arange(M, dtype=jnp.int32))
    ordered = jnp.transpose(jnp.take(synthesised, inverse, axis=0), (1, 2, 3, 0))
    grid_out = jnp.dot(ordered.reshape(LAT * L, 2 * M), table.T, precision=highest, preferred_element_type=jnp.float32)
    return spectral_out, grid_out.reshape(LAT, L, LON)
```

```python
import functools

import jax
import jax.numpy as jnp
from jax import lax
from jax.experimental import pallas as pl
from jax.experimental.pallas import tpu as pltpu
from jax.sharding import PartitionSpec as P

PRECISION = lax.Precision.HIGH


def angle_parts(steps, waves, longitudes):
    phase = waves[:, None] * steps[None, :] % longitudes
    angles = phase.astype(jnp.float32) * (2.0 * jnp.pi / longitudes)
    return jnp.cos(angles), jnp.sin(angles)


def wave_rows(longitudes, waves, devices):
    fine = min(128, longitudes)
    coarse = longitudes // fine
    scale = jnp.float32(longitudes) ** (-0.5)
    cos_a, sin_a = angle_parts(jnp.arange(coarse, dtype=jnp.int32) * fine, waves, longitudes)
    cos_b, sin_b = angle_parts(jnp.arange(fine, dtype=jnp.int32), waves, longitudes)
    cos_a, sin_a, cos_b, sin_b = lax.optimization_barrier(
        (cos_a * scale, sin_a * scale, cos_b, sin_b)
    )
    cos_at = [cos_a[:, i : i + 1] * cos_b - sin_a[:, i : i + 1] * sin_b for i in range(coarse)]
    sin_at = [-sin_a[:, i : i + 1] * cos_b - cos_a[:, i : i + 1] * sin_b for i in range(coarse)]
    cosine = jnp.concatenate(cos_at, axis=1).reshape(devices, -1, longitudes)
    negsine = jnp.concatenate(sin_at, axis=1).reshape(devices, -1, longitudes)
    return jnp.stack([cosine, negsine], axis=1).reshape(-1, longitudes)


def exchange(data):
    return lax.all_to_all(data, ("band", "lev"), split_axis=0, concat_axis=0, tiled=True)


def plain_shards(
    grid_adjoint,
    trajectory,
    legendre_north,
    slot_wavenumber,
    spectral_state,
    to_modes,
    from_modes,
    rates,
):
    lats, levels, longitudes = grid_adjoint.shape
    slots, depth, half = legendre_north.shape
    bands = lax.axis_size("band")
    parts = lax.axis_size("lev")
    devices = bands * parts
    every = parts * levels
    me = lax.axis_index("band") * parts + lax.axis_index("lev")
    own_waves = lax.dynamic_slice_in_dim(slot_wavenumber, me * slots, slots)
    table = wave_rows(longitudes, slot_wavenumber, devices)
    even_k = jnp.arange(depth, dtype=jnp.int32) % 2 == 0

    forced = grid_adjoint * (1.0 + trajectory)
    rows = jnp.swapaxes(forced, 0, 1).reshape(levels * lats, longitudes)
    fourier = lax.dot_general(
        table, rows, (((1,), (1,)), ((), ())), precision=PRECISION, preferred_element_type=jnp.float32
    )
    arrived = exchange(fourier.reshape(devices, 2 * slots, levels * lats))
    arrived = arrived.reshape(bands, parts, 2, slots, levels, lats)
    arrived = arrived.transpose(3, 2, 1, 4, 0, 5).reshape(slots, 2 * every, bands * lats)
    north = arrived[:, :, :half]
    south = arrived[:, :, half:][:, :, ::-1]
    folded = jnp.concatenate([north + south, north - south], axis=1)
    both = lax.dot_general(
        folded, legendre_north, (((2,), (2,)), ((0,), (0,))), precision=PRECISION,
        preferred_element_type=jnp.float32,
    )
    analysed = jnp.where(even_k, both[:, : 2 * every], both[:, 2 * every :])
    analysed = analysed.reshape(slots, 2, every, depth)

    state = spectral_state.transpose(0, 2, 3, 1)
    depth_index = jnp.arange(depth, dtype=jnp.int32)
    valid = (depth_index[None, :] < depth - own_waves[:, None]).astype(jnp.float32)
    total = (analysed + state) * valid[:, None, None, :]
    degree = (own_waves[:, None] + depth_index[None, :]).astype(jnp.float32)
    helm = degree * (degree + 1.0) / (depth * (depth - 1.0))
    modes = jnp.einsum("sclk,pl->scpk", total, to_modes, precision=PRECISION)
    scaled = modes / (1.0 + helm[:, None, None, :] * rates[None, None, :, None])
    spectral = jnp.einsum("scpk,lp->sclk", scaled, from_modes, precision=PRECISION)

    coeffs = spectral.reshape(slots, 2 * every, depth)
    split = jnp.concatenate(
        [jnp.where(even_k, coeffs, 0.0), jnp.where(even_k, 0.0, coeffs)], axis=1
    )
    halves = lax.dot_general(
        split, legendre_north, (((2,), (1,)), ((0,), (0,))), precision=PRECISION,
        preferred_element_type=jnp.float32,
    )
    first = halves[:, : 2 * every]
    second = halves[:, 2 * every :]
    whole = jnp.concatenate([first + second, (first - second)[:, :, ::-1]], axis=2)
    whole = whole.reshape(slots, 2, parts, levels, bands, lats).transpose(4, 2, 1, 0, 3, 5)
    returned = exchange(whole.reshape(devices, 2 * slots, levels * lats))
    grid = lax.dot_general(
        returned.reshape(devices * 2 * slots, levels, lats),
        table,
        (((0,), (0,)), ((), ())),
        precision=PRECISION,
        preferred_element_type=jnp.float32,
    )
    return spectral.transpose(0, 3, 1, 2), jnp.swapaxes(grid, 0, 1)


LANES = 128
SUB = 8
PAIR = 2
PIECES = 8
NN = (((1,), (0,)), ((), ()))
NT = (((1,), (1,)), ((), ()))


def halves_of(x):
    high = x.astype(jnp.bfloat16)
    low = (x - high.astype(jnp.float32)).astype(jnp.bfloat16)
    return high, low


def dot3(a, b, dims):
    def one(x, y):
        return lax.dot_general(x, y, dims, preferred_element_type=jnp.float32)

    return one(a[0], b[0]) + (one(a[0], b[1]) + one(a[1], b[0]))


def fill_table(p_ref, q_ref, cos_ref, sin_ref, high, low):
    rows, longitudes = high.shape
    block = min(64, rows)

    def body(r, carry):
        at = pl.ds(pl.multiple_of(r * block, block), block)
        p, q, c, s = p_ref[at, :], q_ref[at, :], cos_ref[at, :], sin_ref[at, :]
        for i in range(longitudes // LANES):
            h, l = halves_of(p[:, i : i + 1] * c + q[:, i : i + 1] * s)
            high[at, i * LANES : (i + 1) * LANES] = h
            low[at, i * LANES : (i + 1) * LANES] = l
        return carry

    lax.fori_loop(0, rows // block, body, 0)


def forward_kernel(
    dims,
    grid_ref, traj_ref, p_ref, q_ref, cos_ref, sin_ref, leg_ref, state_ref,
    valid_ref, helm_ref, rate_ref, into_ref, outof_ref, back_ref,
    spec_out, returned,
    high, low, forced, stage, traj, rows_h, rows_l, sending, arrived, synth, leg, state, spec,
    grid_sem, traj_sem, send_sem, recv_sem, send2_sem, recv2_sem, leg_sem, state_sem, spec_sem,
):
    bands, parts, lats, levels, longitudes, slots, depth, half = dims
    devices = bands * parts
    every = parts * levels
    pairs = levels // PAIR
    unit = 2 * slots
    message = PAIR * unit
    band, lev = lax.axis_index("band"), lax.axis_index("lev")
    me = band * parts + lev
    south = band >= bands // 2

    def mesh_id(d):
        return (d // parts, lax.rem(d, parts))

    barrier = pltpu.get_barrier_semaphore()

    def greet(i, carry):
        pl.semaphore_signal(
            barrier, inc=1, device_id=mesh_id(jnp.bitwise_xor(me, i)),
            device_id_type=pl.DeviceIdType.MESH,
        )
        return carry

    lax.fori_loop(1, devices, greet, 0)

    span = lats // PIECES
    count = (levels // SUB) * PIECES

    def load_copies(piece):
        block, part = piece // PIECES, lax.rem(piece, PIECES)
        lat = pl.ds(pl.multiple_of(part * span, span), span)
        cut = pl.ds(pl.multiple_of(block * SUB, SUB), SUB)
        slot = lax.rem(piece, 2)
        return (
            pltpu.make_async_copy(grid_ref.at[lat, cut, :], stage.at[slot], grid_sem.at[slot]),
            pltpu.make_async_copy(traj_ref.at[lat, cut, :], traj.at[slot], traj_sem.at[slot]),
        )

    def load_piece(piece):
        for copy in load_copies(piece):
            copy.start()

    def finish_piece(piece):
        block, part = piece // PIECES, lax.rem(piece, PIECES)
        slot = lax.rem(piece, 2)
        for copy in load_copies(piece):
            copy.wait()

        def body(i, carry):
            at = part * span + i
            lat = jnp.where(south, lats - 1 - at, at)
            to = pl.ds(pl.multiple_of((block * lats + lat) * SUB, SUB), SUB)
            x = stage[slot, i] * (1.0 + traj[slot, i])
            for j in range(longitudes // LANES):
                forced[j, to, :] = x[:, j * LANES : (j + 1) * LANES]
            return carry

        lax.fori_loop(0, span, body, 0)

        @pl.when(piece + 2 < count)
        def _():
            load_piece(piece + 2)

    load_piece(jnp.int32(0))
    load_piece(jnp.int32(1))

    def leg_copy(s, slot):
        return pltpu.make_async_copy(leg_ref.at[s], leg.at[slot], leg_sem.at[slot])

    def state_copy(s, slot):
        return pltpu.make_async_copy(state_ref.at[s], state.at[slot], state_sem.at[slot])

    fill_table(p_ref, q_ref, cos_ref, sin_ref, high, low)
    tall = min(256, devices * unit)

    def send_copy(q, d):
        return pltpu.make_async_remote_copy(
            src_ref=sending.at[pl.ds(pl.multiple_of((q * devices + d) * message, SUB), message), :],
            dst_ref=arrived.at[pl.ds(pl.multiple_of((me * pairs + q) * message, SUB), message), :],
            send_sem=send_sem,
            recv_sem=recv_sem,
            device_id=mesh_id(d),
            device_id_type=pl.DeviceIdType.MESH,
        )

    def transform(q):
        first = q * PAIR
        block, local = first // SUB, lax.rem(first, SUB)
        for h in range(PAIR):
            for i in range(longitudes // LANES):
                x = forced[i, pl.ds(block * lats * SUB + local + h, lats, stride=SUB), :]
                rh, rl = halves_of(x)
                rows_h[h * lats : (h + 1) * lats, i * LANES : (i + 1) * LANES] = rh
                rows_l[h * lats : (h + 1) * lats, i * LANES : (i + 1) * LANES] = rl

        def body(r, carry):
            at = pl.ds(pl.multiple_of(r * tall, tall), tall)
            got = dot3((high[at, :], low[at, :]), (rows_h[...], rows_l[...]), NT)
            first = (q * devices + r * (tall // unit)) * message
            for d in range(tall // unit):
                for h in range(PAIR):
                    to = pl.multiple_of(first + (d * PAIR + h) * unit, SUB)
                    sending[pl.ds(to, unit), :] = got[
                        d * unit : (d + 1) * unit, h * lats : (h + 1) * lats
                    ]
            return carry

        lax.fori_loop(0, devices * unit // tall, body, 0)

    def send_pair(q):
        def body(i, carry):
            send_copy(q, jnp.bitwise_xor(me, devices - 1 - i)).start()
            return carry

        lax.fori_loop(0, devices - 1, body, 0)
        pltpu.make_async_copy(
            sending.at[pl.ds(pl.multiple_of((q * devices + me) * message, SUB), message), :],
            arrived.at[pl.ds(pl.multiple_of((me * pairs + q) * message, SUB), message), :],
            recv_sem,
        ).start()

    per = SUB // PAIR

    def outer(block, carry):
        def finish(i, c):
            finish_piece(block * PIECES + i)
            return c

        lax.fori_loop(0, PIECES, finish, 0)

        def run(j, c):
            q = block * per + j
            transform(q)

            @pl.when(q == 0)
            def _():
                pl.semaphore_wait(barrier, devices - 1)

            send_pair(q)
            return c

        lax.fori_loop(0, per, run, 0)
        return carry

    lax.fori_loop(0, levels // SUB, outer, 0)

    leg_copy(0, 0).start()
    state_copy(0, 0).start()
    pltpu.make_async_copy(arrived, arrived, recv_sem).wait()

    lane = lax.broadcasted_iota(jnp.int32, (2 * every, depth), 1)
    even = lax.rem(lane, 2) == 0
    folds = bands // 2

    def column(b, s):
        return jnp.concatenate(
            [
                arrived[pl.ds(b * every * unit + 2 * s + c, every, stride=unit), :]
                for c in range(2)
            ],
            axis=0,
        )

    def send2_copy(s, d):
        return pltpu.make_async_remote_copy(
            src_ref=synth.at[pl.ds(pl.multiple_of((s * devices + d) * 2 * levels, SUB), 2 * levels), :],
            dst_ref=returned.at[pl.ds(pl.multiple_of((me * slots + s) * 2 * levels, SUB), 2 * levels), :],
            send_sem=send2_sem,
            recv_sem=recv2_sem,
            device_id=mesh_id(d),
            device_id_type=pl.DeviceIdType.MESH,
        )

    def one_slot(s, carry):
        slot = lax.rem(s, 2)

        @pl.when(s + 1 < slots)
        def _():
            leg_copy(s + 1, 1 - slot).start()
            state_copy(s + 1, 1 - slot).start()

        leg_copy(s, slot).wait()
        state_copy(s, slot).wait()
        functions = halves_of(leg[slot])
        evens, odds = [], []
        for b in range(folds):
            n, o = column(b, s), column(bands - 1 - b, s)
            evens.append(n + o)
            odds.append(n - o)
        folded = jnp.concatenate(
            [jnp.concatenate(evens, axis=1), jnp.concatenate(odds, axis=1)], axis=0
        )
        both = dot3(halves_of(folded), functions, NT)
        analysed = jnp.where(even, both[: 2 * every], both[2 * every :])
        row = pl.ds(s, 1)
        total = (analysed + state[slot]) * valid_ref[row, :]
        modes = dot3(halves_of(into_ref[...]), halves_of(total), NN)
        scaled = modes / (1.0 + helm_ref[row, :] * rate_ref[:, 0:1])
        scaled = halves_of(scaled)

        @pl.when(s >= 2)
        def _():
            pltpu.make_async_copy(spec.at[slot], spec_out.at[s - 2], spec_sem.at[slot]).wait()

        spec[slot] = dot3(halves_of(outof_ref[...]), scaled, NN)
        pltpu.make_async_copy(spec.at[slot], spec_out.at[s], spec_sem.at[slot]).start()
        coeffs = dot3(halves_of(back_ref[...]), scaled, NN)
        split = jnp.concatenate(
            [jnp.where(even, coeffs, 0.0), jnp.where(even, 0.0, coeffs)], axis=0
        )
        parts_of = dot3(halves_of(split), functions, NN)
        first, second = parts_of[: 2 * every], parts_of[2 * every :]
        north, other = first + second, first - second
        base = s * devices * 2 * levels
        for b in range(folds):
            cut = slice(b * LANES, (b + 1) * LANES)
            to = pl.multiple_of(base + b * 2 * every, SUB)
            synth[pl.ds(to, 2 * every), :] = north[:, cut]
            to = pl.multiple_of(base + (bands - 1 - b) * 2 * every, SUB)
            synth[pl.ds(to, 2 * every), :] = other[:, cut]

        def body(i, c):
            send2_copy(s, jnp.bitwise_xor(me, devices - 1 - i)).start()
            return c

        lax.fori_loop(0, devices - 1, body, 0)
        pltpu.make_async_copy(
            synth.at[pl.ds(pl.multiple_of((s * devices + me) * 2 * levels, SUB), 2 * levels), :],
            returned.at[pl.ds(pl.multiple_of((me * slots + s) * 2 * levels, SUB), 2 * levels), :],
            recv2_sem,
        ).start()
        return carry

    lax.fori_loop(0, slots, one_slot, 0)
    for s in range(max(slots - 2, 0), slots):
        pltpu.make_async_copy(spec.at[s % 2], spec_out.at[s], spec_sem.at[s % 2]).wait()
    sent = pl.ds(0, pairs * (devices - 1) * message)
    pltpu.make_async_copy(sending.at[sent, :], sending.at[sent, :], send_sem).wait()
    sent = pl.ds(0, slots * (devices - 1) * 2 * levels)
    pltpu.make_async_copy(synth.at[sent, :], synth.at[sent, :], send2_sem).wait()
    pltpu.make_async_copy(returned, returned, recv2_sem).wait()


def inverse_kernel(
    dims, returned, p_ref, q_ref, cos_ref, sin_ref, grid_out,
    high, low, arrived, turned, rows_h, rows_l, result, in_sem, out_sem,
):
    bands, parts, lats, levels, longitudes, slots, depth, half = dims
    south = lax.axis_index("band") >= bands // 2
    waves = bands * parts * slots * 2
    step = waves // PIECES
    blocks = step // LANES

    def load(i):
        at = pl.ds(pl.multiple_of(i * step * levels, SUB), step * levels)
        return pltpu.make_async_copy(returned.at[at, :], arrived.at[at, :], in_sem.at[i])

    for i in range(PIECES):
        load(i).start()
    fill_table(p_ref, q_ref, cos_ref, sin_ref, high, low)
    for i in range(PIECES):
        load(i).wait()

        def pull(l, carry):
            x = arrived[pl.ds(i * step * levels + l, step, stride=levels), :].T
            for j in range(blocks):
                turned[i * blocks + j, pl.ds(l, lats, stride=levels), :] = x[
                    :, j * LANES : (j + 1) * LANES
                ]
            return carry

        lax.fori_loop(0, levels, pull, 0)

        def split(r, carry):
            lat = jnp.where(south, lats - 1 - r, r)
            at = pl.ds(pl.multiple_of(lat * levels, levels), levels)
            to = pl.ds(pl.multiple_of(r * levels, levels), levels)
            for j in range(blocks):
                k = i * blocks + j
                h, l = halves_of(turned[k, at, :])
                rows_h[to, k * LANES : (k + 1) * LANES] = h
                rows_l[to, k * LANES : (k + 1) * LANES] = l
            return carry

        lax.fori_loop(0, lats, split, 0)
    wide = 256
    span = lats // PIECES

    def out_copy(block, slot):
        return pltpu.make_async_copy(
            result.at[slot],
            grid_out.at[pl.ds(pl.multiple_of(block * span, span), span), :, :],
            out_sem.at[slot],
        )

    def outer(block, carry):
        slot = lax.rem(block, 2)

        @pl.when(block >= 2)
        def _():
            out_copy(block - 2, slot).wait()

        at = pl.ds(pl.multiple_of(block * span * levels, levels), span * levels)

        def inner(w, c):
            to = pl.ds(pl.multiple_of(w * wide, wide), wide)
            got = dot3((rows_h[at, :], rows_l[at, :]), (high[:, to], low[:, to]), NN)
            result[slot, :, :, to] = got.reshape(span, levels, wide)
            return c

        lax.fori_loop(0, longitudes // wide, inner, 0)
        out_copy(block, slot).start()
        return carry

    lax.fori_loop(0, PIECES, outer, 0)
    for block in range(PIECES - 2, PIECES):
        out_copy(block, block % 2).wait()


def shards(
    grid_adjoint, trajectory, legendre_north, slot_wavenumber, spectral_state,
    to_modes, from_modes, rates,
):
    lats, levels, longitudes = grid_adjoint.shape
    slots, depth, half = legendre_north.shape
    bands = lax.axis_size("band")
    parts = lax.axis_size("lev")
    devices = bands * parts
    every = parts * levels
    fits = (
        lats == LANES and levels % SUB == 0 and longitudes % (2 * LANES) == 0
        and bands % 2 == 0 and half == bands // 2 * lats and depth % LANES == 0
        and (2 * slots) % SUB == 0 and every == to_modes.shape[0]
        and devices & (devices - 1) == 0 and (devices * 2 * slots) % 256 == 0
    )
    if not fits:
        return plain_shards(
            grid_adjoint, trajectory, legendre_north, slot_wavenumber, spectral_state,
            to_modes, from_modes, rates,
        )
    dims = (bands, parts, lats, levels, longitudes, slots, depth, half)
    me = lax.axis_index("band") * parts + lax.axis_index("lev")
    own = lax.dynamic_slice_in_dim(slot_wavenumber, me * slots, slots)

    scale = jnp.float32(longitudes) ** (-0.5)
    coarse = longitudes // LANES
    cos_a, sin_a = angle_parts(jnp.arange(coarse, dtype=jnp.int32) * LANES, slot_wavenumber, longitudes)
    cos_b, sin_b = angle_parts(jnp.arange(LANES, dtype=jnp.int32), slot_wavenumber, longitudes)
    cos_a, sin_a = cos_a * scale, sin_a * scale
    waves = devices * slots * 2
    p = jnp.stack([cos_a, -sin_a], axis=1).reshape(waves, coarse)
    q = jnp.stack([-sin_a, -cos_a], axis=1).reshape(waves, coarse)
    cos_b = jnp.repeat(cos_b, 2, axis=0)
    sin_b = jnp.repeat(sin_b, 2, axis=0)

    depth_index = jnp.arange(depth, dtype=jnp.int32)
    valid = (depth_index[None, :] < depth - own[:, None]).astype(jnp.float32)
    degree = (own[:, None] + depth_index[None, :]).astype(jnp.float32)
    helm = degree * (degree + 1.0) / (depth * (depth - 1.0))
    rate = jnp.broadcast_to(jnp.tile(rates, 2)[:, None], (2 * every, LANES))

    eye = jnp.eye(2, dtype=jnp.float32)
    natural = (eye[:, None, :, None] * to_modes[None, :, None, :]).reshape(2 * every, 2 * every)
    outof = (eye[:, None, :, None] * from_modes[None, :, None, :]).reshape(2 * every, 2 * every)
    back = outof.reshape(2, parts, levels, 2 * every).transpose(1, 0, 2, 3).reshape(2 * every, 2 * every)
    hbm = pl.BlockSpec(memory_space=pl.ANY)
    vmem = pl.BlockSpec(memory_space=pltpu.VMEM)
    f32, bf16 = jnp.float32, jnp.bfloat16
    dma = pltpu.SemaphoreType.DMA
    state = spectral_state.transpose(0, 2, 3, 1).reshape(slots, 2 * every, depth)
    spectral, returned = pl.pallas_call(
        functools.partial(forward_kernel, dims),
        out_shape=(
            jax.ShapeDtypeStruct((slots, 2 * every, depth), f32),
            jax.ShapeDtypeStruct((waves * levels, lats), f32),
        ),
        in_specs=[hbm, hbm] + [vmem] * 4 + [hbm, hbm] + [vmem] * 6,
        out_specs=(hbm, hbm),
        scratch_shapes=[
            pltpu.VMEM((waves, longitudes), bf16),
            pltpu.VMEM((waves, longitudes), bf16),
            pltpu.VMEM((longitudes // LANES, levels * lats, LANES), f32),
            pltpu.VMEM((2, lats // PIECES, SUB, longitudes), f32),
            pltpu.VMEM((2, lats // PIECES, SUB, longitudes), f32),
            pltpu.VMEM((PAIR * lats, longitudes), bf16),
            pltpu.VMEM((PAIR * lats, longitudes), bf16),
            pltpu.VMEM((levels * waves, lats), f32),
            pltpu.VMEM((levels * waves, lats), f32),
            pltpu.VMEM((waves * levels, lats), f32),
            pltpu.VMEM((2, depth, half), f32),
            pltpu.VMEM((2, 2 * every, depth), f32),
            pltpu.VMEM((2, 2 * every, depth), f32),
            dma((2,)), dma((2,)), dma, dma, dma, dma, dma((2,)), dma((2,)), dma((2,)),
        ],
        compiler_params=pltpu.CompilerParams(
            collective_id=0, has_side_effects=True, vmem_limit_bytes=67_043_328
        ),
        name="spectral",
    )(
        grid_adjoint, trajectory, p, q, cos_b, sin_b, legendre_north, state,
        valid, helm, rate, natural, outof, back,
    )
    grid = pl.pallas_call(
        functools.partial(inverse_kernel, dims),
        out_shape=jax.ShapeDtypeStruct(grid_adjoint.shape, f32),
        in_specs=[hbm] + [vmem] * 4,
        out_specs=hbm,
        scratch_shapes=[
            pltpu.VMEM((waves, longitudes), bf16),
            pltpu.VMEM((waves, longitudes), bf16),
            pltpu.VMEM((waves * levels, lats), f32),
            pltpu.VMEM((waves // LANES, lats * levels, LANES), f32),
            pltpu.VMEM((levels * lats, waves), bf16),
            pltpu.VMEM((levels * lats, waves), bf16),
            pltpu.VMEM((2, lats // PIECES, levels, longitudes), f32),
            dma((PIECES,)), dma((2,)),
        ],
        compiler_params=pltpu.CompilerParams(vmem_limit_bytes=67_043_328),
        name="synthesis",
    )(returned, p, q, cos_b, sin_b)
    return spectral.reshape(slots, 2, every, depth).transpose(0, 3, 1, 2), grid


def solution(mesh):
    return jax.shard_map(
        shards,
        mesh=mesh,
        in_specs=(
            P("band", "lev", None),
            P("band", "lev", None),
            P(("band", "lev"), None, None),
            P(),
            P(("band", "lev"), None, None, None),
            P(),
            P(),
            P(),
        ),
        out_specs=(P(("band", "lev"), None, None, None), P("band", "lev", None)),
        check_vma=False,
    )
```

```python
import functools
import math

import jax
import jax.numpy as jnp
from jax import lax
from jax.experimental import pallas as pl
from jax.experimental.pallas import tpu as pltpu
from jax.sharding import PartitionSpec as P

PRECISION = lax.Precision.HIGH


def angle_parts(steps, waves, longitudes):
    phase = waves[:, None] * steps[None, :] % longitudes
    angles = phase.astype(jnp.float32) * (2.0 * jnp.pi / longitudes)
    return jnp.cos(angles), jnp.sin(angles)


def wave_rows(longitudes, waves, devices):
    fine = min(128, longitudes)
    coarse = longitudes // fine
    scale = jnp.float32(longitudes) ** (-0.5)
    cos_a, sin_a = angle_parts(jnp.arange(coarse, dtype=jnp.int32) * fine, waves, longitudes)
    cos_b, sin_b = angle_parts(jnp.arange(fine, dtype=jnp.int32), waves, longitudes)
    cos_a, sin_a, cos_b, sin_b = lax.optimization_barrier(
        (cos_a * scale, sin_a * scale, cos_b, sin_b)
    )
    cos_at = [cos_a[:, i : i + 1] * cos_b - sin_a[:, i : i + 1] * sin_b for i in range(coarse)]
    sin_at = [-sin_a[:, i : i + 1] * cos_b - cos_a[:, i : i + 1] * sin_b for i in range(coarse)]
    cosine = jnp.concatenate(cos_at, axis=1).reshape(devices, -1, longitudes)
    negsine = jnp.concatenate(sin_at, axis=1).reshape(devices, -1, longitudes)
    return jnp.stack([cosine, negsine], axis=1).reshape(-1, longitudes)


def exchange(data):
    return lax.all_to_all(data, ("band", "lev"), split_axis=0, concat_axis=0, tiled=True)


def plain_shards(
    grid_adjoint,
    trajectory,
    legendre_north,
    slot_wavenumber,
    spectral_state,
    to_modes,
    from_modes,
    rates,
):
    lats, levels, longitudes = grid_adjoint.shape
    slots, depth, half = legendre_north.shape
    bands = lax.axis_size("band")
    parts = lax.axis_size("lev")
    devices = bands * parts
    every = parts * levels
    me = lax.axis_index("band") * parts + lax.axis_index("lev")
    own_waves = lax.dynamic_slice_in_dim(slot_wavenumber, me * slots, slots)
    table = wave_rows(longitudes, slot_wavenumber, devices)
    even_k = jnp.arange(depth, dtype=jnp.int32) % 2 == 0

    forced = grid_adjoint * (1.0 + trajectory)
    rows = jnp.swapaxes(forced, 0, 1).reshape(levels * lats, longitudes)
    fourier = lax.dot_general(
        table, rows, (((1,), (1,)), ((), ())), precision=PRECISION, preferred_element_type=jnp.float32
    )
    arrived = exchange(fourier.reshape(devices, 2 * slots, levels * lats))
    arrived = arrived.reshape(bands, parts, 2, slots, levels, lats)
    arrived = arrived.transpose(3, 2, 1, 4, 0, 5).reshape(slots, 2 * every, bands * lats)
    north = arrived[:, :, :half]
    south = arrived[:, :, half:][:, :, ::-1]
    folded = jnp.concatenate([north + south, north - south], axis=1)
    both = lax.dot_general(
        folded, legendre_north, (((2,), (2,)), ((0,), (0,))), precision=PRECISION,
        preferred_element_type=jnp.float32,
    )
    analysed = jnp.where(even_k, both[:, : 2 * every], both[:, 2 * every :])
    analysed = analysed.reshape(slots, 2, every, depth)

    state = spectral_state.transpose(0, 2, 3, 1)
    depth_index = jnp.arange(depth, dtype=jnp.int32)
    valid = (depth_index[None, :] < depth - own_waves[:, None]).astype(jnp.float32)
    total = (analysed + state) * valid[:, None, None, :]
    degree = (own_waves[:, None] + depth_index[None, :]).astype(jnp.float32)
    helm = degree * (degree + 1.0) / (depth * (depth - 1.0))
    modes = jnp.einsum("sclk,pl->scpk", total, to_modes, precision=PRECISION)
    scaled = modes / (1.0 + helm[:, None, None, :] * rates[None, None, :, None])
    spectral = jnp.einsum("scpk,lp->sclk", scaled, from_modes, precision=PRECISION)

    coeffs = spectral.reshape(slots, 2 * every, depth)
    split = jnp.concatenate(
        [jnp.where(even_k, coeffs, 0.0), jnp.where(even_k, 0.0, coeffs)], axis=1
    )
    halves = lax.dot_general(
        split, legendre_north, (((2,), (1,)), ((0,), (0,))), precision=PRECISION,
        preferred_element_type=jnp.float32,
    )
    first = halves[:, : 2 * every]
    second = halves[:, 2 * every :]
    whole = jnp.concatenate([first + second, (first - second)[:, :, ::-1]], axis=2)
    whole = whole.reshape(slots, 2, parts, levels, bands, lats).transpose(4, 2, 1, 0, 3, 5)
    returned = exchange(whole.reshape(devices, 2 * slots, levels * lats))
    grid = lax.dot_general(
        returned.reshape(devices * 2 * slots, levels, lats),
        table,
        (((0,), (0,)), ((), ())),
        precision=PRECISION,
        preferred_element_type=jnp.float32,
    )
    return spectral.transpose(0, 3, 1, 2), jnp.swapaxes(grid, 0, 1)


LANES = 128
SUB = 8
PAIR = 2
PIECES = 8
GROUP = 4
NN = (((1,), (0,)), ((), ()))
NT = (((1,), (1,)), ((), ()))


def halves_of(x):
    high = x.astype(jnp.bfloat16)
    low = (x - high.astype(jnp.float32)).astype(jnp.bfloat16)
    return high, low


def dot1(x, y, dims):
    return lax.dot_general(x, y, dims, preferred_element_type=jnp.float32)


def dot3(a, b, dims):
    return dot1(a[0], b[0], dims) + (dot1(a[0], b[1], dims) + dot1(a[1], b[0], dims))


def aligned(start, size):
    return pl.ds(pl.multiple_of(start, size & -size), size)


def circle(phase, longitudes):
    quarter = longitudes // 4
    quadrant = phase // quarter
    rest = phase - quadrant * quarter
    flip = rest > quarter // 2
    angle = jnp.where(flip, quarter - rest, rest).astype(jnp.float32) * (
        2.0 * math.pi / longitudes
    )
    z = angle * angle
    sine = angle * (
        1.0 + z * (-1 / 6 + z * (1 / 120 + z * (-1 / 5040 + z * (1 / 362880))))
    )
    cosine = 1.0 + z * (
        -0.5 + z * (1 / 24 + z * (-1 / 720 + z * (1 / 40320 + z * (-1 / 3628800))))
    )
    c, s = jnp.where(flip, sine, cosine), jnp.where(flip, cosine, sine)
    odd = lax.rem(quadrant, 2) == 1
    c, s = jnp.where(odd, s, c), jnp.where(odd, c, s)
    c = jnp.where((quadrant == 1) | (quadrant == 2), -c, c)
    return c, jnp.where(quadrant >= 2, -s, s)


def table_rows(waves, imaginary, longitudes):
    column = lax.broadcasted_iota(jnp.int32, waves.shape, 1)
    ca, sa = circle(lax.rem(waves * (column * LANES), longitudes), longitudes)
    cb, sb = circle(lax.rem(waves * column, longitudes), longitudes)
    scale = float(longitudes) ** -0.5
    ca, sa = ca * scale, sa * scale
    p = jnp.where(imaginary, -sa, ca)
    q = jnp.where(imaginary, -ca, -sa)
    return [
        halves_of(p[:, i : i + 1] * cb + q[:, i : i + 1] * sb)
        for i in range(longitudes // LANES)
    ]


def forward_kernel(
    dims,
    grid_ref, traj_ref, wave_ref, leg_ref, state_ref, rate_ref, to_ref, from_ref,
    spec_out, returned, partial,
    high, low, forced, stage, traj, rows_h, rows_l, sending, arrived, synth, leg, state, spec,
    into, outof, back, pulled, turned,
    grid_sem, traj_sem, send_sem, recv_sem, send2_sem, recv2_sem, leg_sem, state_sem, spec_sem,
    pull_sem, part_sem,
):
    bands, parts, lats, levels, longitudes, slots, depth, half = dims
    devices = bands * parts
    every = parts * levels
    pairs = levels // PAIR
    unit = 2 * slots
    message = PAIR * unit
    small = 2 * GROUP
    tall = devices * small
    groups = slots // GROUP
    wide = longitudes // LANES
    band, lev = lax.axis_index("band"), lax.axis_index("lev")
    me = band * parts + lev
    south = band >= bands // 2

    def mesh_id(d):
        return (d // parts, lax.rem(d, parts))

    barrier = pltpu.get_barrier_semaphore()

    def greet(i, carry):
        pl.semaphore_signal(
            barrier, inc=1, device_id=mesh_id(jnp.bitwise_xor(me, i)),
            device_id_type=pl.DeviceIdType.MESH,
        )
        return carry

    lax.fori_loop(1, devices, greet, 0)

    span = lats // PIECES
    count = (levels // SUB) * PIECES

    def load_copies(piece):
        block, part = piece // PIECES, lax.rem(piece, PIECES)
        lat = aligned(part * span, span)
        cut = aligned(block * SUB, SUB)
        slot = lax.rem(piece, 2)
        return (
            pltpu.make_async_copy(grid_ref.at[lat, cut, :], stage.at[slot], grid_sem.at[slot]),
            pltpu.make_async_copy(traj_ref.at[lat, cut, :], traj.at[slot], traj_sem.at[slot]),
        )

    def load_piece(piece):
        for copy in load_copies(piece):
            copy.start()

    def finish_piece(piece):
        block, part = piece // PIECES, lax.rem(piece, PIECES)
        slot = lax.rem(piece, 2)
        for copy in load_copies(piece):
            copy.wait()

        def body(i, carry):
            at = part * span + i
            lat = jnp.where(south, lats - 1 - at, at)
            to = aligned((block * lats + lat) * SUB, SUB)
            x = stage[slot, i] * (1.0 + traj[slot, i])
            for j in range(wide):
                forced[j, to, :] = x[:, j * LANES : (j + 1) * LANES]
            return carry

        lax.fori_loop(0, span, body, 0)

        @pl.when(piece + 2 < count)
        def _():
            load_piece(piece + 2)

    load_piece(jnp.int32(0))
    load_piece(jnp.int32(1))

    def leg_copy(s, slot):
        return pltpu.make_async_copy(leg_ref.at[s], leg.at[slot], leg_sem.at[slot])

    def state_copy(s, slot):
        return pltpu.make_async_copy(state_ref.at[s], state.at[slot], state_sem.at[slot])

    block_rows = 64

    def fill(r, carry):
        at = aligned(r * block_rows, block_rows)
        waves = wave_ref[at, :]
        imaginary = lax.rem(lax.broadcasted_iota(jnp.int32, waves.shape, 0), 2) == 1
        for i, (h, l) in enumerate(table_rows(waves, imaginary, longitudes)):
            high[at, i * LANES : (i + 1) * LANES] = h
            low[at, i * LANES : (i + 1) * LANES] = l
        return carry

    lax.fori_loop(0, devices * unit // block_rows, fill, 0)
    for m in (into, outof, back):
        m[...] = jnp.zeros_like(m)
    for c in range(2):
        cut = slice(c * every, (c + 1) * every)
        into[cut, cut] = to_ref[...]
        outof[cut, cut] = from_ref[...]
        for p in range(parts):
            at = (2 * p + c) * levels
            back[at : at + levels, cut] = from_ref[p * levels : (p + 1) * levels, :]

    def send_copy(q, d):
        return pltpu.make_async_remote_copy(
            src_ref=sending.at[aligned((q * devices + d) * message, message), :],
            dst_ref=arrived.at[aligned((me * pairs + q) * message, message), :],
            send_sem=send_sem,
            recv_sem=recv_sem,
            device_id=mesh_id(d),
            device_id_type=pl.DeviceIdType.MESH,
        )

    def transform(q):
        first = q * PAIR
        block, local = first // SUB, lax.rem(first, SUB)
        for h in range(PAIR):
            for i in range(wide):
                x = forced[i, pl.ds(block * lats * SUB + local + h, lats, stride=SUB), :]
                rh, rl = halves_of(x)
                rows_h[h * lats : (h + 1) * lats, i * LANES : (i + 1) * LANES] = rh
                rows_l[h * lats : (h + 1) * lats, i * LANES : (i + 1) * LANES] = rl

        def body(r, carry):
            at = aligned(r * tall, tall)
            got = dot3((high[at, :], low[at, :]), (rows_h[...], rows_l[...]), NT)
            for d in range(devices):
                for h in range(PAIR):
                    to = (q * devices + d) * message + h * unit + r * small
                    sending[aligned(to, small), :] = got[
                        d * small : (d + 1) * small, h * lats : (h + 1) * lats
                    ]
            return carry

        lax.fori_loop(0, groups, body, 0)

    def send_pair(q):
        def body(i, carry):
            send_copy(q, jnp.bitwise_xor(me, devices - 1 - i)).start()
            return carry

        lax.fori_loop(0, devices - 1, body, 0)
        pltpu.make_async_copy(
            sending.at[aligned((q * devices + me) * message, message), :],
            arrived.at[aligned((me * pairs + q) * message, message), :],
            recv_sem,
        ).start()

    per = SUB // PAIR

    def outer(block, carry):
        def finish(i, c):
            finish_piece(block * PIECES + i)
            return c

        lax.fori_loop(0, PIECES, finish, 0)

        def run(j, c):
            q = block * per + j
            transform(q)

            @pl.when(q == 0)
            def _():
                pl.semaphore_wait(barrier, devices - 1)

            send_pair(q)
            return c

        lax.fori_loop(0, per, run, 0)
        return carry

    lax.fori_loop(0, levels // SUB, outer, 0)

    leg_copy(0, 0).start()
    state_copy(0, 0).start()
    pltpu.make_async_copy(arrived, arrived, recv_sem).wait()

    lane = lax.broadcasted_iota(jnp.int32, (2 * every, depth), 1)
    even = lax.rem(lane, 2) == 0
    folds = bands // 2
    each = 2 * levels

    def column(b, s):
        return jnp.concatenate(
            [
                arrived[pl.ds(b * every * unit + 2 * s + c, every, stride=unit), :]
                for c in range(2)
            ],
            axis=0,
        )

    def send2_copy(s, d, sem):
        return pltpu.make_async_remote_copy(
            src_ref=synth.at[aligned((s * devices + d) * each, each), :],
            dst_ref=returned.at[me, aligned(s * each, each), :],
            send_sem=send2_sem,
            recv_sem=recv2_sem.at[sem],
            device_id=mesh_id(d),
            device_id_type=pl.DeviceIdType.MESH,
        )

    def one_slot(s, carry):
        slot = lax.rem(s, 2)
        sem = jnp.where(s == slots - 1, groups, s // GROUP)

        @pl.when(s + 1 < slots)
        def _():
            leg_copy(s + 1, 1 - slot).start()
            state_copy(s + 1, 1 - slot).start()

        leg_copy(s, slot).wait()
        state_copy(s, slot).wait()
        functions = halves_of(leg[slot])
        evens, odds = [], []
        for b in range(folds):
            n, o = column(b, s), column(bands - 1 - b, s)
            evens.append(n + o)
            odds.append(n - o)
        folded = jnp.concatenate(
            [jnp.concatenate(evens, axis=1), jnp.concatenate(odds, axis=1)], axis=0
        )
        both = dot3(halves_of(folded), functions, NT)
        analysed = jnp.where(even, both[: 2 * every], both[2 * every :])
        wave = wave_ref[
            pl.ds((s // GROUP * devices + me) * small + lax.rem(s, GROUP) * 2, 1), :
        ]
        wave = jnp.concatenate([wave] * (depth // LANES), axis=1)
        order = lax.broadcasted_iota(jnp.int32, (1, depth), 1)
        degree = (wave + order).astype(jnp.float32)
        helm = degree * (degree + 1.0) / (depth * (depth - 1.0))
        total = jnp.where(order < depth - wave, analysed + state[slot], 0.0)
        modes = dot3(halves_of(into[...]), halves_of(total), NN)
        scaled = halves_of(modes / (1.0 + helm * rate_ref[:, 0:1]))

        @pl.when(s >= 2)
        def _():
            pltpu.make_async_copy(spec.at[slot], spec_out.at[s - 2], spec_sem.at[slot]).wait()

        spec[slot] = dot3(halves_of(outof[...]), scaled, NN)
        pltpu.make_async_copy(spec.at[slot], spec_out.at[s], spec_sem.at[slot]).start()
        coeffs = dot3(halves_of(back[...]), scaled, NN)
        split = jnp.concatenate(
            [jnp.where(even, coeffs, 0.0), jnp.where(even, 0.0, coeffs)], axis=0
        )
        both = dot3(halves_of(split), functions, NN)
        first, second = both[: 2 * every], both[2 * every :]
        north, other = first + second, first - second
        base = s * devices * each
        for b in range(folds):
            cut = slice(b * LANES, (b + 1) * LANES)
            synth[aligned(base + b * 2 * every, 2 * every), :] = north[:, cut]
            synth[aligned(base + (bands - 1 - b) * 2 * every, 2 * every), :] = other[:, cut]

        def body(i, c):
            send2_copy(s, jnp.bitwise_xor(me, devices - 1 - i), sem).start()
            return c

        lax.fori_loop(0, devices - 1, body, 0)
        pltpu.make_async_copy(
            synth.at[aligned((s * devices + me) * each, each), :],
            returned.at[me, aligned(s * each, each), :],
            recv2_sem.at[sem],
        ).start()
        return carry

    lax.fori_loop(0, slots, one_slot, 0)

    block = 256

    def part_copy(m):
        at = aligned(m * block, block)
        return pltpu.make_async_copy(forced.at[:, at, :], partial.at[:, at, :], part_sem)

    for g in range(groups):
        last = g == groups - 1
        rows = (GROUP - 1 if last else GROUP) * each
        here = returned.at[:, g * GROUP * each : g * GROUP * each + rows, :]
        into_vmem = pulled.at[:, 0:rows, :]
        pltpu.make_async_copy(here, here, recv2_sem.at[g]).wait()
        copy = pltpu.make_async_copy(here, into_vmem, pull_sem)
        copy.start()
        copy.wait()
        flat = pulled.reshape(devices * GROUP * each, lats)

        def pull(l, carry):
            x = flat[pl.ds(l, tall, stride=levels), :]
            if last:
                row = lax.rem(lax.broadcasted_iota(jnp.int32, x.shape, 0), small)
                x = jnp.where(row < small - 2, x, 0.0)
            x = x.T
            for j in range(tall // LANES):
                turned[j, pl.ds(l, lats, stride=levels), :] = x[:, j * LANES : (j + 1) * LANES]
            return carry

        lax.fori_loop(0, levels, pull, 0)

        def multiply(m, carry):
            for r in range(block // levels):
                to = m * (block // levels) + r
                lat = jnp.where(south, lats - 1 - to, to)
                for j in range(tall // LANES):
                    h, l = halves_of(turned[j, aligned(lat * levels, levels), :])
                    rows_h[r * levels : (r + 1) * levels, j * LANES : (j + 1) * LANES] = h
                    rows_l[r * levels : (r + 1) * levels, j * LANES : (j + 1) * LANES] = l
            ah, al = rows_h[:block, :tall], rows_l[:block, :tall]
            at = aligned(m * block, block)

            def inner(w, c):
                cut = aligned(w * 2 * LANES, 2 * LANES)
                rows_at = slice(g * tall, (g + 1) * tall)
                got = dot3((ah, al), (high[rows_at, cut], low[rows_at, cut]), NN)
                for j in range(2):
                    x = got[:, j * LANES : (j + 1) * LANES]
                    if g > 0:
                        x = x + forced[2 * w + j, at, :]
                    forced[2 * w + j, at, :] = x
                return c

            lax.fori_loop(0, wide // 2, inner, 0)
            if last:
                part_copy(m).start()
            return carry

        lax.fori_loop(0, lats * levels // block, multiply, 0)

    for s in range(max(slots - 2, 0), slots):
        pltpu.make_async_copy(spec.at[s % 2], spec_out.at[s], spec_sem.at[s % 2]).wait()
    pltpu.make_async_copy(forced, partial, part_sem).wait()
    sent = pl.ds(0, pairs * (devices - 1) * message)
    pltpu.make_async_copy(sending.at[sent, :], sending.at[sent, :], send_sem).wait()
    sent = pl.ds(0, slots * (devices - 1) * each)
    pltpu.make_async_copy(synth.at[sent, :], synth.at[sent, :], send2_sem).wait()
    final = returned.at[:, (slots - 1) * each : slots * each, :]
    pltpu.make_async_copy(final, final, recv2_sem.at[groups]).wait()


def finish_kernel(
    dims, returned, partial, spectral, wave_ref, grid_out, spec_out,
    pulled, turned, stacked, table, before, result, spec,
    pull_sem, in_sem, out_sem, spec_in, spec_done,
):
    bands, parts, lats, levels, longitudes, slots, depth, half = dims
    devices = bands * parts
    each = 2 * levels
    small = 2 * GROUP
    wide = longitudes // LANES
    south = lax.axis_index("band") >= bands // 2
    span = lats // PIECES
    block = span * levels

    def in_copy(m, slot):
        at = aligned(m * block, block)
        return pltpu.make_async_copy(partial.at[:, at, :], before.at[slot], in_sem.at[slot])

    def out_copy(m, slot):
        return pltpu.make_async_copy(
            result.at[slot], grid_out.at[aligned(m * span, span), :, :], out_sem.at[slot]
        )

    pull = pltpu.make_async_copy(
        returned.at[:, (slots - 1) * each : slots * each, :], pulled, pull_sem
    )
    pull.start()
    in_copy(0, 0).start()
    in_copy(1, 1).start()
    spec_copy = pltpu.make_async_copy(spectral, spec, spec_in)
    spec_copy.start()

    first = (slots // GROUP - 1) * devices * small + small - 2
    waves = wave_ref[pl.ds(first, devices, stride=small), :]
    waves = jnp.concatenate([waves, waves], axis=0)
    imaginary = lax.broadcasted_iota(jnp.int32, waves.shape, 0) >= devices
    short = 2 * devices
    for i, (h, l) in enumerate(table_rows(waves, imaginary, longitudes)):
        cut = slice(i * LANES, (i + 1) * LANES)
        table[0:short, cut] = h
        table[short : 2 * short, cut] = l
        table[2 * short : 3 * short, cut] = h
        table[3 * short : 4 * short, cut] = jnp.zeros_like(h)
    pull.wait()
    flat = pulled.reshape(devices * each, lats)

    def gather(l, carry):
        x = jnp.concatenate(
            [flat[pl.ds(c * levels + l, devices, stride=each), :] for c in range(2)], axis=0
        )
        turned[pl.ds(l, lats, stride=levels), :] = jnp.concatenate([x, x], axis=0).T
        return carry

    lax.fori_loop(0, levels, gather, 0)
    keep = lax.broadcasted_iota(jnp.int32, (levels, LANES), 1) < short

    def split(r, carry):
        lat = jnp.where(south, lats - 1 - r, r)
        h, l = halves_of(turned[aligned(lat * levels, levels), :])
        to = aligned(r * levels, levels)
        stacked[to, 0:LANES] = h
        stacked[to, LANES : 2 * LANES] = jnp.where(keep, l, jnp.zeros_like(l))
        return carry

    lax.fori_loop(0, lats, split, 0)

    def outer(m, carry):
        slot = lax.rem(m, 2)
        in_copy(m, slot).wait()

        @pl.when(m >= 2)
        def _():
            out_copy(m - 2, slot).wait()

        a = stacked[aligned(m * block, block), :]

        def inner(w, c):
            cut = aligned(w * 2 * LANES, 2 * LANES)
            got = dot1(a, table[:, cut], NN)
            for j in range(2):
                x = got[:, j * LANES : (j + 1) * LANES] + before[slot, 2 * w + j]
                to = aligned((2 * w + j) * LANES, LANES)
                result[slot, :, :, to] = x.reshape(span, levels, LANES)
            return c

        lax.fori_loop(0, wide // 2, inner, 0)
        out_copy(m, slot).start()

        @pl.when(m + 2 < PIECES)
        def _():
            in_copy(m + 2, slot).start()

        return carry

    spec_copy.wait()
    done = pltpu.make_async_copy(spec, spec_out, spec_done)
    done.start()
    lax.fori_loop(0, PIECES, outer, 0)
    for m in range(PIECES - 2, PIECES):
        out_copy(m, m % 2).wait()
    done.wait()


def shards(
    grid_adjoint, trajectory, legendre_north, slot_wavenumber, spectral_state,
    to_modes, from_modes, rates,
):
    lats, levels, longitudes = grid_adjoint.shape
    slots, depth, half = legendre_north.shape
    bands = lax.axis_size("band")
    parts = lax.axis_size("lev")
    devices = bands * parts
    every = parts * levels
    fits = (
        lats == LANES and levels == 2 * SUB and 4 * devices == LANES
        and longitudes % (2 * LANES) == 0 and longitudes & (longitudes - 1) == 0
        and bands % 2 == 0 and half == bands // 2 * lats and depth % LANES == 0
        and slots % GROUP == 0 and 2 * every == LANES and to_modes.shape[0] == every
    )
    if not fits:
        return plain_shards(
            grid_adjoint, trajectory, legendre_north, slot_wavenumber, spectral_state,
            to_modes, from_modes, rates,
        )
    dims = (bands, parts, lats, levels, longitudes, slots, depth, half)
    count = devices * slots * 2
    waves = slot_wavenumber.reshape(devices, slots // GROUP, GROUP).transpose(1, 0, 2)
    waves = jnp.broadcast_to(waves[:, :, :, None, None], waves.shape + (2, LANES))
    waves = waves.reshape(count, LANES)
    rate = jnp.broadcast_to(rates[None, :, None], (2, every, LANES)).reshape(2 * every, LANES)

    hbm = pl.BlockSpec(memory_space=pl.ANY)
    vmem = pl.BlockSpec(memory_space=pltpu.VMEM)
    f32, bf16 = jnp.float32, jnp.bfloat16
    dma = pltpu.SemaphoreType.DMA
    wide = longitudes // LANES
    state = spectral_state.transpose(0, 2, 3, 1).reshape(slots, 2 * every, depth)
    square = pltpu.VMEM((2 * every, 2 * every), f32)
    spectral, returned, partial = pl.pallas_call(
        functools.partial(forward_kernel, dims),
        out_shape=(
            jax.ShapeDtypeStruct((slots, 2 * every, depth), f32),
            jax.ShapeDtypeStruct((devices, slots * 2 * levels, lats), f32),
            jax.ShapeDtypeStruct((wide, lats * levels, LANES), f32),
        ),
        in_specs=[hbm, hbm, vmem, hbm, hbm, vmem, vmem, vmem],
        out_specs=(hbm, hbm, hbm),
        scratch_shapes=[
            pltpu.VMEM((count, longitudes), bf16),
            pltpu.VMEM((count, longitudes), bf16),
            pltpu.VMEM((wide, levels * lats, LANES), f32),
            pltpu.VMEM((2, lats // PIECES, SUB, longitudes), f32),
            pltpu.VMEM((2, lats // PIECES, SUB, longitudes), f32),
            pltpu.VMEM((PAIR * lats, longitudes), bf16),
            pltpu.VMEM((PAIR * lats, longitudes), bf16),
            pltpu.VMEM((levels * count, lats), f32),
            pltpu.VMEM((levels * count, lats), f32),
            pltpu.VMEM((count * levels, lats), f32),
            pltpu.VMEM((2, depth, half), f32),
            pltpu.VMEM((2, 2 * every, depth), f32),
            pltpu.VMEM((2, 2 * every, depth), f32),
            square, square, square,
            pltpu.VMEM((devices, GROUP * 2 * levels, lats), f32),
            pltpu.VMEM((devices * 2 * GROUP // LANES, lats * levels, LANES), f32),
            dma((2,)), dma((2,)), dma, dma, dma, dma((slots // GROUP + 1,)),
            dma((2,)), dma((2,)), dma((2,)), dma, dma,
        ],
        compiler_params=pltpu.CompilerParams(
            collective_id=0, has_side_effects=True, vmem_limit_bytes=67_043_328
        ),
        name="spectral",
    )(
        grid_adjoint, trajectory, waves, legendre_north, state, rate, to_modes, from_modes,
    )
    grid, spectral = pl.pallas_call(
        functools.partial(finish_kernel, dims),
        out_shape=(
            jax.ShapeDtypeStruct(grid_adjoint.shape, f32),
            jax.ShapeDtypeStruct(spectral.shape, f32),
        ),
        in_specs=[hbm, hbm, hbm, vmem],
        out_specs=(hbm, hbm),
        scratch_shapes=[
            pltpu.VMEM((devices, 2 * levels, lats), f32),
            pltpu.VMEM((lats * levels, LANES), f32),
            pltpu.VMEM((lats * levels, 2 * LANES), bf16),
            pltpu.VMEM((2 * LANES, longitudes), bf16),
            pltpu.VMEM((2, wide, lats // PIECES * levels, LANES), f32),
            pltpu.VMEM((2, lats // PIECES, levels, longitudes), f32),
            pltpu.VMEM(spectral.shape, f32),
            dma, dma((2,)), dma((2,)), dma, dma,
        ],
        compiler_params=pltpu.CompilerParams(vmem_limit_bytes=67_043_328),
        name="finish",
    )(returned, partial, spectral, waves)
    return spectral.reshape(slots, 2, every, depth).transpose(0, 3, 1, 2), grid


def solution(mesh):
    return jax.shard_map(
        shards,
        mesh=mesh,
        in_specs=(
            P("band", "lev", None),
            P("band", "lev", None),
            P(("band", "lev"), None, None),
            P(),
            P(("band", "lev"), None, None, None),
            P(),
            P(),
            P(),
        ),
        out_specs=(P(("band", "lev"), None, None, None), P("band", "lev", None)),
        check_vma=False,
    )
```

```python
import functools
import math

import jax
import jax.numpy as jnp
from jax import lax
from jax.experimental import pallas as pl
from jax.experimental.pallas import tpu as pltpu
from jax.sharding import PartitionSpec as P

PRECISION = lax.Precision.HIGH


def angle_parts(steps, waves, longitudes):
    phase = waves[:, None] * steps[None, :] % longitudes
    angles = phase.astype(jnp.float32) * (2.0 * jnp.pi / longitudes)
    return jnp.cos(angles), jnp.sin(angles)


def wave_rows(longitudes, waves, devices):
    fine = min(128, longitudes)
    coarse = longitudes // fine
    scale = jnp.float32(longitudes) ** (-0.5)
    cos_a, sin_a = angle_parts(jnp.arange(coarse, dtype=jnp.int32) * fine, waves, longitudes)
    cos_b, sin_b = angle_parts(jnp.arange(fine, dtype=jnp.int32), waves, longitudes)
    cos_a, sin_a, cos_b, sin_b = lax.optimization_barrier(
        (cos_a * scale, sin_a * scale, cos_b, sin_b)
    )
    cos_at = [cos_a[:, i : i + 1] * cos_b - sin_a[:, i : i + 1] * sin_b for i in range(coarse)]
    sin_at = [-sin_a[:, i : i + 1] * cos_b - cos_a[:, i : i + 1] * sin_b for i in range(coarse)]
    cosine = jnp.concatenate(cos_at, axis=1).reshape(devices, -1, longitudes)
    negsine = jnp.concatenate(sin_at, axis=1).reshape(devices, -1, longitudes)
    return jnp.stack([cosine, negsine], axis=1).reshape(-1, longitudes)


def exchange(data):
    return lax.all_to_all(data, ("band", "lev"), split_axis=0, concat_axis=0, tiled=True)


def plain_shards(
    grid_adjoint,
    trajectory,
    legendre_north,
    slot_wavenumber,
    spectral_state,
    to_modes,
    from_modes,
    rates,
):
    lats, levels, longitudes = grid_adjoint.shape
    slots, depth, half = legendre_north.shape
    bands = lax.axis_size("band")
    parts = lax.axis_size("lev")
    devices = bands * parts
    every = parts * levels
    me = lax.axis_index("band") * parts + lax.axis_index("lev")
    own_waves = lax.dynamic_slice_in_dim(slot_wavenumber, me * slots, slots)
    table = wave_rows(longitudes, slot_wavenumber, devices)
    even_k = jnp.arange(depth, dtype=jnp.int32) % 2 == 0

    forced = grid_adjoint * (1.0 + trajectory)
    rows = jnp.swapaxes(forced, 0, 1).reshape(levels * lats, longitudes)
    fourier = lax.dot_general(
        table, rows, (((1,), (1,)), ((), ())), precision=PRECISION, preferred_element_type=jnp.float32
    )
    arrived = exchange(fourier.reshape(devices, 2 * slots, levels * lats))
    arrived = arrived.reshape(bands, parts, 2, slots, levels, lats)
    arrived = arrived.transpose(3, 2, 1, 4, 0, 5).reshape(slots, 2 * every, bands * lats)
    north = arrived[:, :, :half]
    south = arrived[:, :, half:][:, :, ::-1]
    folded = jnp.concatenate([north + south, north - south], axis=1)
    both = lax.dot_general(
        folded, legendre_north, (((2,), (2,)), ((0,), (0,))), precision=PRECISION,
        preferred_element_type=jnp.float32,
    )
    analysed = jnp.where(even_k, both[:, : 2 * every], both[:, 2 * every :])
    analysed = analysed.reshape(slots, 2, every, depth)

    state = spectral_state.transpose(0, 2, 3, 1)
    depth_index = jnp.arange(depth, dtype=jnp.int32)
    valid = (depth_index[None, :] < depth - own_waves[:, None]).astype(jnp.float32)
    total = (analysed + state) * valid[:, None, None, :]
    degree = (own_waves[:, None] + depth_index[None, :]).astype(jnp.float32)
    helm = degree * (degree + 1.0) / (depth * (depth - 1.0))
    modes = jnp.einsum("sclk,pl->scpk", total, to_modes, precision=PRECISION)
    scaled = modes / (1.0 + helm[:, None, None, :] * rates[None, None, :, None])
    spectral = jnp.einsum("scpk,lp->sclk", scaled, from_modes, precision=PRECISION)

    coeffs = spectral.reshape(slots, 2 * every, depth)
    split = jnp.concatenate(
        [jnp.where(even_k, coeffs, 0.0), jnp.where(even_k, 0.0, coeffs)], axis=1
    )
    halves = lax.dot_general(
        split, legendre_north, (((2,), (1,)), ((0,), (0,))), precision=PRECISION,
        preferred_element_type=jnp.float32,
    )
    first = halves[:, : 2 * every]
    second = halves[:, 2 * every :]
    whole = jnp.concatenate([first + second, (first - second)[:, :, ::-1]], axis=2)
    whole = whole.reshape(slots, 2, parts, levels, bands, lats).transpose(4, 2, 1, 0, 3, 5)
    returned = exchange(whole.reshape(devices, 2 * slots, levels * lats))
    grid = lax.dot_general(
        returned.reshape(devices * 2 * slots, levels, lats),
        table,
        (((0,), (0,)), ((), ())),
        precision=PRECISION,
        preferred_element_type=jnp.float32,
    )
    return spectral.transpose(0, 3, 1, 2), jnp.swapaxes(grid, 0, 1)


LANES = 128
SUB = 8
PAIR = 2
PIECES = 8
GROUP = 4
KEEP = 48_000_000
NN = (((1,), (0,)), ((), ()))
NT = (((1,), (1,)), ((), ()))


def halves_of(x):
    high = x.astype(jnp.bfloat16)
    low = (x - high.astype(jnp.float32)).astype(jnp.bfloat16)
    return high, low


def dot1(x, y, dims):
    return lax.dot_general(x, y, dims, preferred_element_type=jnp.float32)


def dot3(a, b, dims):
    return dot1(a[0], b[0], dims) + (dot1(a[0], b[1], dims) + dot1(a[1], b[0], dims))


def aligned(start, size):
    return pl.ds(pl.multiple_of(start, size & -size), size)


def circle(phase, longitudes):
    quarter = longitudes // 4
    quadrant = phase // quarter
    rest = phase - quadrant * quarter
    flip = rest > quarter // 2
    angle = jnp.where(flip, quarter - rest, rest).astype(jnp.float32) * (
        2.0 * math.pi / longitudes
    )
    z = angle * angle
    sine = angle * (
        1.0 + z * (-1 / 6 + z * (1 / 120 + z * (-1 / 5040 + z * (1 / 362880))))
    )
    cosine = 1.0 + z * (
        -0.5 + z * (1 / 24 + z * (-1 / 720 + z * (1 / 40320 + z * (-1 / 3628800))))
    )
    c, s = jnp.where(flip, sine, cosine), jnp.where(flip, cosine, sine)
    odd = lax.rem(quadrant, 2) == 1
    c, s = jnp.where(odd, s, c), jnp.where(odd, c, s)
    c = jnp.where((quadrant == 1) | (quadrant == 2), -c, c)
    return c, jnp.where(quadrant >= 2, -s, s)


def table_rows(waves, imaginary, longitudes):
    column = lax.broadcasted_iota(jnp.int32, waves.shape, 1)
    ca, sa = circle(lax.rem(waves * (column * LANES), longitudes), longitudes)
    cb, sb = circle(lax.rem(waves * column, longitudes), longitudes)
    scale = float(longitudes) ** -0.5
    ca, sa = ca * scale, sa * scale
    p = jnp.where(imaginary, -sa, ca)
    q = jnp.where(imaginary, -ca, -sa)
    return [
        halves_of(p[:, i : i + 1] * cb + q[:, i : i + 1] * sb)
        for i in range(longitudes // LANES)
    ]


def forward_kernel(
    dims,
    grid_ref, traj_ref, wave_ref, leg_ref, state_ref, rate_ref, to_ref, from_ref,
    spec_out, returned, forced,
    high, low, stage, traj, rows_h, rows_l, sending, arrived, synth, leg, state, spec,
    into, outof, back, flat_h, flat_l,
    grid_sem, traj_sem, send_sem, recv_sem, send2_sem, recv2_sem, leg_sem, state_sem, spec_sem,
    pull_sem,
):
    bands, parts, lats, levels, longitudes, slots, depth, half = dims
    devices = bands * parts
    every = parts * levels
    pairs = levels // PAIR
    unit = 2 * slots
    message = PAIR * unit
    small = 2 * GROUP
    tall = devices * small
    groups = slots // GROUP
    count_rows = devices * unit
    wide = longitudes // LANES
    band, lev = lax.axis_index("band"), lax.axis_index("lev")
    me = band * parts + lev
    south = band >= bands // 2

    def mesh_id(d):
        return (d // parts, lax.rem(d, parts))

    barrier = pltpu.get_barrier_semaphore()

    def greet(i, carry):
        pl.semaphore_signal(
            barrier, inc=1, device_id=mesh_id(jnp.bitwise_xor(me, i)),
            device_id_type=pl.DeviceIdType.MESH,
        )
        return carry

    lax.fori_loop(1, devices, greet, 0)

    span = lats // PIECES
    count = (levels // SUB) * PIECES

    def load_copies(piece):
        block, part = piece // PIECES, lax.rem(piece, PIECES)
        lat = aligned(part * span, span)
        cut = aligned(block * SUB, SUB)
        slot = lax.rem(piece, 2)
        return (
            pltpu.make_async_copy(grid_ref.at[lat, cut, :], stage.at[slot], grid_sem.at[slot]),
            pltpu.make_async_copy(traj_ref.at[lat, cut, :], traj.at[slot], traj_sem.at[slot]),
        )

    def load_piece(piece):
        for copy in load_copies(piece):
            copy.start()

    def finish_piece(piece):
        block, part = piece // PIECES, lax.rem(piece, PIECES)
        slot = lax.rem(piece, 2)
        for copy in load_copies(piece):
            copy.wait()

        def body(i, carry):
            at = part * span + i
            lat = jnp.where(south, lats - 1 - at, at)
            to = aligned((block * lats + lat) * SUB, SUB)
            x = stage[slot, i] * (1.0 + traj[slot, i])
            for j in range(wide):
                forced[j, to, :] = x[:, j * LANES : (j + 1) * LANES]
            return carry

        lax.fori_loop(0, span, body, 0)

        @pl.when(piece + 2 < count)
        def _():
            load_piece(piece + 2)

    load_piece(jnp.int32(0))
    load_piece(jnp.int32(1))

    def leg_copy(s, slot):
        return pltpu.make_async_copy(leg_ref.at[s], leg.at[slot], leg_sem.at[slot])

    def state_copy(s, slot):
        return pltpu.make_async_copy(state_ref.at[s], state.at[slot], state_sem.at[slot])

    block_rows = 64

    def fill(r, carry):
        at = aligned(r * block_rows, block_rows)
        waves = wave_ref[at, :]
        imaginary = lax.rem(lax.broadcasted_iota(jnp.int32, waves.shape, 0), 2) == 1
        for i, (h, l) in enumerate(table_rows(waves, imaginary, longitudes)):
            high[at, i * LANES : (i + 1) * LANES] = h
            low[at, i * LANES : (i + 1) * LANES] = l
        return carry

    lax.fori_loop(0, devices * unit // block_rows, fill, 0)
    for m in (into, outof, back):
        m[...] = jnp.zeros_like(m)
    for c in range(2):
        cut = slice(c * every, (c + 1) * every)
        into[cut, cut] = to_ref[...]
        outof[cut, cut] = from_ref[...]
        for p in range(parts):
            at = (2 * p + c) * levels
            back[at : at + levels, cut] = from_ref[p * levels : (p + 1) * levels, :]

    def send_copy(q, d):
        return pltpu.make_async_remote_copy(
            src_ref=sending.at[aligned((q * devices + d) * message, message), :],
            dst_ref=arrived.at[aligned((me * pairs + q) * message, message), :],
            send_sem=send_sem,
            recv_sem=recv_sem,
            device_id=mesh_id(d),
            device_id_type=pl.DeviceIdType.MESH,
        )

    def transform(q):
        first = q * PAIR
        block, local = first // SUB, lax.rem(first, SUB)
        for h in range(PAIR):
            for i in range(wide):
                x = forced[i, pl.ds(block * lats * SUB + local + h, lats, stride=SUB), :]
                rh, rl = halves_of(x)
                rows_h[h * lats : (h + 1) * lats, i * LANES : (i + 1) * LANES] = rh
                rows_l[h * lats : (h + 1) * lats, i * LANES : (i + 1) * LANES] = rl

        def body(r, carry):
            at = aligned(r * tall, tall)
            got = dot3((high[at, :], low[at, :]), (rows_h[...], rows_l[...]), NT)
            for d in range(devices):
                for h in range(PAIR):
                    to = (q * devices + d) * message + h * unit + r * small
                    sending[aligned(to, small), :] = got[
                        d * small : (d + 1) * small, h * lats : (h + 1) * lats
                    ]
            return carry

        lax.fori_loop(0, groups, body, 0)

    def send_pair(q):
        def body(i, carry):
            send_copy(q, jnp.bitwise_xor(me, devices - 1 - i)).start()
            return carry

        lax.fori_loop(0, devices - 1, body, 0)
        pltpu.make_async_copy(
            sending.at[aligned((q * devices + me) * message, message), :],
            arrived.at[aligned((me * pairs + q) * message, message), :],
            recv_sem,
        ).start()

    per = SUB // PAIR

    def outer(block, carry):
        def finish(i, c):
            finish_piece(block * PIECES + i)
            return c

        lax.fori_loop(0, PIECES, finish, 0)

        def run(j, c):
            q = block * per + j
            transform(q)

            @pl.when(q == 0)
            def _():
                pl.semaphore_wait(barrier, devices - 1)

            send_pair(q)
            return c

        lax.fori_loop(0, per, run, 0)
        return carry

    lax.fori_loop(0, levels // SUB, outer, 0)

    leg_copy(0, 0).start()
    state_copy(0, 0).start()
    pltpu.make_async_copy(arrived, arrived, recv_sem).wait()

    lane = lax.broadcasted_iota(jnp.int32, (2 * every, depth), 1)
    even = lax.rem(lane, 2) == 0
    folds = bands // 2
    each = 2 * levels

    def column(b, s):
        return jnp.concatenate(
            [
                arrived[pl.ds(b * every * unit + 2 * s + c, every, stride=unit), :]
                for c in range(2)
            ],
            axis=0,
        )

    def send2_copy(s, d, sem):
        return pltpu.make_async_remote_copy(
            src_ref=synth.at[aligned((s * devices + d) * each, each), :],
            dst_ref=returned.at[me, aligned(s * each, each), :],
            send_sem=send2_sem,
            recv_sem=recv2_sem.at[sem],
            device_id=mesh_id(d),
            device_id_type=pl.DeviceIdType.MESH,
        )

    def one_slot(s, carry):
        slot = lax.rem(s, 2)
        sem = jnp.where(s == slots - 1, groups, s // GROUP)

        @pl.when(s + 1 < slots)
        def _():
            leg_copy(s + 1, 1 - slot).start()
            state_copy(s + 1, 1 - slot).start()

        leg_copy(s, slot).wait()
        state_copy(s, slot).wait()
        functions = halves_of(leg[slot])
        evens, odds = [], []
        for b in range(folds):
            n, o = column(b, s), column(bands - 1 - b, s)
            evens.append(n + o)
            odds.append(n - o)
        folded = jnp.concatenate(
            [jnp.concatenate(evens, axis=1), jnp.concatenate(odds, axis=1)], axis=0
        )
        both = dot3(halves_of(folded), functions, NT)
        analysed = jnp.where(even, both[: 2 * every], both[2 * every :])
        wave = wave_ref[
            pl.ds((s // GROUP * devices + me) * small + lax.rem(s, GROUP) * 2, 1), :
        ]
        wave = jnp.concatenate([wave] * (depth // LANES), axis=1)
        order = lax.broadcasted_iota(jnp.int32, (1, depth), 1)
        degree = (wave + order).astype(jnp.float32)
        helm = degree * (degree + 1.0) / (depth * (depth - 1.0))
        total = jnp.where(order < depth - wave, analysed + state[slot], 0.0)
        modes = dot3(halves_of(into[...]), halves_of(total), NN)
        scaled = halves_of(modes / (1.0 + helm * rate_ref[:, 0:1]))

        @pl.when(s >= 2)
        def _():
            pltpu.make_async_copy(spec.at[slot], spec_out.at[s - 2], spec_sem.at[slot]).wait()

        spec[slot] = dot3(halves_of(outof[...]), scaled, NN)
        pltpu.make_async_copy(spec.at[slot], spec_out.at[s], spec_sem.at[slot]).start()
        coeffs = dot3(halves_of(back[...]), scaled, NN)
        split = jnp.concatenate(
            [jnp.where(even, coeffs, 0.0), jnp.where(even, 0.0, coeffs)], axis=0
        )
        both = dot3(halves_of(split), functions, NN)
        first, second = both[: 2 * every], both[2 * every :]
        north, other = first + second, first - second
        base = s * devices * each
        for b in range(folds):
            cut = slice(b * LANES, (b + 1) * LANES)
            synth[aligned(base + b * 2 * every, 2 * every), :] = north[:, cut]
            synth[aligned(base + (bands - 1 - b) * 2 * every, 2 * every), :] = other[:, cut]

        def body(i, c):
            send2_copy(s, jnp.bitwise_xor(me, devices - 1 - i), sem).start()
            return c

        lax.fori_loop(0, devices - 1, body, 0)
        pltpu.make_async_copy(
            synth.at[aligned((s * devices + me) * each, each), :],
            returned.at[me, aligned(s * each, each), :],
            recv2_sem.at[sem],
        ).start()
        return carry

    lax.fori_loop(0, slots, one_slot, 0)

    staged = devices * GROUP * each
    pulled = arrived.reshape(levels * count_rows // (GROUP * each), GROUP * each, lats)
    block = 1024

    for g in range(groups):
        last = g == groups - 1
        rows = (GROUP - 1 if last else GROUP) * each
        here = returned.at[:, g * GROUP * each : g * GROUP * each + rows, :]
        pltpu.make_async_copy(here, here, recv2_sem.at[g]).wait()
        copy = pltpu.make_async_copy(here, pulled.at[0:devices, 0:rows, :], pull_sem)
        copy.start()
        copy.wait()

        def pull(l, carry):
            x = arrived[pl.ds(l, tall, stride=levels), :]
            if last:
                row = lax.rem(lax.broadcasted_iota(jnp.int32, x.shape, 0), small)
                x = jnp.where(row < small - 2, x, 0.0)
            x = x.T
            for j in range(tall // LANES):
                arrived[pl.ds(staged + j * lats * levels + l, lats, stride=levels), :] = x[
                    :, j * LANES : (j + 1) * LANES
                ]
            return carry

        lax.fori_loop(0, levels, pull, 0)

        def split(r, carry):
            lat = jnp.where(south, lats - 1 - r, r)
            to = aligned(r * levels, levels)
            for j in range(tall // LANES):
                x = arrived[aligned(staged + (j * lats + lat) * levels, levels), :]
                h, l = halves_of(x)
                flat_h[to, j * LANES : (j + 1) * LANES] = h
                flat_l[to, j * LANES : (j + 1) * LANES] = l
            return carry

        lax.fori_loop(0, lats, split, 0)

        def multiply(m, carry):
            at = aligned(m * block, block)

            def inner(w, c):
                cut = aligned(w * 2 * LANES, 2 * LANES)
                rows_at = slice(g * tall, (g + 1) * tall)
                got = dot3(
                    (flat_h[at, :], flat_l[at, :]), (high[rows_at, cut], low[rows_at, cut]), NN
                )
                for j in range(2):
                    x = got[:, j * LANES : (j + 1) * LANES]
                    if g > 0:
                        x = x + forced[2 * w + j, at, :]
                    forced[2 * w + j, at, :] = x
                return c

            lax.fori_loop(0, wide // 2, inner, 0)
            return carry

        lax.fori_loop(0, lats * levels // block, multiply, 0)

    for s in range(max(slots - 2, 0), slots):
        pltpu.make_async_copy(spec.at[s % 2], spec_out.at[s], spec_sem.at[s % 2]).wait()
    sent = pl.ds(0, pairs * (devices - 1) * message)
    pltpu.make_async_copy(sending.at[sent, :], sending.at[sent, :], send_sem).wait()
    sent = pl.ds(0, slots * (devices - 1) * each)
    pltpu.make_async_copy(synth.at[sent, :], synth.at[sent, :], send2_sem).wait()
    final = returned.at[:, (slots - 1) * each : slots * each, :]
    pltpu.make_async_copy(final, final, recv2_sem.at[groups]).wait()


def finish_kernel(
    dims, returned, partial, spectral, wave_ref, grid_out, spec_out,
    pulled, turned, stacked, table, result, spec,
    pull_sem, out_sem, spec_in, spec_done,
):
    bands, parts, lats, levels, longitudes, slots, depth, half = dims
    devices = bands * parts
    each = 2 * levels
    small = 2 * GROUP
    wide = longitudes // LANES
    south = lax.axis_index("band") >= bands // 2
    span = lats // PIECES
    block = span * levels

    def out_copy(m, slot):
        return pltpu.make_async_copy(
            result.at[slot], grid_out.at[aligned(m * span, span), :, :], out_sem.at[slot]
        )

    pull = pltpu.make_async_copy(
        returned.at[:, (slots - 1) * each : slots * each, :], pulled, pull_sem
    )
    pull.start()
    spec_copy = pltpu.make_async_copy(spectral, spec, spec_in)
    spec_copy.start()

    first = (slots // GROUP - 1) * devices * small + small - 2
    waves = wave_ref[pl.ds(first, devices, stride=small), :]
    waves = jnp.concatenate([waves, waves], axis=0)
    imaginary = lax.broadcasted_iota(jnp.int32, waves.shape, 0) >= devices
    short = 2 * devices
    for i, (h, l) in enumerate(table_rows(waves, imaginary, longitudes)):
        cut = slice(i * LANES, (i + 1) * LANES)
        table[0:short, cut] = h
        table[short : 2 * short, cut] = l
        table[2 * short : 3 * short, cut] = h
        table[3 * short : 4 * short, cut] = jnp.zeros_like(h)
    pull.wait()
    flat = pulled.reshape(devices * each, lats)

    def gather(l, carry):
        x = jnp.concatenate(
            [flat[pl.ds(c * levels + l, devices, stride=each), :] for c in range(2)], axis=0
        )
        turned[pl.ds(l, lats, stride=levels), :] = jnp.concatenate([x, x], axis=0).T
        return carry

    lax.fori_loop(0, levels, gather, 0)
    keep = lax.broadcasted_iota(jnp.int32, (levels, LANES), 1) < short

    def split(r, carry):
        lat = jnp.where(south, lats - 1 - r, r)
        h, l = halves_of(turned[aligned(lat * levels, levels), :])
        to = aligned(r * levels, levels)
        stacked[to, 0:LANES] = h
        stacked[to, LANES : 2 * LANES] = jnp.where(keep, l, jnp.zeros_like(l))
        return carry

    lax.fori_loop(0, lats, split, 0)

    def outer(m, carry):
        slot = lax.rem(m, 2)
        @pl.when(m >= 2)
        def _():
            out_copy(m - 2, slot).wait()

        at = aligned(m * block, block)
        a = stacked[at, :]

        def inner(w, c):
            cut = aligned(w * 2 * LANES, 2 * LANES)
            got = dot1(a, table[:, cut], NN)
            for j in range(2):
                x = got[:, j * LANES : (j + 1) * LANES] + partial[2 * w + j, at, :]
                to = aligned((2 * w + j) * LANES, LANES)
                result[slot, :, :, to] = x.reshape(span, levels, LANES)
            return c

        lax.fori_loop(0, wide // 2, inner, 0)
        out_copy(m, slot).start()

        return carry

    spec_copy.wait()
    done = pltpu.make_async_copy(spec, spec_out, spec_done)
    done.start()
    lax.fori_loop(0, PIECES, outer, 0)
    for m in range(PIECES - 2, PIECES):
        out_copy(m, m % 2).wait()
    done.wait()


def shards(
    grid_adjoint, trajectory, legendre_north, slot_wavenumber, spectral_state,
    to_modes, from_modes, rates,
):
    lats, levels, longitudes = grid_adjoint.shape
    slots, depth, half = legendre_north.shape
    bands = lax.axis_size("band")
    parts = lax.axis_size("lev")
    devices = bands * parts
    every = parts * levels
    fits = (
        lats == LANES and levels == 2 * SUB and 4 * devices == LANES
        and longitudes % (2 * LANES) == 0 and longitudes & (longitudes - 1) == 0
        and bands % 2 == 0 and half == bands // 2 * lats and depth % LANES == 0
        and slots % GROUP == 0 and 2 * every == LANES and to_modes.shape[0] == every
    )
    if not fits:
        return plain_shards(
            grid_adjoint, trajectory, legendre_north, slot_wavenumber, spectral_state,
            to_modes, from_modes, rates,
        )
    dims = (bands, parts, lats, levels, longitudes, slots, depth, half)
    count = devices * slots * 2
    waves = slot_wavenumber.reshape(devices, slots // GROUP, GROUP).transpose(1, 0, 2)
    waves = jnp.broadcast_to(waves[:, :, :, None, None], waves.shape + (2, LANES))
    waves = waves.reshape(count, LANES)
    rate = jnp.broadcast_to(rates[None, :, None], (2, every, LANES)).reshape(2 * every, LANES)

    hbm = pl.BlockSpec(memory_space=pl.ANY)
    vmem = pl.BlockSpec(memory_space=pltpu.VMEM)
    f32, bf16 = jnp.float32, jnp.bfloat16
    dma = pltpu.SemaphoreType.DMA
    wide = longitudes // LANES
    state = spectral_state.transpose(0, 2, 3, 1).reshape(slots, 2 * every, depth)
    square = pltpu.VMEM((2 * every, 2 * every), f32)
    spectral, returned, partial = pl.pallas_call(
        functools.partial(forward_kernel, dims),
        out_shape=(
            jax.ShapeDtypeStruct((slots, 2 * every, depth), f32),
            jax.ShapeDtypeStruct((devices, slots * 2 * levels, lats), f32),
            pltpu.VMEM((wide, lats * levels, LANES), f32),
        ),
        in_specs=[hbm, hbm, vmem, hbm, hbm, vmem, vmem, vmem],
        out_specs=(hbm, hbm, vmem),
        scratch_shapes=[
            pltpu.VMEM((count, longitudes), bf16),
            pltpu.VMEM((count, longitudes), bf16),
            pltpu.VMEM((2, lats // PIECES, SUB, longitudes), f32),
            pltpu.VMEM((2, lats // PIECES, SUB, longitudes), f32),
            pltpu.VMEM((PAIR * lats, longitudes), bf16),
            pltpu.VMEM((PAIR * lats, longitudes), bf16),
            pltpu.VMEM((levels * count, lats), f32),
            pltpu.VMEM((levels * count, lats), f32),
            pltpu.VMEM((count * levels, lats), f32),
            pltpu.VMEM((2, depth, half), f32),
            pltpu.VMEM((2, 2 * every, depth), f32),
            pltpu.VMEM((2, 2 * every, depth), f32),
            square, square, square,
            pltpu.VMEM((lats * levels, devices * 2 * GROUP), bf16),
            pltpu.VMEM((lats * levels, devices * 2 * GROUP), bf16),
            dma((2,)), dma((2,)), dma, dma, dma, dma((slots // GROUP + 1,)),
            dma((2,)), dma((2,)), dma((2,)), dma,
        ],
        compiler_params=pltpu.CompilerParams(
            collective_id=0, has_side_effects=True, vmem_limit_bytes=KEEP
        ),
        name="spectral",
    )(
        grid_adjoint, trajectory, waves, legendre_north, state, rate, to_modes, from_modes,
    )
    grid, spectral = pl.pallas_call(
        functools.partial(finish_kernel, dims),
        out_shape=(
            jax.ShapeDtypeStruct(grid_adjoint.shape, f32),
            jax.ShapeDtypeStruct(spectral.shape, f32),
        ),
        in_specs=[hbm, vmem, hbm, vmem],
        out_specs=(hbm, hbm),
        scratch_shapes=[
            pltpu.VMEM((devices, 2 * levels, lats), f32),
            pltpu.VMEM((lats * levels, LANES), f32),
            pltpu.VMEM((lats * levels, 2 * LANES), bf16),
            pltpu.VMEM((2 * LANES, longitudes), bf16),
            pltpu.VMEM((2, lats // PIECES, levels, longitudes), f32),
            pltpu.VMEM(spectral.shape, f32),
            dma, dma((2,)), dma, dma,
        ],
        compiler_params=pltpu.CompilerParams(vmem_limit_bytes=KEEP),
        name="finish",
    )(returned, partial, spectral, waves)
    return spectral.reshape(slots, 2, every, depth).transpose(0, 3, 1, 2), grid


def solution(mesh):
    return jax.shard_map(
        shards,
        mesh=mesh,
        in_specs=(
            P("band", "lev", None),
            P("band", "lev", None),
            P(("band", "lev"), None, None),
            P(),
            P(("band", "lev"), None, None, None),
            P(),
            P(),
            P(),
        ),
        out_specs=(P(("band", "lev"), None, None, None), P("band", "lev", None)),
        check_vma=False,
    )
```

```python
import functools
import math

import jax
import jax.numpy as jnp
from jax import lax
from jax.experimental import pallas as pl
from jax.experimental.pallas import tpu as pltpu
from jax.sharding import PartitionSpec as P

PRECISION = lax.Precision.HIGH


def angle_parts(steps, waves, longitudes):
    phase = waves[:, None] * steps[None, :] % longitudes
    angles = phase.astype(jnp.float32) * (2.0 * jnp.pi / longitudes)
    return jnp.cos(angles), jnp.sin(angles)


def wave_rows(longitudes, waves, devices):
    fine = min(128, longitudes)
    coarse = longitudes // fine
    scale = jnp.float32(longitudes) ** (-0.5)
    cos_a, sin_a = angle_parts(jnp.arange(coarse, dtype=jnp.int32) * fine, waves, longitudes)
    cos_b, sin_b = angle_parts(jnp.arange(fine, dtype=jnp.int32), waves, longitudes)
    cos_a, sin_a, cos_b, sin_b = lax.optimization_barrier(
        (cos_a * scale, sin_a * scale, cos_b, sin_b)
    )
    cos_at = [cos_a[:, i : i + 1] * cos_b - sin_a[:, i : i + 1] * sin_b for i in range(coarse)]
    sin_at = [-sin_a[:, i : i + 1] * cos_b - cos_a[:, i : i + 1] * sin_b for i in range(coarse)]
    cosine = jnp.concatenate(cos_at, axis=1).reshape(devices, -1, longitudes)
    negsine = jnp.concatenate(sin_at, axis=1).reshape(devices, -1, longitudes)
    return jnp.stack([cosine, negsine], axis=1).reshape(-1, longitudes)


def exchange(data):
    return lax.all_to_all(data, ("band", "lev"), split_axis=0, concat_axis=0, tiled=True)


def plain_shards(
    grid_adjoint,
    trajectory,
    legendre_north,
    slot_wavenumber,
    spectral_state,
    to_modes,
    from_modes,
    rates,
):
    lats, levels, longitudes = grid_adjoint.shape
    slots, depth, half = legendre_north.shape
    bands = lax.axis_size("band")
    parts = lax.axis_size("lev")
    devices = bands * parts
    every = parts * levels
    me = lax.axis_index("band") * parts + lax.axis_index("lev")
    own_waves = lax.dynamic_slice_in_dim(slot_wavenumber, me * slots, slots)
    table = wave_rows(longitudes, slot_wavenumber, devices)
    even_k = jnp.arange(depth, dtype=jnp.int32) % 2 == 0

    forced = grid_adjoint * (1.0 + trajectory)
    rows = jnp.swapaxes(forced, 0, 1).reshape(levels * lats, longitudes)
    fourier = lax.dot_general(
        table, rows, (((1,), (1,)), ((), ())), precision=PRECISION, preferred_element_type=jnp.float32
    )
    arrived = exchange(fourier.reshape(devices, 2 * slots, levels * lats))
    arrived = arrived.reshape(bands, parts, 2, slots, levels, lats)
    arrived = arrived.transpose(3, 2, 1, 4, 0, 5).reshape(slots, 2 * every, bands * lats)
    north = arrived[:, :, :half]
    south = arrived[:, :, half:][:, :, ::-1]
    folded = jnp.concatenate([north + south, north - south], axis=1)
    both = lax.dot_general(
        folded, legendre_north, (((2,), (2,)), ((0,), (0,))), precision=PRECISION,
        preferred_element_type=jnp.float32,
    )
    analysed = jnp.where(even_k, both[:, : 2 * every], both[:, 2 * every :])
    analysed = analysed.reshape(slots, 2, every, depth)

    state = spectral_state.transpose(0, 2, 3, 1)
    depth_index = jnp.arange(depth, dtype=jnp.int32)
    valid = (depth_index[None, :] < depth - own_waves[:, None]).astype(jnp.float32)
    total = (analysed + state) * valid[:, None, None, :]
    degree = (own_waves[:, None] + depth_index[None, :]).astype(jnp.float32)
    helm = degree * (degree + 1.0) / (depth * (depth - 1.0))
    modes = jnp.einsum("sclk,pl->scpk", total, to_modes, precision=PRECISION)
    scaled = modes / (1.0 + helm[:, None, None, :] * rates[None, None, :, None])
    spectral = jnp.einsum("scpk,lp->sclk", scaled, from_modes, precision=PRECISION)

    coeffs = spectral.reshape(slots, 2 * every, depth)
    split = jnp.concatenate(
        [jnp.where(even_k, coeffs, 0.0), jnp.where(even_k, 0.0, coeffs)], axis=1
    )
    halves = lax.dot_general(
        split, legendre_north, (((2,), (1,)), ((0,), (0,))), precision=PRECISION,
        preferred_element_type=jnp.float32,
    )
    first = halves[:, : 2 * every]
    second = halves[:, 2 * every :]
    whole = jnp.concatenate([first + second, (first - second)[:, :, ::-1]], axis=2)
    whole = whole.reshape(slots, 2, parts, levels, bands, lats).transpose(4, 2, 1, 0, 3, 5)
    returned = exchange(whole.reshape(devices, 2 * slots, levels * lats))
    grid = lax.dot_general(
        returned.reshape(devices * 2 * slots, levels, lats),
        table,
        (((0,), (0,)), ((), ())),
        precision=PRECISION,
        preferred_element_type=jnp.float32,
    )
    return spectral.transpose(0, 3, 1, 2), jnp.swapaxes(grid, 0, 1)


LANES = 128
SUB = 8
PAIR = 2
PIECES = 8
GROUP = 4
BLOCKS = 4
GRANT = 50_000_000
LAST_GRANT = 44_000_000
NN = (((1,), (0,)), ((), ()))
NT = (((1,), (1,)), ((), ()))


def halves_of(x):
    high = x.astype(jnp.bfloat16)
    low = (x - high.astype(jnp.float32)).astype(jnp.bfloat16)
    return high, low


def dot1(x, y, dims):
    return lax.dot_general(x, y, dims, preferred_element_type=jnp.float32)


def dot3(a, b, dims):
    return dot1(a[0], b[0], dims) + (dot1(a[0], b[1], dims) + dot1(a[1], b[0], dims))


def aligned(start, size):
    return pl.ds(pl.multiple_of(start, size & -size), size)


def circle(phase, longitudes):
    quarter = longitudes // 4
    quadrant = phase >> (quarter.bit_length() - 1)
    rest = phase & (quarter - 1)
    flip = rest > quarter // 2
    angle = jnp.where(flip, quarter - rest, rest).astype(jnp.float32) * (
        2.0 * math.pi / longitudes
    )
    z = angle * angle
    sine = angle * (
        1.0 + z * (-1 / 6 + z * (1 / 120 + z * (-1 / 5040 + z * (1 / 362880))))
    )
    cosine = 1.0 + z * (
        -0.5 + z * (1 / 24 + z * (-1 / 720 + z * (1 / 40320 + z * (-1 / 3628800))))
    )
    c, s = jnp.where(flip, sine, cosine), jnp.where(flip, cosine, sine)
    odd = (quadrant & 1) == 1
    c, s = jnp.where(odd, s, c), jnp.where(odd, c, s)
    c = jnp.where((quadrant == 1) | (quadrant == 2), -c, c)
    return c, jnp.where(quadrant >= 2, -s, s)


def table_rows(waves, imaginary, longitudes):
    column = lax.broadcasted_iota(jnp.int32, waves.shape, 1)
    ca, sa = circle((waves * (column * LANES)) & (longitudes - 1), longitudes)
    cb, sb = circle((waves * column) & (longitudes - 1), longitudes)
    scale = float(longitudes) ** -0.5
    ca, sa = ca * scale, sa * scale
    p = jnp.where(imaginary, -sa, ca)
    q = jnp.where(imaginary, -ca, -sa)
    return [
        halves_of(p[:, i : i + 1] * cb + q[:, i : i + 1] * sb)
        for i in range(longitudes // LANES)
    ]


def wave_columns(slot_ref, own):
    for i in range(slot_ref.shape[0]):
        row = jnp.broadcast_to(slot_ref[i : i + 1, :].astype(jnp.float32), (LANES, LANES))
        own[i * LANES : (i + 1) * LANES, :] = row.T.astype(jnp.int32)


def single_table(waves, table, longitudes):
    devices = waves.shape[0]
    waves = jnp.concatenate([waves, waves], axis=0)
    imaginary = lax.broadcasted_iota(jnp.int32, waves.shape, 0) >= devices
    short = 2 * devices
    for i, (h, l) in enumerate(table_rows(waves, imaginary, longitudes)):
        cut = slice(i * LANES, (i + 1) * LANES)
        table[0:short, cut] = h
        table[short : 2 * short, cut] = l
        table[2 * short : 3 * short, cut] = h
        table[3 * short : 4 * short, cut] = jnp.zeros_like(h)


def single_rows(dims, south, flat, turned, base, stacked):
    bands, parts, lats, levels = dims[:4]
    devices = bands * parts

    def gather(l, carry):
        x = jnp.concatenate(
            [flat[pl.ds(c * levels + l, devices, stride=2 * levels), :] for c in range(2)], axis=0
        )
        turned[pl.ds(base + l, lats, stride=levels), :] = jnp.concatenate([x, x], axis=0).T
        return carry

    lax.fori_loop(0, levels, gather, 0)
    keep = lax.broadcasted_iota(jnp.int32, (levels, LANES), 1) < 2 * devices

    def split(r, carry):
        lat = jnp.where(south, lats - 1 - r, r)
        h, l = halves_of(turned[aligned(base + lat * levels, levels), :])
        to = aligned(r * levels, levels)
        stacked[to, 0:LANES] = h
        stacked[to, LANES : 2 * LANES] = jnp.where(keep, l, jnp.zeros_like(l))
        return carry

    lax.fori_loop(0, lats, split, 0)


def forward_kernel(
    dims,
    grid_ref, traj_ref, slot_ref, leg_ref, state_ref, rate_ref, to_ref, from_ref,
    spec_out, returned, forced,
    high, low, stage, traj, rows_h, rows_l, sending, arrived, synth, leg, state, spec,
    into, outof, back, flat_h, flat_l, wave_own, wave_ref, rate_col, single,
    grid_sem, traj_sem, send_sem, recv_sem, send2_sem, recv2_sem, leg_sem, state_sem, spec_sem,
    pull_sem,
):
    bands, parts, lats, levels, longitudes, slots, depth, half = dims
    devices = bands * parts
    every = parts * levels
    pairs = levels // PAIR
    unit = 2 * slots
    message = PAIR * unit
    small = 2 * GROUP
    tall = devices * small
    groups = slots // GROUP
    count_rows = devices * unit
    wide = longitudes // LANES
    band, lev = lax.axis_index("band"), lax.axis_index("lev")
    me = band * parts + lev
    south = band >= bands // 2

    def mesh_id(d):
        return (d // parts, lax.rem(d, parts))

    barrier = pltpu.get_barrier_semaphore()

    def greet(i, carry):
        pl.semaphore_signal(
            barrier, inc=1, device_id=mesh_id(jnp.bitwise_xor(me, i)),
            device_id_type=pl.DeviceIdType.MESH,
        )
        return carry

    lax.fori_loop(1, devices, greet, 0)

    span = lats // PIECES
    count = (levels // SUB) * PIECES

    def load_copies(piece):
        block, part = piece // PIECES, lax.rem(piece, PIECES)
        lat = aligned(part * span, span)
        cut = aligned(block * SUB, SUB)
        slot = lax.rem(piece, 2)
        return (
            pltpu.make_async_copy(grid_ref.at[lat, cut, :], stage.at[slot], grid_sem.at[slot]),
            pltpu.make_async_copy(traj_ref.at[lat, cut, :], traj.at[slot], traj_sem.at[slot]),
        )

    def load_piece(piece):
        for copy in load_copies(piece):
            copy.start()

    def finish_piece(piece):
        block, part = piece // PIECES, lax.rem(piece, PIECES)
        slot = lax.rem(piece, 2)
        for copy in load_copies(piece):
            copy.wait()

        def body(i, carry):
            at = part * span + i
            lat = jnp.where(south, lats - 1 - at, at)
            to = aligned((block * lats + lat) * SUB, SUB)
            x = stage[slot, i] * (1.0 + traj[slot, i])
            for j in range(wide):
                forced[j, to, :] = x[:, j * LANES : (j + 1) * LANES]
            return carry

        lax.fori_loop(0, span, body, 0)

        @pl.when(piece + 2 < count)
        def _():
            load_piece(piece + 2)

    load_piece(jnp.int32(0))
    load_piece(jnp.int32(1))

    def leg_copy(s, slot):
        return pltpu.make_async_copy(leg_ref.at[s], leg.at[slot], leg_sem.at[slot])

    def state_copy(s, slot):
        return pltpu.make_async_copy(state_ref.at[s], state.at[slot], state_sem.at[slot])

    wave_columns(slot_ref, wave_own)
    for g in range(groups):
        for i in range(GROUP):
            x = wave_own[pl.ds(g * GROUP + i, devices, stride=slots), :]
            for c in range(2):
                wave_ref[pl.ds(g * tall + 2 * i + c, devices, stride=small), :] = x
    rate = jnp.concatenate([rate_ref[...], rate_ref[...]], axis=1)
    rate_col[...] = jnp.broadcast_to(rate, (2 * every, 2 * every)).T
    block_rows = 64

    def fill(r, carry):
        at = aligned(r * block_rows, block_rows)
        waves = wave_ref[at, :]
        imaginary = (lax.broadcasted_iota(jnp.int32, waves.shape, 0) & 1) == 1
        for i, (h, l) in enumerate(table_rows(waves, imaginary, longitudes)):
            high[at, i * LANES : (i + 1) * LANES] = h
            low[at, i * LANES : (i + 1) * LANES] = l
        return carry

    def greeted_copy(source, target, d, sem):
        return pltpu.make_async_remote_copy(
            src_ref=sending.at[source, :],
            dst_ref=arrived.at[target, :],
            send_sem=send_sem,
            recv_sem=recv_sem.at[sem],
            device_id=mesh_id(d),
            device_id_type=pl.DeviceIdType.MESH,
        )

    def partner(i):
        return jnp.bitwise_xor(me, devices - 1 - i)

    def send_pair(q):
        to = aligned((me * pairs + q) * message, message)

        def body(i, carry):
            d = partner(i)
            greeted_copy(aligned((q * devices + d) * message, message), to, d, 0).start()
            return carry

        lax.fori_loop(0, devices - 1, body, 0)
        pltpu.make_async_copy(
            sending.at[aligned((q * devices + me) * message, message), :],
            arrived.at[to, :],
            recv_sem.at[0],
        ).start()

    def send_part(q, r, sem):
        def cut(first, h):
            return aligned(first * message + h * unit + r * small, small)

        def body(i, carry):
            d = partner(i)
            for h in range(PAIR):
                greeted_copy(
                    cut(q * devices + d, h), cut(me * pairs + q, h), d, sem
                ).start()
            return carry

        lax.fori_loop(0, devices - 1, body, 0)
        for h in range(PAIR):
            pltpu.make_async_copy(
                sending.at[cut(q * devices + me, h), :],
                arrived.at[cut(me * pairs + q, h), :],
                recv_sem.at[sem],
            ).start()

    def extract(q):
        first = q * PAIR
        block, local = first // SUB, lax.rem(first, SUB)
        for h in range(PAIR):
            for i in range(wide):
                x = forced[i, pl.ds(block * lats * SUB + local + h, lats, stride=SUB), :]
                rh, rl = halves_of(x)
                rows_h[h * lats : (h + 1) * lats, i * LANES : (i + 1) * LANES] = rh
                rows_l[h * lats : (h + 1) * lats, i * LANES : (i + 1) * LANES] = rl

    def transform(q, r):
        at = aligned(r * tall, tall)
        got = dot3((high[at, :], low[at, :]), (rows_h[...], rows_l[...]), NT)
        for d in range(devices):
            for h in range(PAIR):
                to = (q * devices + d) * message + h * unit + r * small
                sending[aligned(to, small), :] = got[
                    d * small : (d + 1) * small, h * lats : (h + 1) * lats
                ]

    per = SUB // PAIR
    blocks = levels // SUB

    def finish(i, c):
        finish_piece(i)
        return c

    lax.fori_loop(0, PIECES, finish, 0)
    extract(jnp.int32(0))

    def opening(r, carry):
        lax.fori_loop(r * (tall // block_rows), (r + 1) * (tall // block_rows), fill, 0)
        transform(0, r)

        @pl.when(r == 0)
        def _():
            pl.semaphore_wait(barrier, devices - 1)

        send_part(0, r, 0)
        return carry

    lax.fori_loop(0, groups, opening, 0)

    def middle(q, carry):
        @pl.when(lax.rem(q, per) == 0)
        def _():
            lax.fori_loop(q // per * PIECES, (q // per + 1) * PIECES, finish, 0)

        extract(q)

        def each_group(r, c):
            transform(q, r)
            return c

        lax.fori_loop(0, groups, each_group, 0)
        send_pair(q)
        return carry

    lax.fori_loop(1, pairs - 1, middle, 0)
    extract(jnp.int32(pairs - 1))

    def closing(r, carry):
        transform(pairs - 1, r)
        send_part(pairs - 1, r, r + 1)
        return carry

    lax.fori_loop(0, groups, closing, 0)
    for m in (into, outof, back):
        m[...] = jnp.zeros_like(m)
    for c in range(2):
        cut = slice(c * every, (c + 1) * every)
        into[cut, cut] = to_ref[...]
        outof[cut, cut] = from_ref[...]
        for p in range(parts):
            at = (2 * p + c) * levels
            back[at : at + levels, cut] = from_ref[p * levels : (p + 1) * levels, :]

    leg_copy(0, 0).start()
    state_copy(0, 0).start()
    before = arrived.at[pl.ds(0, (pairs - 1) * devices * message), :]
    pltpu.make_async_copy(before, before, recv_sem.at[0]).wait()
    last_part = arrived.at[pl.ds(0, devices * PAIR * small), :]

    lane = lax.broadcasted_iota(jnp.int32, (2 * every, depth), 1)
    even = lax.rem(lane, 2) == 0
    folds = bands // 2
    each = 2 * levels
    whole = slots - GROUP

    def column(b, s):
        return jnp.concatenate(
            [
                arrived[pl.ds(b * every * unit + 2 * s + c, every, stride=unit), :]
                for c in range(2)
            ],
            axis=0,
        )

    def send2_copy(s, d, sem):
        return pltpu.make_async_remote_copy(
            src_ref=synth.at[aligned((s * devices + d) * each, each), :],
            dst_ref=returned.at[me, aligned(s * each, each), :],
            send_sem=send2_sem,
            recv_sem=recv2_sem.at[sem],
            device_id=mesh_id(d),
            device_id_type=pl.DeviceIdType.MESH,
        )

    def one_slot(s, carry):
        slot = lax.rem(s, 2)
        sem = jnp.where(s < whole, s // GROUP, groups - 1 + s - whole)

        @pl.when(lax.rem(s, GROUP) == 0)
        def _():
            pltpu.make_async_copy(last_part, last_part, recv_sem.at[s // GROUP + 1]).wait()

        @pl.when(s + 1 < slots)
        def _():
            leg_copy(s + 1, 1 - slot).start()
            state_copy(s + 1, 1 - slot).start()

        leg_copy(s, slot).wait()
        state_copy(s, slot).wait()
        functions = halves_of(leg[slot])
        evens, odds = [], []
        for b in range(folds):
            n, o = column(b, s), column(bands - 1 - b, s)
            evens.append(n + o)
            odds.append(n - o)
        folded = jnp.concatenate(
            [jnp.concatenate(evens, axis=1), jnp.concatenate(odds, axis=1)], axis=0
        )
        both = dot3(halves_of(folded), functions, NT)
        analysed = jnp.where(even, both[: 2 * every], both[2 * every :])
        wave = wave_ref[
            pl.ds((s // GROUP * devices + me) * small + lax.rem(s, GROUP) * 2, 1), :
        ]
        wave = jnp.concatenate([wave] * (depth // LANES), axis=1)
        order = lax.broadcasted_iota(jnp.int32, (1, depth), 1)
        degree = (wave + order).astype(jnp.float32)
        helm = degree * (degree + 1.0) / (depth * (depth - 1.0))
        total = jnp.where(order < depth - wave, analysed + state[slot], 0.0)
        modes = dot3(halves_of(into[...]), halves_of(total), NN)
        scaled = halves_of(modes / (1.0 + helm * rate_col[:, 0:1]))

        @pl.when(s >= 2)
        def _():
            pltpu.make_async_copy(spec.at[slot], spec_out.at[s - 2], spec_sem.at[slot]).wait()

        spec[slot] = dot3(halves_of(outof[...]), scaled, NN)
        pltpu.make_async_copy(spec.at[slot], spec_out.at[s], spec_sem.at[slot]).start()
        coeffs = dot3(halves_of(back[...]), scaled, NN)
        split = jnp.concatenate(
            [jnp.where(even, coeffs, 0.0), jnp.where(even, 0.0, coeffs)], axis=0
        )
        both = dot3(halves_of(split), functions, NN)
        first, second = both[: 2 * every], both[2 * every :]
        north, other = first + second, first - second
        base = s * devices * each
        for b in range(folds):
            cut = slice(b * LANES, (b + 1) * LANES)
            synth[aligned(base + b * 2 * every, 2 * every), :] = north[:, cut]
            synth[aligned(base + (bands - 1 - b) * 2 * every, 2 * every), :] = other[:, cut]

        def body(i, c):
            send2_copy(s, partner(i), sem).start()
            return c

        lax.fori_loop(0, devices - 1, body, 0)
        pltpu.make_async_copy(
            synth.at[aligned((s * devices + me) * each, each), :],
            returned.at[me, aligned(s * each, each), :],
            recv2_sem.at[sem],
        ).start()
        return carry

    lax.fori_loop(0, slots, one_slot, 0)

    staged = devices * GROUP * each
    pulled = arrived.reshape(levels * count_rows // (GROUP * each), GROUP * each, lats)
    block = 1024

    for g in range(groups - 1):
        rows = GROUP * each
        here = returned.at[:, g * rows : (g + 1) * rows, :]
        pltpu.make_async_copy(here, here, recv2_sem.at[g]).wait()
        copy = pltpu.make_async_copy(here, pulled.at[0:devices, 0:rows, :], pull_sem)
        copy.start()
        copy.wait()

        def pull(l, carry):
            x = arrived[pl.ds(l, tall, stride=levels), :]
            x = x.T
            for j in range(tall // LANES):
                arrived[pl.ds(staged + j * lats * levels + l, lats, stride=levels), :] = x[
                    :, j * LANES : (j + 1) * LANES
                ]
            return carry

        lax.fori_loop(0, levels, pull, 0)

        def split(r, carry):
            lat = jnp.where(south, lats - 1 - r, r)
            to = aligned(r * levels, levels)
            for j in range(tall // LANES):
                x = arrived[aligned(staged + (j * lats + lat) * levels, levels), :]
                h, l = halves_of(x)
                flat_h[to, j * LANES : (j + 1) * LANES] = h
                flat_l[to, j * LANES : (j + 1) * LANES] = l
            return carry

        lax.fori_loop(0, lats, split, 0)

        def multiply(m, carry):
            at = aligned(m * block, block)

            def inner(w, c):
                cut = aligned(w * 2 * LANES, 2 * LANES)
                rows_at = slice(g * tall, (g + 1) * tall)
                got = dot3(
                    (flat_h[at, :], flat_l[at, :]), (high[rows_at, cut], low[rows_at, cut]), NN
                )
                for j in range(2):
                    x = got[:, j * LANES : (j + 1) * LANES]
                    if g > 0:
                        x = x + forced[2 * w + j, at, :]
                    forced[2 * w + j, at, :] = x
                return c

            lax.fori_loop(0, wide // 2, inner, 0)
            return carry

        lax.fori_loop(0, lats * levels // block, multiply, 0)

    thin = arrived.reshape(levels * count_rows // each, each, lats)

    def lone(i, carry):
        s = whole + i
        single_table(wave_own[pl.ds(s, devices, stride=slots), :], single, longitudes)
        here = returned.at[:, aligned(s * each, each), :]
        pltpu.make_async_copy(here, here, recv2_sem.at[groups - 1 + i]).wait()
        copy = pltpu.make_async_copy(here, thin.at[0:devices], pull_sem)
        copy.start()
        copy.wait()
        single_rows(dims, south, arrived, arrived, staged, flat_h)

        def multiply(m, carry):
            at = aligned(m * block, block)

            def inner(w, c):
                got = dot1(flat_h[at, :], single[:, aligned(w * 2 * LANES, 2 * LANES)], NN)
                for j in range(2):
                    forced[2 * w + j, at, :] = (
                        forced[2 * w + j, at, :] + got[:, j * LANES : (j + 1) * LANES]
                    )
                return c

            lax.fori_loop(0, wide // 2, inner, 0)
            return carry

        lax.fori_loop(0, lats * levels // block, multiply, 0)
        return carry

    lax.fori_loop(0, GROUP - 1, lone, 0)

    for s in range(max(slots - 2, 0), slots):
        pltpu.make_async_copy(spec.at[s % 2], spec_out.at[s], spec_sem.at[s % 2]).wait()
    sent = pl.ds(0, pairs * (devices - 1) * message)
    pltpu.make_async_copy(sending.at[sent, :], sending.at[sent, :], send_sem).wait()
    sent = pl.ds(0, slots * (devices - 1) * each)
    pltpu.make_async_copy(synth.at[sent, :], synth.at[sent, :], send2_sem).wait()
    final = returned.at[:, (slots - 1) * each : slots * each, :]
    pltpu.make_async_copy(final, final, recv2_sem.at[groups - 1 + GROUP - 1]).wait()


def finish_kernel(
    dims, returned, partial, spectral, slot_ref, grid_out, spec_out,
    pulled, turned, stacked, table, result, spec, wave_own,
    pull_sem, out_sem, spec_in, spec_done,
):
    bands, parts, lats, levels, longitudes, slots, depth, half = dims
    devices = bands * parts
    each = 2 * levels
    wide = longitudes // LANES
    south = lax.axis_index("band") >= bands // 2
    span = lats // BLOCKS
    block = span * levels

    def out_copy(m, slot):
        return pltpu.make_async_copy(
            result.at[slot], grid_out.at[aligned(m * span, span), :, :], out_sem.at[slot]
        )

    pull = pltpu.make_async_copy(
        returned.at[:, (slots - 1) * each : slots * each, :], pulled, pull_sem
    )
    pull.start()
    spec_copy = pltpu.make_async_copy(spectral, spec, spec_in)
    spec_copy.start()

    wave_columns(slot_ref, wave_own)
    single_table(wave_own[pl.ds(slots - 1, devices, stride=slots), :], table, longitudes)
    pull.wait()
    single_rows(dims, south, pulled.reshape(devices * each, lats), turned, 0, stacked)

    def outer(m, carry):
        slot = lax.rem(m, 2)
        @pl.when(m >= 2)
        def _():
            out_copy(m - 2, slot).wait()

        at = aligned(m * block, block)
        a = stacked[at, :]

        def inner(w, c):
            cut = aligned(w * 2 * LANES, 2 * LANES)
            got = dot1(a, table[:, cut], NN)
            for j in range(2):
                x = got[:, j * LANES : (j + 1) * LANES] + partial[2 * w + j, at, :]
                to = aligned((2 * w + j) * LANES, LANES)
                result[slot, :, :, to] = x.reshape(span, levels, LANES)
            return c

        lax.fori_loop(0, wide // 2, inner, 0)
        out_copy(m, slot).start()

        return carry

    spec_copy.wait()
    done = pltpu.make_async_copy(spec, spec_out, spec_done)
    done.start()
    lax.fori_loop(0, BLOCKS, outer, 0)
    for m in range(BLOCKS - 2, BLOCKS):
        out_copy(m, m % 2).wait()
    done.wait()


def shards(
    grid_adjoint, trajectory, legendre_north, slot_wavenumber, spectral_state,
    to_modes, from_modes, rates,
):
    lats, levels, longitudes = grid_adjoint.shape
    slots, depth, half = legendre_north.shape
    bands = lax.axis_size("band")
    parts = lax.axis_size("lev")
    devices = bands * parts
    every = parts * levels
    fits = (
        lats == LANES and levels == 2 * SUB and 4 * devices == LANES
        and longitudes % (2 * LANES) == 0 and longitudes & (longitudes - 1) == 0
        and bands % 2 == 0 and half == bands // 2 * lats and depth % LANES == 0
        and slots % GROUP == 0 and devices * slots % LANES == 0 and levels // PAIR >= 3 and 2 * every == LANES and to_modes.shape[0] == every
    )
    if not fits:
        return plain_shards(
            grid_adjoint, trajectory, legendre_north, slot_wavenumber, spectral_state,
            to_modes, from_modes, rates,
        )
    dims = (bands, parts, lats, levels, longitudes, slots, depth, half)
    count = devices * slots * 2
    hbm = pl.BlockSpec(memory_space=pl.ANY)
    vmem = pl.BlockSpec(memory_space=pltpu.VMEM)
    f32, bf16 = jnp.float32, jnp.bfloat16
    dma = pltpu.SemaphoreType.DMA
    wide = longitudes // LANES
    numbers = slot_wavenumber.reshape(-1, LANES)
    state = spectral_state.transpose(0, 2, 3, 1).reshape(slots, 2 * every, depth)
    square = pltpu.VMEM((2 * every, 2 * every), f32)
    spectral, returned, partial = pl.pallas_call(
        functools.partial(forward_kernel, dims),
        out_shape=(
            jax.ShapeDtypeStruct((slots, 2 * every, depth), f32),
            jax.ShapeDtypeStruct((devices, slots * 2 * levels, lats), f32),
            pltpu.VMEM((wide, lats * levels, LANES), f32),
        ),
        in_specs=[hbm, hbm, vmem, hbm, hbm, vmem, vmem, vmem],
        out_specs=(hbm, hbm, vmem),
        scratch_shapes=[
            pltpu.VMEM((count, longitudes), bf16),
            pltpu.VMEM((count, longitudes), bf16),
            pltpu.VMEM((2, lats // PIECES, SUB, longitudes), f32),
            pltpu.VMEM((2, lats // PIECES, SUB, longitudes), f32),
            pltpu.VMEM((PAIR * lats, longitudes), bf16),
            pltpu.VMEM((PAIR * lats, longitudes), bf16),
            pltpu.VMEM((levels * count, lats), f32),
            pltpu.VMEM((levels * count, lats), f32),
            pltpu.VMEM((count * levels, lats), f32),
            pltpu.VMEM((2, depth, half), f32),
            pltpu.VMEM((2, 2 * every, depth), f32),
            pltpu.VMEM((2, 2 * every, depth), f32),
            square, square, square,
            pltpu.VMEM((lats * levels, devices * 2 * GROUP), bf16),
            pltpu.VMEM((lats * levels, devices * 2 * GROUP), bf16),
            pltpu.VMEM((devices * slots, LANES), jnp.int32),
            pltpu.VMEM((count, LANES), jnp.int32),
            square,
            pltpu.VMEM((2 * LANES, longitudes), bf16),
            dma((2,)), dma((2,)), dma, dma((slots // GROUP + 1,)), dma,
            dma((slots // GROUP - 1 + GROUP,)),
            dma((2,)), dma((2,)), dma((2,)), dma,
        ],
        compiler_params=pltpu.CompilerParams(
            collective_id=0, has_side_effects=True, vmem_limit_bytes=GRANT
        ),
        name="spectral",
    )(
        grid_adjoint, trajectory, numbers, legendre_north, state, rates.reshape(1, every),
        to_modes, from_modes,
    )
    grid, spectral = pl.pallas_call(
        functools.partial(finish_kernel, dims),
        out_shape=(
            jax.ShapeDtypeStruct(grid_adjoint.shape, f32),
            jax.ShapeDtypeStruct(spectral.shape, f32),
        ),
        in_specs=[hbm, vmem, hbm, vmem],
        out_specs=(hbm, hbm),
        scratch_shapes=[
            pltpu.VMEM((devices, 2 * levels, lats), f32),
            pltpu.VMEM((lats * levels, LANES), f32),
            pltpu.VMEM((lats * levels, 2 * LANES), bf16),
            pltpu.VMEM((2 * LANES, longitudes), bf16),
            pltpu.VMEM((2, lats // BLOCKS, levels, longitudes), f32),
            pltpu.VMEM(spectral.shape, f32),
            pltpu.VMEM((devices * slots, LANES), jnp.int32),
            dma, dma((2,)), dma, dma,
        ],
        compiler_params=pltpu.CompilerParams(vmem_limit_bytes=LAST_GRANT),
        name="finish",
    )(returned, pltpu.with_memory_space_constraint(partial, pltpu.VMEM), spectral, numbers)
    return spectral.reshape(slots, 2, every, depth).transpose(0, 3, 1, 2), grid


def solution(mesh):
    return jax.shard_map(
        shards,
        mesh=mesh,
        in_specs=(
            P("band", "lev", None),
            P("band", "lev", None),
            P(("band", "lev"), None, None),
            P(),
            P(("band", "lev"), None, None, None),
            P(),
            P(),
            P(),
        ),
        out_specs=(P(("band", "lev"), None, None, None), P("band", "lev", None)),
        check_vma=False,
    )
```

```python
import functools
import math

import jax
import jax.numpy as jnp
from jax import lax
from jax.experimental import pallas as pl
from jax.experimental.pallas import tpu as pltpu
from jax.sharding import PartitionSpec as P

PRECISION = lax.Precision.HIGH


def angle_parts(steps, waves, longitudes):
    phase = waves[:, None] * steps[None, :] % longitudes
    angles = phase.astype(jnp.float32) * (2.0 * jnp.pi / longitudes)
    return jnp.cos(angles), jnp.sin(angles)


def wave_rows(longitudes, waves, devices):
    fine = min(128, longitudes)
    coarse = longitudes // fine
    scale = jnp.float32(longitudes) ** (-0.5)
    cos_a, sin_a = angle_parts(jnp.arange(coarse, dtype=jnp.int32) * fine, waves, longitudes)
    cos_b, sin_b = angle_parts(jnp.arange(fine, dtype=jnp.int32), waves, longitudes)
    cos_a, sin_a, cos_b, sin_b = lax.optimization_barrier(
        (cos_a * scale, sin_a * scale, cos_b, sin_b)
    )
    cos_at = [cos_a[:, i : i + 1] * cos_b - sin_a[:, i : i + 1] * sin_b for i in range(coarse)]
    sin_at = [-sin_a[:, i : i + 1] * cos_b - cos_a[:, i : i + 1] * sin_b for i in range(coarse)]
    cosine = jnp.concatenate(cos_at, axis=1).reshape(devices, -1, longitudes)
    negsine = jnp.concatenate(sin_at, axis=1).reshape(devices, -1, longitudes)
    return jnp.stack([cosine, negsine], axis=1).reshape(-1, longitudes)


def exchange(data):
    return lax.all_to_all(data, ("band", "lev"), split_axis=0, concat_axis=0, tiled=True)


def plain_shards(
    grid_adjoint,
    trajectory,
    legendre_north,
    slot_wavenumber,
    spectral_state,
    to_modes,
    from_modes,
    rates,
):
    lats, levels, longitudes = grid_adjoint.shape
    slots, depth, half = legendre_north.shape
    bands = lax.axis_size("band")
    parts = lax.axis_size("lev")
    devices = bands * parts
    every = parts * levels
    me = lax.axis_index("band") * parts + lax.axis_index("lev")
    own_waves = lax.dynamic_slice_in_dim(slot_wavenumber, me * slots, slots)
    table = wave_rows(longitudes, slot_wavenumber, devices)
    even_k = jnp.arange(depth, dtype=jnp.int32) % 2 == 0

    forced = grid_adjoint * (1.0 + trajectory)
    rows = jnp.swapaxes(forced, 0, 1).reshape(levels * lats, longitudes)
    fourier = lax.dot_general(
        table, rows, (((1,), (1,)), ((), ())), precision=PRECISION, preferred_element_type=jnp.float32
    )
    arrived = exchange(fourier.reshape(devices, 2 * slots, levels * lats))
    arrived = arrived.reshape(bands, parts, 2, slots, levels, lats)
    arrived = arrived.transpose(3, 2, 1, 4, 0, 5).reshape(slots, 2 * every, bands * lats)
    north = arrived[:, :, :half]
    south = arrived[:, :, half:][:, :, ::-1]
    folded = jnp.concatenate([north + south, north - south], axis=1)
    both = lax.dot_general(
        folded, legendre_north, (((2,), (2,)), ((0,), (0,))), precision=PRECISION,
        preferred_element_type=jnp.float32,
    )
    analysed = jnp.where(even_k, both[:, : 2 * every], both[:, 2 * every :])
    analysed = analysed.reshape(slots, 2, every, depth)

    state = spectral_state.transpose(0, 2, 3, 1)
    depth_index = jnp.arange(depth, dtype=jnp.int32)
    valid = (depth_index[None, :] < depth - own_waves[:, None]).astype(jnp.float32)
    total = (analysed + state) * valid[:, None, None, :]
    degree = (own_waves[:, None] + depth_index[None, :]).astype(jnp.float32)
    helm = degree * (degree + 1.0) / (depth * (depth - 1.0))
    modes = jnp.einsum("sclk,pl->scpk", total, to_modes, precision=PRECISION)
    scaled = modes / (1.0 + helm[:, None, None, :] * rates[None, None, :, None])
    spectral = jnp.einsum("scpk,lp->sclk", scaled, from_modes, precision=PRECISION)

    coeffs = spectral.reshape(slots, 2 * every, depth)
    split = jnp.concatenate(
        [jnp.where(even_k, coeffs, 0.0), jnp.where(even_k, 0.0, coeffs)], axis=1
    )
    halves = lax.dot_general(
        split, legendre_north, (((2,), (1,)), ((0,), (0,))), precision=PRECISION,
        preferred_element_type=jnp.float32,
    )
    first = halves[:, : 2 * every]
    second = halves[:, 2 * every :]
    whole = jnp.concatenate([first + second, (first - second)[:, :, ::-1]], axis=2)
    whole = whole.reshape(slots, 2, parts, levels, bands, lats).transpose(4, 2, 1, 0, 3, 5)
    returned = exchange(whole.reshape(devices, 2 * slots, levels * lats))
    grid = lax.dot_general(
        returned.reshape(devices * 2 * slots, levels, lats),
        table,
        (((0,), (0,)), ((), ())),
        precision=PRECISION,
        preferred_element_type=jnp.float32,
    )
    return spectral.transpose(0, 3, 1, 2), jnp.swapaxes(grid, 0, 1)


LANES = 128
SUB = 8
PAIR = 2
PIECES = 8
GROUP = 4
BLOCKS = 4
GRANT = 50_000_000
LAST_GRANT = 44_000_000
NN = (((1,), (0,)), ((), ()))
NT = (((1,), (1,)), ((), ()))


def halves_of(x):
    high = x.astype(jnp.bfloat16)
    low = (x - high.astype(jnp.float32)).astype(jnp.bfloat16)
    return high, low


def dot1(x, y, dims):
    return lax.dot_general(x, y, dims, preferred_element_type=jnp.float32)


def dot3(a, b, dims):
    return dot1(a[0], b[0], dims) + (dot1(a[0], b[1], dims) + dot1(a[1], b[0], dims))


def aligned(start, size):
    return pl.ds(pl.multiple_of(start, size & -size), size)


def circle(phase, longitudes):
    quarter = longitudes // 4
    quadrant = phase >> (quarter.bit_length() - 1)
    rest = phase & (quarter - 1)
    flip = rest > quarter // 2
    angle = jnp.where(flip, quarter - rest, rest).astype(jnp.float32) * (
        2.0 * math.pi / longitudes
    )
    z = angle * angle
    sine = angle * (
        1.0 + z * (-1 / 6 + z * (1 / 120 + z * (-1 / 5040 + z * (1 / 362880))))
    )
    cosine = 1.0 + z * (
        -0.5 + z * (1 / 24 + z * (-1 / 720 + z * (1 / 40320 + z * (-1 / 3628800))))
    )
    c, s = jnp.where(flip, sine, cosine), jnp.where(flip, cosine, sine)
    odd = (quadrant & 1) == 1
    c, s = jnp.where(odd, s, c), jnp.where(odd, c, s)
    c = jnp.where((quadrant == 1) | (quadrant == 2), -c, c)
    return c, jnp.where(quadrant >= 2, -s, s)


def table_rows(waves, imaginary, longitudes):
    column = lax.broadcasted_iota(jnp.int32, waves.shape, 1)
    ca, sa = circle((waves * (column * LANES)) & (longitudes - 1), longitudes)
    cb, sb = circle((waves * column) & (longitudes - 1), longitudes)
    scale = float(longitudes) ** -0.5
    ca, sa = ca * scale, sa * scale
    p = jnp.where(imaginary, -sa, ca)
    q = jnp.where(imaginary, -ca, -sa)
    return [
        halves_of(p[:, i : i + 1] * cb + q[:, i : i + 1] * sb)
        for i in range(longitudes // LANES)
    ]


def wave_columns(slot_ref, own):
    for i in range(slot_ref.shape[0]):
        row = jnp.broadcast_to(slot_ref[i : i + 1, :].astype(jnp.float32), (LANES, LANES))
        own[i * LANES : (i + 1) * LANES, :] = row.T.astype(jnp.int32)


def last_rows(dims, south, flat, turned, stacked):
    bands, parts, lats, levels = dims[:4]

    def gather(l, carry):
        x = flat[pl.ds(l, LANES // 2, stride=levels), :]
        turned[pl.ds(l, lats, stride=levels), :] = jnp.concatenate([x, x], axis=0).T
        return carry

    lax.fori_loop(0, levels, gather, 0)
    keep = lax.broadcasted_iota(jnp.int32, (levels, LANES), 1) < LANES // 2

    def split(r, carry):
        lat = jnp.where(south, lats - 1 - r, r)
        h, l = halves_of(turned[aligned(lat * levels, levels), :])
        to = aligned(r * levels, levels)
        stacked[to, 0:LANES] = h
        stacked[to, LANES : 2 * LANES] = jnp.where(keep, l, jnp.zeros_like(l))
        return carry

    lax.fori_loop(0, lats, split, 0)


def senders(quarter):
    return (
        quarter,
        jnp.bitwise_xor(quarter, 1),
        jnp.where(quarter < 2, 3, 0),
        jnp.where(quarter < 2, 2, 1),
    )


ARRIVALS = (
    ((1, 0), (1, 1), (2, 0), (3, 0)),
    ((0, 0), (0, 1), (0, 2), (2, 1)),
    ((1, 2), (1, 3), (2, 2), (2, 3)),
    ((0, 3), (3, 1), (3, 2)),
)


def forward_kernel(
    dims,
    grid_ref, traj_ref, slot_ref, leg_ref, state_ref, rate_ref, to_ref, from_ref,
    spec_out, returned, forced,
    high, low, stage, traj, rows_h, rows_l, sending, arrived, synth, leg, state, spec,
    into, outof, back, flat_h, flat_l, wave_own, wave_ref, rate_col,
    grid_sem, traj_sem, send_sem, recv_sem, send2_sem, recv2_sem, leg_sem, state_sem, spec_sem,
    pull_sem,
):
    bands, parts, lats, levels, longitudes, slots, depth, half = dims
    devices = bands * parts
    every = parts * levels
    pairs = levels // PAIR
    unit = 2 * slots
    message = PAIR * unit
    small = 2 * GROUP
    tall = devices * small
    groups = slots // GROUP
    count_rows = devices * unit
    wide = longitudes // LANES
    band, lev = lax.axis_index("band"), lax.axis_index("lev")
    me = band * parts + lev
    south = band >= bands // 2

    def mesh_id(d):
        return (d // parts, lax.rem(d, parts))

    barrier = pltpu.get_barrier_semaphore()

    def greet(i, carry):
        pl.semaphore_signal(
            barrier, inc=1, device_id=mesh_id(jnp.bitwise_xor(me, i)),
            device_id_type=pl.DeviceIdType.MESH,
        )
        return carry

    lax.fori_loop(1, devices, greet, 0)

    span = lats // PIECES
    count = (levels // SUB) * PIECES

    def load_copies(piece):
        block, part = piece // PIECES, lax.rem(piece, PIECES)
        lat = aligned(part * span, span)
        cut = aligned(block * SUB, SUB)
        slot = lax.rem(piece, 2)
        return (
            pltpu.make_async_copy(grid_ref.at[lat, cut, :], stage.at[slot], grid_sem.at[slot]),
            pltpu.make_async_copy(traj_ref.at[lat, cut, :], traj.at[slot], traj_sem.at[slot]),
        )

    def load_piece(piece):
        for copy in load_copies(piece):
            copy.start()

    def finish_piece(piece):
        block, part = piece // PIECES, lax.rem(piece, PIECES)
        slot = lax.rem(piece, 2)
        for copy in load_copies(piece):
            copy.wait()

        def body(i, carry):
            at = part * span + i
            lat = jnp.where(south, lats - 1 - at, at)
            to = aligned((block * lats + lat) * SUB, SUB)
            x = stage[slot, i] * (1.0 + traj[slot, i])
            for j in range(wide):
                forced[j, to, :] = x[:, j * LANES : (j + 1) * LANES]
            return carry

        lax.fori_loop(0, span, body, 0)

        @pl.when(piece + 2 < count)
        def _():
            load_piece(piece + 2)

    load_piece(jnp.int32(0))
    load_piece(jnp.int32(1))

    def leg_copy(s, slot):
        return pltpu.make_async_copy(leg_ref.at[s], leg.at[slot], leg_sem.at[slot])

    def state_copy(s, slot):
        return pltpu.make_async_copy(state_ref.at[s], state.at[slot], state_sem.at[slot])

    wave_columns(slot_ref, wave_own)
    for g in range(groups):
        for i in range(GROUP):
            x = wave_own[pl.ds(g * GROUP + i, devices, stride=slots), :]
            for c in range(2):
                wave_ref[pl.ds(g * tall + 2 * i + c, devices, stride=small), :] = x
    rate = jnp.concatenate([rate_ref[...], rate_ref[...]], axis=1)
    rate_col[...] = jnp.broadcast_to(rate, (2 * every, 2 * every)).T
    block_rows = 64

    def fill(r, carry):
        at = aligned(r * block_rows, block_rows)
        waves = wave_ref[at, :]
        imaginary = (lax.broadcasted_iota(jnp.int32, waves.shape, 0) & 1) == 1
        for i, (h, l) in enumerate(table_rows(waves, imaginary, longitudes)):
            high[at, i * LANES : (i + 1) * LANES] = h
            low[at, i * LANES : (i + 1) * LANES] = l
        return carry

    def greeted_copy(source, target, d, sem):
        return pltpu.make_async_remote_copy(
            src_ref=sending.at[source, :],
            dst_ref=arrived.at[target, :],
            send_sem=send_sem,
            recv_sem=recv_sem.at[sem],
            device_id=mesh_id(d),
            device_id_type=pl.DeviceIdType.MESH,
        )

    def partner(i):
        return jnp.bitwise_xor(me, devices - 1 - i)

    def send_pair(q):
        to = aligned((me * pairs + q) * message, message)

        def body(i, carry):
            d = partner(i)
            greeted_copy(aligned((q * devices + d) * message, message), to, d, 0).start()
            return carry

        lax.fori_loop(0, devices - 1, body, 0)
        pltpu.make_async_copy(
            sending.at[aligned((q * devices + me) * message, message), :],
            arrived.at[to, :],
            recv_sem.at[0],
        ).start()

    def send_part(q, r, sem):
        def cut(first, h):
            return aligned(first * message + h * unit + r * small, small)

        def body(i, carry):
            d = partner(i)
            for h in range(PAIR):
                greeted_copy(
                    cut(q * devices + d, h), cut(me * pairs + q, h), d, sem
                ).start()
            return carry

        lax.fori_loop(0, devices - 1, body, 0)
        for h in range(PAIR):
            pltpu.make_async_copy(
                sending.at[cut(q * devices + me, h), :],
                arrived.at[cut(me * pairs + q, h), :],
                recv_sem.at[sem],
            ).start()

    def extract(q):
        first = q * PAIR
        block, local = first // SUB, lax.rem(first, SUB)
        for h in range(PAIR):
            for i in range(wide):
                x = forced[i, pl.ds(block * lats * SUB + local + h, lats, stride=SUB), :]
                rh, rl = halves_of(x)
                rows_h[h * lats : (h + 1) * lats, i * LANES : (i + 1) * LANES] = rh
                rows_l[h * lats : (h + 1) * lats, i * LANES : (i + 1) * LANES] = rl

    def transform(q, r):
        at = aligned(r * tall, tall)
        got = dot3((high[at, :], low[at, :]), (rows_h[...], rows_l[...]), NT)
        for d in range(devices):
            for h in range(PAIR):
                to = (q * devices + d) * message + h * unit + r * small
                sending[aligned(to, small), :] = got[
                    d * small : (d + 1) * small, h * lats : (h + 1) * lats
                ]

    per = SUB // PAIR
    blocks = levels // SUB

    def finish(i, c):
        finish_piece(i)
        return c

    lax.fori_loop(0, PIECES, finish, 0)
    extract(jnp.int32(0))

    def opening(r, carry):
        lax.fori_loop(r * (tall // block_rows), (r + 1) * (tall // block_rows), fill, 0)
        transform(0, r)

        @pl.when(r == 0)
        def _():
            pl.semaphore_wait(barrier, devices - 1)

        send_part(0, r, 0)
        return carry

    lax.fori_loop(0, groups, opening, 0)

    def middle(q, carry):
        @pl.when(lax.rem(q, per) == 0)
        def _():
            lax.fori_loop(q // per * PIECES, (q // per + 1) * PIECES, finish, 0)

        extract(q)

        def each_group(r, c):
            transform(q, r)
            return c

        lax.fori_loop(0, groups, each_group, 0)
        send_pair(q)
        return carry

    lax.fori_loop(1, pairs - 1, middle, 0)
    extract(jnp.int32(pairs - 1))

    def closing(r, carry):
        transform(pairs - 1, r)
        send_part(pairs - 1, r, r + 1)
        return carry

    lax.fori_loop(0, groups, closing, 0)
    for m in (into, outof, back):
        m[...] = jnp.zeros_like(m)
    for c in range(2):
        cut = slice(c * every, (c + 1) * every)
        into[cut, cut] = to_ref[...]
        outof[cut, cut] = from_ref[...]
        for p in range(parts):
            at = (2 * p + c) * levels
            back[at : at + levels, cut] = from_ref[p * levels : (p + 1) * levels, :]

    leg_copy(0, 0).start()
    state_copy(0, 0).start()
    before = arrived.at[pl.ds(0, (pairs - 1) * devices * message), :]
    pltpu.make_async_copy(before, before, recv_sem.at[0]).wait()
    last_part = arrived.at[pl.ds(0, devices * PAIR * small), :]

    lane = lax.broadcasted_iota(jnp.int32, (2 * every, depth), 1)
    even = lax.rem(lane, 2) == 0
    folds = bands // 2
    each = 2 * levels
    quarter = devices // 4
    order = senders(me // quarter)

    def column(b, s):
        return jnp.concatenate(
            [
                arrived[pl.ds(b * every * unit + 2 * s + c, every, stride=unit), :]
                for c in range(2)
            ],
            axis=0,
        )

    def send2_copy(s, d, sem):
        return pltpu.make_async_remote_copy(
            src_ref=synth.at[aligned((s * devices + d) * each, each), :],
            dst_ref=returned.at[me, aligned(s * each, each), :],
            send_sem=send2_sem,
            recv_sem=recv2_sem.at[sem],
            device_id=mesh_id(d),
            device_id_type=pl.DeviceIdType.MESH,
        )

    def one_slot(s, carry):
        slot = lax.rem(s, 2)
        sem = me // quarter * groups + s // GROUP

        @pl.when(lax.rem(s, GROUP) == 0)
        def _():
            pltpu.make_async_copy(last_part, last_part, recv_sem.at[s // GROUP + 1]).wait()

        @pl.when(s + 1 < slots)
        def _():
            leg_copy(s + 1, 1 - slot).start()
            state_copy(s + 1, 1 - slot).start()

        leg_copy(s, slot).wait()
        state_copy(s, slot).wait()
        functions = halves_of(leg[slot])
        evens, odds = [], []
        for b in range(folds):
            n, o = column(b, s), column(bands - 1 - b, s)
            evens.append(n + o)
            odds.append(n - o)
        folded = jnp.concatenate(
            [jnp.concatenate(evens, axis=1), jnp.concatenate(odds, axis=1)], axis=0
        )
        both = dot3(halves_of(folded), functions, NT)
        analysed = jnp.where(even, both[: 2 * every], both[2 * every :])
        wave = wave_ref[
            pl.ds((s // GROUP * devices + me) * small + lax.rem(s, GROUP) * 2, 1), :
        ]
        wave = jnp.concatenate([wave] * (depth // LANES), axis=1)
        order = lax.broadcasted_iota(jnp.int32, (1, depth), 1)
        degree = (wave + order).astype(jnp.float32)
        helm = degree * (degree + 1.0) / (depth * (depth - 1.0))
        total = jnp.where(order < depth - wave, analysed + state[slot], 0.0)
        modes = dot3(halves_of(into[...]), halves_of(total), NN)
        scaled = halves_of(modes / (1.0 + helm * rate_col[:, 0:1]))

        @pl.when(s >= 2)
        def _():
            pltpu.make_async_copy(spec.at[slot], spec_out.at[s - 2], spec_sem.at[slot]).wait()

        spec[slot] = dot3(halves_of(outof[...]), scaled, NN)
        pltpu.make_async_copy(spec.at[slot], spec_out.at[s], spec_sem.at[slot]).start()
        coeffs = dot3(halves_of(back[...]), scaled, NN)
        split = jnp.concatenate(
            [jnp.where(even, coeffs, 0.0), jnp.where(even, 0.0, coeffs)], axis=0
        )
        both = dot3(halves_of(split), functions, NN)
        first, second = both[: 2 * every], both[2 * every :]
        north, other = first + second, first - second
        base = s * devices * each
        for b in range(folds):
            cut = slice(b * LANES, (b + 1) * LANES)
            synth[aligned(base + b * 2 * every, 2 * every), :] = north[:, cut]
            synth[aligned(base + (bands - 1 - b) * 2 * every, 2 * every), :] = other[:, cut]

        def body(i, c):
            send2_copy(s, partner(i), sem).start()
            return c

        lax.fori_loop(0, devices - 1, body, 0)
        pltpu.make_async_copy(
            synth.at[aligned((s * devices + me) * each, each), :],
            returned.at[me, aligned(s * each, each), :],
            recv2_sem.at[sem],
        ).start()
        return carry

    lax.fori_loop(0, slots, one_slot, 0)

    rows = GROUP * each
    staged = devices * rows
    pulled = arrived.reshape(levels * count_rows // rows, rows, lats)
    block = 1024
    piece = quarter * small

    def landed(c, g):
        return returned.at[aligned(order[c] * quarter, quarter), g * rows : (g + 1) * rows, :]

    for number, units in enumerate(ARRIVALS):
        copies = []
        for u, (c, g) in enumerate(units):
            here = landed(c, g)
            pltpu.make_async_copy(here, here, recv2_sem.at[order[c] * groups + g]).wait()
            copy = pltpu.make_async_copy(
                here, pulled.at[u * quarter : (u + 1) * quarter], pull_sem.at[u]
            )
            copy.start()
            copies.append(copy)
        for copy in copies:
            copy.wait()
        filled = len(units) * piece

        def pull(l, carry):
            x = arrived[pl.ds(l, tall, stride=levels), :]
            if filled < tall:
                x = jnp.where(lax.broadcasted_iota(jnp.int32, x.shape, 0) < filled, x, 0.0)
            x = x.T
            for j in range(tall // LANES):
                arrived[pl.ds(staged + j * lats * levels + l, lats, stride=levels), :] = x[
                    :, j * LANES : (j + 1) * LANES
                ]
            return carry

        lax.fori_loop(0, levels, pull, 0)

        def split(r, carry):
            lat = jnp.where(south, lats - 1 - r, r)
            to = aligned(r * levels, levels)
            for j in range(tall // LANES):
                x = arrived[aligned(staged + (j * lats + lat) * levels, levels), :]
                h, l = halves_of(x)
                flat_h[to, j * LANES : (j + 1) * LANES] = h
                flat_l[to, j * LANES : (j + 1) * LANES] = l
            return carry

        lax.fori_loop(0, lats, split, 0)
        chosen = (units + units[:1])[: tall // piece]

        def multiply(m, carry):
            at = aligned(m * block, block)

            def inner(w, carry2):
                cut = aligned(w * 2 * LANES, 2 * LANES)
                table = [
                    jnp.concatenate(
                        [part[aligned(g * tall + order[c] * piece, piece), cut] for c, g in chosen],
                        axis=0,
                    )
                    for part in (high, low)
                ]
                got = dot3((flat_h[at, :], flat_l[at, :]), table, NN)
                for j in range(2):
                    x = got[:, j * LANES : (j + 1) * LANES]
                    if number > 0:
                        x = x + forced[2 * w + j, at, :]
                    forced[2 * w + j, at, :] = x
                return carry2

            lax.fori_loop(0, wide // 2, inner, 0)
            return carry

        lax.fori_loop(0, lats * levels // block, multiply, 0)

    for s in range(max(slots - 2, 0), slots):
        pltpu.make_async_copy(spec.at[s % 2], spec_out.at[s], spec_sem.at[s % 2]).wait()
    sent = pl.ds(0, pairs * (devices - 1) * message)
    pltpu.make_async_copy(sending.at[sent, :], sending.at[sent, :], send_sem).wait()
    sent = pl.ds(0, slots * (devices - 1) * each)
    pltpu.make_async_copy(synth.at[sent, :], synth.at[sent, :], send2_sem).wait()
    final = landed(3, groups - 1)
    pltpu.make_async_copy(final, final, recv2_sem.at[order[3] * groups + groups - 1]).wait()


def finish_kernel(
    dims, returned, partial, spectral, slot_ref, grid_out, spec_out,
    pulled, turned, stacked, table, result, spec, wave_own, waves,
    pull_sem, out_sem, spec_in, spec_done,
):
    bands, parts, lats, levels, longitudes, slots, depth, half = dims
    devices = bands * parts
    each = 2 * levels
    wide = longitudes // LANES
    south = lax.axis_index("band") >= bands // 2
    span = lats // BLOCKS
    block = span * levels

    def out_copy(m, slot):
        return pltpu.make_async_copy(
            result.at[slot], grid_out.at[aligned(m * span, span), :, :], out_sem.at[slot]
        )

    quarter = devices // 4
    me = lax.axis_index("band") * parts + lax.axis_index("lev")
    first = senders(me // quarter)[3] * quarter
    rows = GROUP * each
    pull = pltpu.make_async_copy(
        returned.at[aligned(first, quarter), slots * each - rows : slots * each, :], pulled, pull_sem
    )
    pull.start()
    spec_copy = pltpu.make_async_copy(spectral, spec, spec_in)
    spec_copy.start()

    wave_columns(slot_ref, wave_own)
    for i in range(GROUP):
        x = wave_own[pl.ds(first * slots + slots - GROUP + i, quarter, stride=slots), :]
        for c in range(2):
            waves[pl.ds(2 * i + c, quarter, stride=2 * GROUP), :] = x
    imaginary = (lax.broadcasted_iota(jnp.int32, waves.shape, 0) & 1) == 1
    short = quarter * 2 * GROUP
    for i, (h, l) in enumerate(table_rows(waves[...], imaginary, longitudes)):
        cut = slice(i * LANES, (i + 1) * LANES)
        table[0:short, cut] = h
        table[short : 2 * short, cut] = l
        table[2 * short : 3 * short, cut] = h
        table[3 * short : 4 * short, cut] = jnp.zeros_like(h)
    pull.wait()
    last_rows(dims, south, pulled.reshape(quarter * rows, lats), turned, stacked)

    def outer(m, carry):
        slot = lax.rem(m, 2)
        @pl.when(m >= 2)
        def _():
            out_copy(m - 2, slot).wait()

        at = aligned(m * block, block)
        a = stacked[at, :]

        def inner(w, c):
            cut = aligned(w * 2 * LANES, 2 * LANES)
            got = dot1(a, table[:, cut], NN)
            for j in range(2):
                x = got[:, j * LANES : (j + 1) * LANES] + partial[2 * w + j, at, :]
                to = aligned((2 * w + j) * LANES, LANES)
                result[slot, :, :, to] = x.reshape(span, levels, LANES)
            return c

        lax.fori_loop(0, wide // 2, inner, 0)
        out_copy(m, slot).start()

        return carry

    spec_copy.wait()
    done = pltpu.make_async_copy(spec, spec_out, spec_done)
    done.start()
    lax.fori_loop(0, BLOCKS, outer, 0)
    for m in range(BLOCKS - 2, BLOCKS):
        out_copy(m, m % 2).wait()
    done.wait()


def shards(
    grid_adjoint, trajectory, legendre_north, slot_wavenumber, spectral_state,
    to_modes, from_modes, rates,
):
    lats, levels, longitudes = grid_adjoint.shape
    slots, depth, half = legendre_north.shape
    bands = lax.axis_size("band")
    parts = lax.axis_size("lev")
    devices = bands * parts
    every = parts * levels
    fits = (
        lats == LANES and levels == 2 * SUB and 4 * devices == LANES
        and longitudes % (2 * LANES) == 0 and longitudes & (longitudes - 1) == 0
        and bands % 2 == 0 and half == bands // 2 * lats and depth % LANES == 0
        and slots == 4 * GROUP and devices * slots % LANES == 0 and levels // PAIR >= 3 and 2 * every == LANES and to_modes.shape[0] == every
    )
    if not fits:
        return plain_shards(
            grid_adjoint, trajectory, legendre_north, slot_wavenumber, spectral_state,
            to_modes, from_modes, rates,
        )
    dims = (bands, parts, lats, levels, longitudes, slots, depth, half)
    count = devices * slots * 2
    hbm = pl.BlockSpec(memory_space=pl.ANY)
    vmem = pl.BlockSpec(memory_space=pltpu.VMEM)
    f32, bf16 = jnp.float32, jnp.bfloat16
    dma = pltpu.SemaphoreType.DMA
    wide = longitudes // LANES
    numbers = slot_wavenumber.reshape(-1, LANES)
    state = spectral_state.transpose(0, 2, 3, 1).reshape(slots, 2 * every, depth)
    square = pltpu.VMEM((2 * every, 2 * every), f32)
    spectral, returned, partial = pl.pallas_call(
        functools.partial(forward_kernel, dims),
        out_shape=(
            jax.ShapeDtypeStruct((slots, 2 * every, depth), f32),
            jax.ShapeDtypeStruct((devices, slots * 2 * levels, lats), f32),
            pltpu.VMEM((wide, lats * levels, LANES), f32),
        ),
        in_specs=[hbm, hbm, vmem, hbm, hbm, vmem, vmem, vmem],
        out_specs=(hbm, hbm, vmem),
        scratch_shapes=[
            pltpu.VMEM((count, longitudes), bf16),
            pltpu.VMEM((count, longitudes), bf16),
            pltpu.VMEM((2, lats // PIECES, SUB, longitudes), f32),
            pltpu.VMEM((2, lats // PIECES, SUB, longitudes), f32),
            pltpu.VMEM((PAIR * lats, longitudes), bf16),
            pltpu.VMEM((PAIR * lats, longitudes), bf16),
            pltpu.VMEM((levels * count, lats), f32),
            pltpu.VMEM((levels * count, lats), f32),
            pltpu.VMEM((count * levels, lats), f32),
            pltpu.VMEM((2, depth, half), f32),
            pltpu.VMEM((2, 2 * every, depth), f32),
            pltpu.VMEM((2, 2 * every, depth), f32),
            square, square, square,
            pltpu.VMEM((lats * levels, devices * 2 * GROUP), bf16),
            pltpu.VMEM((lats * levels, devices * 2 * GROUP), bf16),
            pltpu.VMEM((devices * slots, LANES), jnp.int32),
            pltpu.VMEM((count, LANES), jnp.int32),
            square,
            dma((2,)), dma((2,)), dma, dma((slots // GROUP + 1,)), dma,
            dma((slots,)),
            dma((2,)), dma((2,)), dma((2,)), dma((4,)),
        ],
        compiler_params=pltpu.CompilerParams(
            collective_id=0, has_side_effects=True, vmem_limit_bytes=GRANT
        ),
        name="spectral",
    )(
        grid_adjoint, trajectory, numbers, legendre_north, state, rates.reshape(1, every),
        to_modes, from_modes,
    )
    grid, spectral = pl.pallas_call(
        functools.partial(finish_kernel, dims),
        out_shape=(
            jax.ShapeDtypeStruct(grid_adjoint.shape, f32),
            jax.ShapeDtypeStruct(spectral.shape, f32),
        ),
        in_specs=[hbm, vmem, hbm, vmem],
        out_specs=(hbm, hbm),
        scratch_shapes=[
            pltpu.VMEM((devices // 4, GROUP * 2 * levels, lats), f32),
            pltpu.VMEM((lats * levels, LANES), f32),
            pltpu.VMEM((lats * levels, 2 * LANES), bf16),
            pltpu.VMEM((2 * LANES, longitudes), bf16),
            pltpu.VMEM((2, lats // BLOCKS, levels, longitudes), f32),
            pltpu.VMEM(spectral.shape, f32),
            pltpu.VMEM((devices * slots, LANES), jnp.int32),
            pltpu.VMEM((LANES // 2, LANES), jnp.int32),
            dma, dma((2,)), dma, dma,
        ],
        compiler_params=pltpu.CompilerParams(vmem_limit_bytes=LAST_GRANT),
        name="finish",
    )(returned, pltpu.with_memory_space_constraint(partial, pltpu.VMEM), spectral, numbers)
    return spectral.reshape(slots, 2, every, depth).transpose(0, 3, 1, 2), grid


def solution(mesh):
    return jax.shard_map(
        shards,
        mesh=mesh,
        in_specs=(
            P("band", "lev", None),
            P("band", "lev", None),
            P(("band", "lev"), None, None),
            P(),
            P(("band", "lev"), None, None, None),
            P(),
            P(),
            P(),
        ),
        out_specs=(P(("band", "lev"), None, None, None), P("band", "lev", None)),
        check_vma=False,
    )
```

```python
import functools
import math

import jax
import jax.numpy as jnp
from jax import lax
from jax.experimental import pallas as pl
from jax.experimental.pallas import tpu as pltpu
from jax.sharding import PartitionSpec as P

PRECISION = lax.Precision.HIGH


def angle_parts(steps, waves, longitudes):
    phase = waves[:, None] * steps[None, :] % longitudes
    angles = phase.astype(jnp.float32) * (2.0 * jnp.pi / longitudes)
    return jnp.cos(angles), jnp.sin(angles)


def wave_rows(longitudes, waves, devices):
    fine = min(128, longitudes)
    coarse = longitudes // fine
    scale = jnp.float32(longitudes) ** (-0.5)
    cos_a, sin_a = angle_parts(jnp.arange(coarse, dtype=jnp.int32) * fine, waves, longitudes)
    cos_b, sin_b = angle_parts(jnp.arange(fine, dtype=jnp.int32), waves, longitudes)
    cos_a, sin_a, cos_b, sin_b = lax.optimization_barrier(
        (cos_a * scale, sin_a * scale, cos_b, sin_b)
    )
    cos_at = [cos_a[:, i : i + 1] * cos_b - sin_a[:, i : i + 1] * sin_b for i in range(coarse)]
    sin_at = [-sin_a[:, i : i + 1] * cos_b - cos_a[:, i : i + 1] * sin_b for i in range(coarse)]
    cosine = jnp.concatenate(cos_at, axis=1).reshape(devices, -1, longitudes)
    negsine = jnp.concatenate(sin_at, axis=1).reshape(devices, -1, longitudes)
    return jnp.stack([cosine, negsine], axis=1).reshape(-1, longitudes)


def exchange(data):
    return lax.all_to_all(data, ("band", "lev"), split_axis=0, concat_axis=0, tiled=True)


def plain_shards(
    grid_adjoint,
    trajectory,
    legendre_north,
    slot_wavenumber,
    spectral_state,
    to_modes,
    from_modes,
    rates,
):
    lats, levels, longitudes = grid_adjoint.shape
    slots, depth, half = legendre_north.shape
    bands = lax.axis_size("band")
    parts = lax.axis_size("lev")
    devices = bands * parts
    every = parts * levels
    me = lax.axis_index("band") * parts + lax.axis_index("lev")
    own_waves = lax.dynamic_slice_in_dim(slot_wavenumber, me * slots, slots)
    table = wave_rows(longitudes, slot_wavenumber, devices)
    even_k = jnp.arange(depth, dtype=jnp.int32) % 2 == 0

    forced = grid_adjoint * (1.0 + trajectory)
    rows = jnp.swapaxes(forced, 0, 1).reshape(levels * lats, longitudes)
    fourier = lax.dot_general(
        table, rows, (((1,), (1,)), ((), ())), precision=PRECISION, preferred_element_type=jnp.float32
    )
    arrived = exchange(fourier.reshape(devices, 2 * slots, levels * lats))
    arrived = arrived.reshape(bands, parts, 2, slots, levels, lats)
    arrived = arrived.transpose(3, 2, 1, 4, 0, 5).reshape(slots, 2 * every, bands * lats)
    north = arrived[:, :, :half]
    south = arrived[:, :, half:][:, :, ::-1]
    folded = jnp.concatenate([north + south, north - south], axis=1)
    both = lax.dot_general(
        folded, legendre_north, (((2,), (2,)), ((0,), (0,))), precision=PRECISION,
        preferred_element_type=jnp.float32,
    )
    analysed = jnp.where(even_k, both[:, : 2 * every], both[:, 2 * every :])
    analysed = analysed.reshape(slots, 2, every, depth)

    state = spectral_state.transpose(0, 2, 3, 1)
    depth_index = jnp.arange(depth, dtype=jnp.int32)
    valid = (depth_index[None, :] < depth - own_waves[:, None]).astype(jnp.float32)
    total = (analysed + state) * valid[:, None, None, :]
    degree = (own_waves[:, None] + depth_index[None, :]).astype(jnp.float32)
    helm = degree * (degree + 1.0) / (depth * (depth - 1.0))
    modes = jnp.einsum("sclk,pl->scpk", total, to_modes, precision=PRECISION)
    scaled = modes / (1.0 + helm[:, None, None, :] * rates[None, None, :, None])
    spectral = jnp.einsum("scpk,lp->sclk", scaled, from_modes, precision=PRECISION)

    coeffs = spectral.reshape(slots, 2 * every, depth)
    split = jnp.concatenate(
        [jnp.where(even_k, coeffs, 0.0), jnp.where(even_k, 0.0, coeffs)], axis=1
    )
    halves = lax.dot_general(
        split, legendre_north, (((2,), (1,)), ((0,), (0,))), precision=PRECISION,
        preferred_element_type=jnp.float32,
    )
    first = halves[:, : 2 * every]
    second = halves[:, 2 * every :]
    whole = jnp.concatenate([first + second, (first - second)[:, :, ::-1]], axis=2)
    whole = whole.reshape(slots, 2, parts, levels, bands, lats).transpose(4, 2, 1, 0, 3, 5)
    returned = exchange(whole.reshape(devices, 2 * slots, levels * lats))
    grid = lax.dot_general(
        returned.reshape(devices * 2 * slots, levels, lats),
        table,
        (((0,), (0,)), ((), ())),
        precision=PRECISION,
        preferred_element_type=jnp.float32,
    )
    return spectral.transpose(0, 3, 1, 2), jnp.swapaxes(grid, 0, 1)


LANES = 128
SUB = 8
PAIR = 2
PIECES = 8
GROUP = 4
GRANT = 50_000_000
LAST_GRANT = 44_000_000
NN = (((1,), (0,)), ((), ()))
NT = (((1,), (1,)), ((), ()))


def halves_of(x):
    high = x.astype(jnp.bfloat16)
    low = (x - high.astype(jnp.float32)).astype(jnp.bfloat16)
    return high, low


def dot1(x, y, dims):
    return lax.dot_general(x, y, dims, preferred_element_type=jnp.float32)


def dot3(a, b, dims):
    return dot1(a[0], b[0], dims) + (dot1(a[0], b[1], dims) + dot1(a[1], b[0], dims))


def aligned(start, size):
    return pl.ds(pl.multiple_of(start, size & -size), size)


def circle(phase, longitudes):
    quarter = longitudes // 4
    quadrant = phase >> (quarter.bit_length() - 1)
    rest = phase & (quarter - 1)
    flip = rest > quarter // 2
    angle = jnp.where(flip, quarter - rest, rest).astype(jnp.float32) * (
        2.0 * math.pi / longitudes
    )
    z = angle * angle
    sine = angle * (
        1.0 + z * (-1 / 6 + z * (1 / 120 + z * (-1 / 5040 + z * (1 / 362880))))
    )
    cosine = 1.0 + z * (
        -0.5 + z * (1 / 24 + z * (-1 / 720 + z * (1 / 40320 + z * (-1 / 3628800))))
    )
    c, s = jnp.where(flip, sine, cosine), jnp.where(flip, cosine, sine)
    odd = (quadrant & 1) == 1
    c, s = jnp.where(odd, s, c), jnp.where(odd, c, s)
    c = jnp.where((quadrant == 1) | (quadrant == 2), -c, c)
    return c, jnp.where(quadrant >= 2, -s, s)


def table_rows(waves, imaginary, longitudes):
    column = lax.broadcasted_iota(jnp.int32, waves.shape, 1)
    ca, sa = circle((waves * (column * LANES)) & (longitudes - 1), longitudes)
    cb, sb = circle((waves * column) & (longitudes - 1), longitudes)
    scale = float(longitudes) ** -0.5
    ca, sa = ca * scale, sa * scale
    p = jnp.where(imaginary, -sa, ca)
    q = jnp.where(imaginary, -ca, -sa)
    return [
        halves_of(p[:, i : i + 1] * cb + q[:, i : i + 1] * sb)
        for i in range(longitudes // LANES)
    ]


def wave_columns(slot_ref, own):
    for i in range(slot_ref.shape[0]):
        row = jnp.broadcast_to(slot_ref[i : i + 1, :].astype(jnp.float32), (LANES, LANES))
        own[i * LANES : (i + 1) * LANES, :] = row.T.astype(jnp.int32)


def senders(quarter):
    return (
        quarter,
        jnp.bitwise_xor(quarter, 1),
        jnp.where(quarter < 2, 3, 0),
        jnp.where(quarter < 2, 2, 1),
    )


ARRIVALS = (
    ((1, 0), (1, 1), (2, 0), (3, 0)),
    ((0, 0), (0, 1), (0, 2), (2, 1)),
    ((1, 2), (1, 3), (2, 2), (2, 3)),
    ((0, 3), (3, 1), (3, 2)),
)


def forward_kernel(
    dims,
    grid_ref, traj_ref, slot_in, leg_ref, state_ref, rate_in, to_in, from_in,
    spec_out, returned, forced,
    high, low, stage, traj, rows_h, rows_l, sending, arrived, synth, leg, state, spec,
    into, outof, back, flat_h, flat_l, wave_own, wave_ref, rate_col,
    slot_ref, rate_ref, to_ref, from_ref,
    grid_sem, traj_sem, send_sem, recv_sem, send2_sem, recv2_sem, leg_sem, state_sem, spec_sem,
    pull_sem, tiny_sem,
):
    bands, parts, lats, levels, longitudes, slots, depth, half = dims
    devices = bands * parts
    every = parts * levels
    pairs = levels // PAIR
    unit = 2 * slots
    message = PAIR * unit
    small = 2 * GROUP
    tall = devices * small
    groups = slots // GROUP
    count_rows = devices * unit
    wide = longitudes // LANES
    band, lev = lax.axis_index("band"), lax.axis_index("lev")
    me = band * parts + lev
    south = band >= bands // 2

    def mesh_id(d):
        return (d // parts, lax.rem(d, parts))

    tiny = [
        pltpu.make_async_copy(source, target, tiny_sem.at[i])
        for i, (source, target) in enumerate(
            ((slot_in, slot_ref), (rate_in, rate_ref), (to_in, to_ref), (from_in, from_ref))
        )
    ]
    for copy in tiny:
        copy.start()
    barrier = pltpu.get_barrier_semaphore()

    def greet(i, carry):
        pl.semaphore_signal(
            barrier, inc=1, device_id=mesh_id(jnp.bitwise_xor(me, i)),
            device_id_type=pl.DeviceIdType.MESH,
        )
        return carry


    span = lats // PIECES
    count = (levels // SUB) * PIECES

    def load_copies(piece):
        block, part = piece // PIECES, lax.rem(piece, PIECES)
        lat = aligned(part * span, span)
        cut = aligned(block * SUB, SUB)
        slot = lax.rem(piece, 2)
        return (
            pltpu.make_async_copy(grid_ref.at[lat, cut, :], stage.at[slot], grid_sem.at[slot]),
            pltpu.make_async_copy(traj_ref.at[lat, cut, :], traj.at[slot], traj_sem.at[slot]),
        )

    def load_piece(piece):
        for copy in load_copies(piece):
            copy.start()

    def finish_piece(piece):
        block, part = piece // PIECES, lax.rem(piece, PIECES)
        slot = lax.rem(piece, 2)
        for copy in load_copies(piece):
            copy.wait()

        def body(i, carry):
            at = part * span + i
            lat = jnp.where(south, lats - 1 - at, at)
            to = aligned((block * lats + lat) * SUB, SUB)
            x = stage[slot, i] * (1.0 + traj[slot, i])
            for j in range(wide):
                forced[j, to, :] = x[:, j * LANES : (j + 1) * LANES]
            return carry

        lax.fori_loop(0, span, body, 0)

        @pl.when(piece + 2 < count)
        def _():
            load_piece(piece + 2)

    load_piece(jnp.int32(0))
    load_piece(jnp.int32(1))
    lax.fori_loop(1, devices, greet, 0)

    def leg_copy(s, slot):
        return pltpu.make_async_copy(leg_ref.at[s], leg.at[slot], leg_sem.at[slot])

    def state_copy(s, slot):
        return pltpu.make_async_copy(state_ref.at[s], state.at[slot], state_sem.at[slot])

    tiny[0].wait()
    wave_columns(slot_ref, wave_own)
    for g in range(groups):
        for i in range(GROUP):
            x = wave_own[pl.ds(g * GROUP + i, devices, stride=slots), :]
            for c in range(2):
                wave_ref[pl.ds(g * tall + 2 * i + c, devices, stride=small), :] = x
    block_rows = 64

    def fill(r, carry):
        at = aligned(r * block_rows, block_rows)
        waves = wave_ref[at, :]
        imaginary = (lax.broadcasted_iota(jnp.int32, waves.shape, 0) & 1) == 1
        for i, (h, l) in enumerate(table_rows(waves, imaginary, longitudes)):
            high[at, i * LANES : (i + 1) * LANES] = h
            low[at, i * LANES : (i + 1) * LANES] = l
        return carry

    def greeted_copy(source, target, d, sem):
        return pltpu.make_async_remote_copy(
            src_ref=sending.at[source, :],
            dst_ref=arrived.at[target, :],
            send_sem=send_sem,
            recv_sem=recv_sem.at[sem],
            device_id=mesh_id(d),
            device_id_type=pl.DeviceIdType.MESH,
        )

    def partner(i):
        return jnp.bitwise_xor(me, devices - 1 - i)

    def send_pair(q):
        to = aligned((me * pairs + q) * message, message)

        def body(i, carry):
            d = partner(i)
            greeted_copy(aligned((q * devices + d) * message, message), to, d, 0).start()
            return carry

        lax.fori_loop(0, devices - 1, body, 0)
        pltpu.make_async_copy(
            sending.at[aligned((q * devices + me) * message, message), :],
            arrived.at[to, :],
            recv_sem.at[0],
        ).start()

    def send_part(q, r, sem):
        def cut(first, h):
            return aligned(first * message + h * unit + r * small, small)

        def body(i, carry):
            d = partner(i)
            for h in range(PAIR):
                greeted_copy(
                    cut(q * devices + d, h), cut(me * pairs + q, h), d, sem
                ).start()
            return carry

        lax.fori_loop(0, devices - 1, body, 0)
        for h in range(PAIR):
            pltpu.make_async_copy(
                sending.at[cut(q * devices + me, h), :],
                arrived.at[cut(me * pairs + q, h), :],
                recv_sem.at[sem],
            ).start()

    def extract(q):
        first = q * PAIR
        block, local = first // SUB, lax.rem(first, SUB)
        for h in range(PAIR):
            for i in range(wide):
                x = forced[i, pl.ds(block * lats * SUB + local + h, lats, stride=SUB), :]
                rh, rl = halves_of(x)
                rows_h[h * lats : (h + 1) * lats, i * LANES : (i + 1) * LANES] = rh
                rows_l[h * lats : (h + 1) * lats, i * LANES : (i + 1) * LANES] = rl

    def transform(q, r):
        at = aligned(r * tall, tall)
        got = dot3((high[at, :], low[at, :]), (rows_h[...], rows_l[...]), NT)
        for d in range(devices):
            for h in range(PAIR):
                to = (q * devices + d) * message + h * unit + r * small
                sending[aligned(to, small), :] = got[
                    d * small : (d + 1) * small, h * lats : (h + 1) * lats
                ]

    per = SUB // PAIR
    blocks = levels // SUB

    def finish(i, c):
        finish_piece(i)
        return c

    fills = devices * unit // block_rows // PIECES // 2

    def begin(i, c):
        lax.fori_loop(i * fills, (i + 1) * fills, fill, 0)
        return finish(i, c)

    lax.fori_loop(0, PIECES, begin, 0)
    extract(jnp.int32(0))

    def opening(r, carry):
        @pl.when(r >= groups // 2)
        def _():
            lax.fori_loop(r * (tall // block_rows), (r + 1) * (tall // block_rows), fill, 0)

        transform(0, r)

        @pl.when(r == 0)
        def _():
            pl.semaphore_wait(barrier, devices - 1)

        send_part(0, r, 0)
        return carry

    lax.fori_loop(0, groups, opening, 0)

    def middle(q, carry):
        @pl.when(lax.rem(q, per) == 0)
        def _():
            lax.fori_loop(q // per * PIECES, (q // per + 1) * PIECES, finish, 0)

        extract(q)

        def each_group(r, c):
            transform(q, r)
            return c

        lax.fori_loop(0, groups, each_group, 0)
        send_pair(q)
        return carry

    lax.fori_loop(1, pairs - 1, middle, 0)
    extract(jnp.int32(pairs - 1))

    def closing(r, carry):
        transform(pairs - 1, r)
        send_part(pairs - 1, r, r + 1)
        return carry

    lax.fori_loop(0, groups, closing, 0)
    for copy in tiny[1:]:
        copy.wait()
    rate = jnp.concatenate([rate_ref[...], rate_ref[...]], axis=1)
    rate_col[...] = jnp.broadcast_to(rate, (2 * every, 2 * every)).T
    for m in (into, outof, back):
        m[...] = jnp.zeros_like(m)
    for c in range(2):
        cut = slice(c * every, (c + 1) * every)
        into[cut, cut] = to_ref[...]
        outof[cut, cut] = from_ref[...]
        for p in range(parts):
            at = (2 * p + c) * levels
            back[at : at + levels, cut] = from_ref[p * levels : (p + 1) * levels, :]

    leg_copy(0, 0).start()
    state_copy(0, 0).start()
    before = arrived.at[pl.ds(0, (pairs - 1) * devices * message), :]
    pltpu.make_async_copy(before, before, recv_sem.at[0]).wait()
    last_part = arrived.at[pl.ds(0, devices * PAIR * small), :]

    lane = lax.broadcasted_iota(jnp.int32, (2 * every, depth), 1)
    even = lax.rem(lane, 2) == 0
    folds = bands // 2
    each = 2 * levels
    quarter = devices // 4
    order = senders(me // quarter)

    def column(b, s):
        return jnp.concatenate(
            [
                arrived[pl.ds(b * every * unit + 2 * s + c, every, stride=unit), :]
                for c in range(2)
            ],
            axis=0,
        )

    def send2_copy(s, d, sem):
        return pltpu.make_async_remote_copy(
            src_ref=synth.at[aligned((s * devices + d) * each, each), :],
            dst_ref=returned.at[me, aligned(s * each, each), :],
            send_sem=send2_sem,
            recv_sem=recv2_sem.at[sem],
            device_id=mesh_id(d),
            device_id_type=pl.DeviceIdType.MESH,
        )

    def one_slot(s, carry):
        slot = lax.rem(s, 2)
        sem = me // quarter * groups + s // GROUP

        @pl.when(lax.rem(s, GROUP) == 0)
        def _():
            pltpu.make_async_copy(last_part, last_part, recv_sem.at[s // GROUP + 1]).wait()

        @pl.when(s + 1 < slots)
        def _():
            leg_copy(s + 1, 1 - slot).start()
            state_copy(s + 1, 1 - slot).start()

        leg_copy(s, slot).wait()
        state_copy(s, slot).wait()
        functions = halves_of(leg[slot])
        evens, odds = [], []
        for b in range(folds):
            n, o = column(b, s), column(bands - 1 - b, s)
            evens.append(n + o)
            odds.append(n - o)
        folded = jnp.concatenate(
            [jnp.concatenate(evens, axis=1), jnp.concatenate(odds, axis=1)], axis=0
        )
        both = dot3(halves_of(folded), functions, NT)
        analysed = jnp.where(even, both[: 2 * every], both[2 * every :])
        wave = wave_ref[
            pl.ds((s // GROUP * devices + me) * small + lax.rem(s, GROUP) * 2, 1), :
        ]
        wave = jnp.concatenate([wave] * (depth // LANES), axis=1)
        order = lax.broadcasted_iota(jnp.int32, (1, depth), 1)
        degree = (wave + order).astype(jnp.float32)
        helm = degree * (degree + 1.0) / (depth * (depth - 1.0))
        total = jnp.where(order < depth - wave, analysed + state[slot], 0.0)
        modes = dot3(halves_of(into[...]), halves_of(total), NN)
        scaled = halves_of(modes / (1.0 + helm * rate_col[:, 0:1]))

        @pl.when(s >= 2)
        def _():
            pltpu.make_async_copy(spec.at[slot], spec_out.at[s - 2], spec_sem.at[slot]).wait()

        spec[slot] = dot3(halves_of(outof[...]), scaled, NN)
        pltpu.make_async_copy(spec.at[slot], spec_out.at[s], spec_sem.at[slot]).start()
        coeffs = dot3(halves_of(back[...]), scaled, NN)
        split = jnp.concatenate(
            [jnp.where(even, coeffs, 0.0), jnp.where(even, 0.0, coeffs)], axis=0
        )
        both = dot3(halves_of(split), functions, NN)
        first, second = both[: 2 * every], both[2 * every :]
        north, other = first + second, first - second
        base = s * devices * each
        for b in range(folds):
            cut = slice(b * LANES, (b + 1) * LANES)
            synth[aligned(base + b * 2 * every, 2 * every), :] = north[:, cut]
            synth[aligned(base + (bands - 1 - b) * 2 * every, 2 * every), :] = other[:, cut]

        def body(i, c):
            send2_copy(s, partner(i), sem).start()
            return c

        lax.fori_loop(0, devices - 1, body, 0)
        pltpu.make_async_copy(
            synth.at[aligned((s * devices + me) * each, each), :],
            returned.at[me, aligned(s * each, each), :],
            recv2_sem.at[sem],
        ).start()
        return carry

    lax.fori_loop(0, slots, one_slot, 0)

    rows = GROUP * each
    staged = devices * rows
    pulled = arrived.reshape(levels * count_rows // rows, rows, lats)
    block = 1024
    piece = quarter * small

    def landed(c, g):
        return returned.at[aligned(order[c] * quarter, quarter), g * rows : (g + 1) * rows, :]

    for number, units in enumerate(ARRIVALS):
        copies = []
        for u, (c, g) in enumerate(units):
            here = landed(c, g)
            pltpu.make_async_copy(here, here, recv2_sem.at[order[c] * groups + g]).wait()
            copy = pltpu.make_async_copy(
                here, pulled.at[u * quarter : (u + 1) * quarter], pull_sem.at[u]
            )
            copy.start()
            copies.append(copy)
        for copy in copies:
            copy.wait()
        filled = len(units) * piece

        def pull(l, carry):
            x = arrived[pl.ds(l, tall, stride=levels), :]
            if filled < tall:
                x = jnp.where(lax.broadcasted_iota(jnp.int32, x.shape, 0) < filled, x, 0.0)
            x = x.T
            for j in range(tall // LANES):
                arrived[pl.ds(staged + j * lats * levels + l, lats, stride=levels), :] = x[
                    :, j * LANES : (j + 1) * LANES
                ]
            return carry

        lax.fori_loop(0, levels, pull, 0)

        def split(r, carry):
            lat = jnp.where(south, lats - 1 - r, r)
            to = aligned(r * levels, levels)
            for j in range(tall // LANES):
                x = arrived[aligned(staged + (j * lats + lat) * levels, levels), :]
                h, l = halves_of(x)
                flat_h[to, j * LANES : (j + 1) * LANES] = h
                flat_l[to, j * LANES : (j + 1) * LANES] = l
            return carry

        lax.fori_loop(0, lats, split, 0)
        chosen = (units + units[:1])[: tall // piece]

        def multiply(m, carry):
            at = aligned(m * block, block)

            def inner(w, carry2):
                cut = aligned(w * 2 * LANES, 2 * LANES)
                table = [
                    jnp.concatenate(
                        [part[aligned(g * tall + order[c] * piece, piece), cut] for c, g in chosen],
                        axis=0,
                    )
                    for part in (high, low)
                ]
                got = dot3((flat_h[at, :], flat_l[at, :]), table, NN)
                for j in range(2):
                    x = got[:, j * LANES : (j + 1) * LANES]
                    if number > 0:
                        x = x + forced[2 * w + j, at, :]
                    forced[2 * w + j, at, :] = x
                return carry2

            lax.fori_loop(0, wide // 2, inner, 0)
            return carry

        lax.fori_loop(0, lats * levels // block, multiply, 0)

    for s in range(max(slots - 2, 0), slots):
        pltpu.make_async_copy(spec.at[s % 2], spec_out.at[s], spec_sem.at[s % 2]).wait()
    sent = pl.ds(0, pairs * (devices - 1) * message)
    pltpu.make_async_copy(sending.at[sent, :], sending.at[sent, :], send_sem).wait()
    sent = pl.ds(0, slots * (devices - 1) * each)
    pltpu.make_async_copy(synth.at[sent, :], synth.at[sent, :], send2_sem).wait()
    final = landed(3, groups - 1)
    pltpu.make_async_copy(final, final, recv2_sem.at[order[3] * groups + groups - 1]).wait()


def finish_kernel(
    dims, returned, partial, spectral, slot_ref, grid_out, spec_out,
    pulled, turned, stacked, table, result, spec, wave_own, waves,
    pull_sem, out_sem, spec_in, spec_done,
):
    bands, parts, lats, levels, longitudes, slots, depth, half = dims
    devices = bands * parts
    each = 2 * levels
    wide = longitudes // LANES
    south = lax.axis_index("band") >= bands // 2
    block = 1024
    span = block // levels

    def out_copy(w, slot):
        return pltpu.make_async_copy(
            result.at[slot],
            grid_out.at[:, :, aligned(w * 2 * LANES, 2 * LANES)],
            out_sem.at[slot],
        )

    quarter = devices // 4
    me = lax.axis_index("band") * parts + lax.axis_index("lev")
    first = senders(me // quarter)[3] * quarter
    rows = GROUP * each
    pull = pltpu.make_async_copy(
        returned.at[aligned(first, quarter), slots * each - rows : slots * each, :], pulled, pull_sem
    )
    pull.start()
    spec_copy = pltpu.make_async_copy(spectral, spec, spec_in)
    spec_copy.start()

    wave_columns(slot_ref, wave_own)
    for i in range(GROUP):
        x = wave_own[pl.ds(first * slots + slots - GROUP + i, quarter, stride=slots), :]
        for c in range(2):
            waves[pl.ds(2 * i + c, quarter, stride=2 * GROUP), :] = x
    imaginary = (lax.broadcasted_iota(jnp.int32, waves.shape, 0) & 1) == 1
    short = quarter * 2 * GROUP
    for i, (h, l) in enumerate(table_rows(waves[...], imaginary, longitudes)):
        cut = slice(i * LANES, (i + 1) * LANES)
        table[0:short, cut] = h
        table[short : 2 * short, cut] = l
        table[2 * short : 3 * short, cut] = h
        table[3 * short : 4 * short, cut] = jnp.zeros_like(h)
    spec_copy.wait()
    done = pltpu.make_async_copy(spec, spec_out, spec_done)
    done.start()
    pull.wait()
    flat = pulled.reshape(quarter * rows, lats)
    for l in range(levels):
        x = flat[pl.ds(l, LANES // 2, stride=levels), :]
        turned[pl.ds(l, lats, stride=levels), :] = jnp.concatenate([x, x], axis=0).T
    keep = lax.broadcasted_iota(jnp.int32, (levels, LANES), 1) < LANES // 2

    burst = 8

    def split(i, carry):
        for e in range(burst):
            r = i * burst + e
            lat = jnp.where(south, lats - 1 - r, r)
            h, l = halves_of(turned[aligned(lat * levels, levels), :])
            to = aligned(r * levels, levels)
            stacked[to, 0:LANES] = h
            stacked[to, LANES : 2 * LANES] = jnp.where(keep, l, jnp.zeros_like(l))
        return carry

    lax.fori_loop(0, lats // burst, split, 0)

    def outer(w, carry):
        slot = lax.rem(w, 2)

        @pl.when(w >= 2)
        def _():
            out_copy(w - 2, slot).wait()

        cut = aligned(w * 2 * LANES, 2 * LANES)
        for m in range(lats // span):
            at = slice(m * block, (m + 1) * block)
            got = dot1(stacked[at, :], table[:, cut], NN)
            for j in range(2):
                x = got[:, j * LANES : (j + 1) * LANES] + partial[2 * w + j, at, :]
                result[slot, m * span : (m + 1) * span, :, j * LANES : (j + 1) * LANES] = (
                    x.reshape(span, levels, LANES)
                )
        out_copy(w, slot).start()
        return carry

    turns = wide // 2
    lax.fori_loop(0, turns, outer, 0)
    for w in range(turns - 2, turns):
        out_copy(w, w % 2).wait()
    done.wait()


def shards(
    grid_adjoint, trajectory, legendre_north, slot_wavenumber, spectral_state,
    to_modes, from_modes, rates,
):
    lats, levels, longitudes = grid_adjoint.shape
    slots, depth, half = legendre_north.shape
    bands = lax.axis_size("band")
    parts = lax.axis_size("lev")
    devices = bands * parts
    every = parts * levels
    fits = (
        lats == LANES and levels == 2 * SUB and 4 * devices == LANES
        and longitudes % (2 * LANES) == 0 and longitudes & (longitudes - 1) == 0
        and bands % 2 == 0 and half == bands // 2 * lats and depth % LANES == 0
        and slots == 4 * GROUP and devices * slots % LANES == 0 and levels // PAIR >= 3 and 2 * every == LANES and to_modes.shape[0] == every
    )
    if not fits:
        return plain_shards(
            grid_adjoint, trajectory, legendre_north, slot_wavenumber, spectral_state,
            to_modes, from_modes, rates,
        )
    dims = (bands, parts, lats, levels, longitudes, slots, depth, half)
    count = devices * slots * 2
    hbm = pl.BlockSpec(memory_space=pl.ANY)
    vmem = pl.BlockSpec(memory_space=pltpu.VMEM)
    f32, bf16 = jnp.float32, jnp.bfloat16
    dma = pltpu.SemaphoreType.DMA
    wide = longitudes // LANES
    numbers = slot_wavenumber.reshape(-1, LANES)
    state = spectral_state.transpose(0, 2, 3, 1).reshape(slots, 2 * every, depth)
    square = pltpu.VMEM((2 * every, 2 * every), f32)
    spectral, returned, partial = pl.pallas_call(
        functools.partial(forward_kernel, dims),
        out_shape=(
            jax.ShapeDtypeStruct((slots, 2 * every, depth), f32),
            jax.ShapeDtypeStruct((devices, slots * 2 * levels, lats), f32),
            pltpu.VMEM((wide, lats * levels, LANES), f32),
        ),
        in_specs=[hbm] * 8,
        out_specs=(hbm, hbm, vmem),
        scratch_shapes=[
            pltpu.VMEM((count, longitudes), bf16),
            pltpu.VMEM((count, longitudes), bf16),
            pltpu.VMEM((2, lats // PIECES, SUB, longitudes), f32),
            pltpu.VMEM((2, lats // PIECES, SUB, longitudes), f32),
            pltpu.VMEM((PAIR * lats, longitudes), bf16),
            pltpu.VMEM((PAIR * lats, longitudes), bf16),
            pltpu.VMEM((levels * count, lats), f32),
            pltpu.VMEM((levels * count, lats), f32),
            pltpu.VMEM((count * levels, lats), f32),
            pltpu.VMEM((2, depth, half), f32),
            pltpu.VMEM((2, 2 * every, depth), f32),
            pltpu.VMEM((2, 2 * every, depth), f32),
            square, square, square,
            pltpu.VMEM((lats * levels, devices * 2 * GROUP), bf16),
            pltpu.VMEM((lats * levels, devices * 2 * GROUP), bf16),
            pltpu.VMEM((devices * slots, LANES), jnp.int32),
            pltpu.VMEM((count, LANES), jnp.int32),
            square,
            pltpu.VMEM(numbers.shape, jnp.int32),
            pltpu.VMEM((1, every), f32),
            pltpu.VMEM(to_modes.shape, f32),
            pltpu.VMEM(from_modes.shape, f32),
            dma((2,)), dma((2,)), dma, dma((slots // GROUP + 1,)), dma,
            dma((slots,)),
            dma((2,)), dma((2,)), dma((2,)), dma((4,)), dma((4,)),
        ],
        compiler_params=pltpu.CompilerParams(
            collective_id=0, has_side_effects=True, vmem_limit_bytes=GRANT
        ),
        name="spectral",
    )(
        grid_adjoint, trajectory, numbers, legendre_north, state, rates.reshape(1, every),
        to_modes, from_modes,
    )
    grid, spectral = pl.pallas_call(
        functools.partial(finish_kernel, dims),
        out_shape=(
            jax.ShapeDtypeStruct(grid_adjoint.shape, f32),
            jax.ShapeDtypeStruct(spectral.shape, f32),
        ),
        in_specs=[hbm, vmem, hbm, vmem],
        out_specs=(hbm, hbm),
        scratch_shapes=[
            pltpu.VMEM((devices // 4, GROUP * 2 * levels, lats), f32),
            pltpu.VMEM((lats * levels, LANES), f32),
            pltpu.VMEM((lats * levels, 2 * LANES), bf16),
            pltpu.VMEM((2 * LANES, longitudes), bf16),
            pltpu.VMEM((2, lats, levels, 2 * LANES), f32),
            pltpu.VMEM(spectral.shape, f32),
            pltpu.VMEM((devices * slots, LANES), jnp.int32),
            pltpu.VMEM((LANES // 2, LANES), jnp.int32),
            dma, dma((2,)), dma, dma,
        ],
        compiler_params=pltpu.CompilerParams(vmem_limit_bytes=LAST_GRANT),
        name="finish",
    )(returned, pltpu.with_memory_space_constraint(partial, pltpu.VMEM), spectral, numbers)
    return spectral.reshape(slots, 2, every, depth).transpose(0, 3, 1, 2), grid


def solution(mesh):
    return jax.shard_map(
        shards,
        mesh=mesh,
        in_specs=(
            P("band", "lev", None),
            P("band", "lev", None),
            P(("band", "lev"), None, None),
            P(),
            P(("band", "lev"), None, None, None),
            P(),
            P(),
            P(),
        ),
        out_specs=(P(("band", "lev"), None, None, None), P("band", "lev", None)),
        check_vma=False,
    )
```

```python
import functools
import math

import jax
import jax.numpy as jnp
from jax import lax
from jax.experimental import pallas as pl
from jax.experimental.pallas import tpu as pltpu
from jax.sharding import PartitionSpec as P

PRECISION = lax.Precision.HIGH


def angle_parts(steps, waves, longitudes):
    phase = waves[:, None] * steps[None, :] % longitudes
    angles = phase.astype(jnp.float32) * (2.0 * jnp.pi / longitudes)
    return jnp.cos(angles), jnp.sin(angles)


def wave_rows(longitudes, waves, devices):
    fine = min(128, longitudes)
    coarse = longitudes // fine
    scale = jnp.float32(longitudes) ** (-0.5)
    cos_a, sin_a = angle_parts(jnp.arange(coarse, dtype=jnp.int32) * fine, waves, longitudes)
    cos_b, sin_b = angle_parts(jnp.arange(fine, dtype=jnp.int32), waves, longitudes)
    cos_a, sin_a, cos_b, sin_b = lax.optimization_barrier(
        (cos_a * scale, sin_a * scale, cos_b, sin_b)
    )
    cos_at = [cos_a[:, i : i + 1] * cos_b - sin_a[:, i : i + 1] * sin_b for i in range(coarse)]
    sin_at = [-sin_a[:, i : i + 1] * cos_b - cos_a[:, i : i + 1] * sin_b for i in range(coarse)]
    cosine = jnp.concatenate(cos_at, axis=1).reshape(devices, -1, longitudes)
    negsine = jnp.concatenate(sin_at, axis=1).reshape(devices, -1, longitudes)
    return jnp.stack([cosine, negsine], axis=1).reshape(-1, longitudes)


def exchange(data):
    return lax.all_to_all(data, ("band", "lev"), split_axis=0, concat_axis=0, tiled=True)


def plain_shards(
    grid_adjoint,
    trajectory,
    legendre_north,
    slot_wavenumber,
    spectral_state,
    to_modes,
    from_modes,
    rates,
):
    lats, levels, longitudes = grid_adjoint.shape
    slots, depth, half = legendre_north.shape
    bands = lax.axis_size("band")
    parts = lax.axis_size("lev")
    devices = bands * parts
    every = parts * levels
    me = lax.axis_index("band") * parts + lax.axis_index("lev")
    own_waves = lax.dynamic_slice_in_dim(slot_wavenumber, me * slots, slots)
    table = wave_rows(longitudes, slot_wavenumber, devices)
    even_k = jnp.arange(depth, dtype=jnp.int32) % 2 == 0

    forced = grid_adjoint * (1.0 + trajectory)
    rows = jnp.swapaxes(forced, 0, 1).reshape(levels * lats, longitudes)
    fourier = lax.dot_general(
        table, rows, (((1,), (1,)), ((), ())), precision=PRECISION, preferred_element_type=jnp.float32
    )
    arrived = exchange(fourier.reshape(devices, 2 * slots, levels * lats))
    arrived = arrived.reshape(bands, parts, 2, slots, levels, lats)
    arrived = arrived.transpose(3, 2, 1, 4, 0, 5).reshape(slots, 2 * every, bands * lats)
    north = arrived[:, :, :half]
    south = arrived[:, :, half:][:, :, ::-1]
    folded = jnp.concatenate([north + south, north - south], axis=1)
    both = lax.dot_general(
        folded, legendre_north, (((2,), (2,)), ((0,), (0,))), precision=PRECISION,
        preferred_element_type=jnp.float32,
    )
    analysed = jnp.where(even_k, both[:, : 2 * every], both[:, 2 * every :])
    analysed = analysed.reshape(slots, 2, every, depth)

    state = spectral_state.transpose(0, 2, 3, 1)
    depth_index = jnp.arange(depth, dtype=jnp.int32)
    valid = (depth_index[None, :] < depth - own_waves[:, None]).astype(jnp.float32)
    total = (analysed + state) * valid[:, None, None, :]
    degree = (own_waves[:, None] + depth_index[None, :]).astype(jnp.float32)
    helm = degree * (degree + 1.0) / (depth * (depth - 1.0))
    modes = jnp.einsum("sclk,pl->scpk", total, to_modes, precision=PRECISION)
    scaled = modes / (1.0 + helm[:, None, None, :] * rates[None, None, :, None])
    spectral = jnp.einsum("scpk,lp->sclk", scaled, from_modes, precision=PRECISION)

    coeffs = spectral.reshape(slots, 2 * every, depth)
    split = jnp.concatenate(
        [jnp.where(even_k, coeffs, 0.0), jnp.where(even_k, 0.0, coeffs)], axis=1
    )
    halves = lax.dot_general(
        split, legendre_north, (((2,), (1,)), ((0,), (0,))), precision=PRECISION,
        preferred_element_type=jnp.float32,
    )
    first = halves[:, : 2 * every]
    second = halves[:, 2 * every :]
    whole = jnp.concatenate([first + second, (first - second)[:, :, ::-1]], axis=2)
    whole = whole.reshape(slots, 2, parts, levels, bands, lats).transpose(4, 2, 1, 0, 3, 5)
    returned = exchange(whole.reshape(devices, 2 * slots, levels * lats))
    grid = lax.dot_general(
        returned.reshape(devices * 2 * slots, levels, lats),
        table,
        (((0,), (0,)), ((), ())),
        precision=PRECISION,
        preferred_element_type=jnp.float32,
    )
    return spectral.transpose(0, 3, 1, 2), jnp.swapaxes(grid, 0, 1)


LANES = 128
SUB = 8
PAIR = 2
PIECES = 8
GROUP = 4
GRANT = 47_000_000
LAST_GRANT = 43_000_000
NN = (((1,), (0,)), ((), ()))
NT = (((1,), (1,)), ((), ()))


def halves_of(x):
    high = x.astype(jnp.bfloat16)
    low = (x - high.astype(jnp.float32)).astype(jnp.bfloat16)
    return high, low


def dot1(x, y, dims):
    return lax.dot_general(x, y, dims, preferred_element_type=jnp.float32)


def dot3(a, b, dims):
    return dot1(a[0], b[0], dims) + (dot1(a[0], b[1], dims) + dot1(a[1], b[0], dims))


def aligned(start, size):
    return pl.ds(pl.multiple_of(start, size & -size), size)


def circle(phase, longitudes):
    quarter = longitudes // 4
    quadrant = phase >> (quarter.bit_length() - 1)
    rest = phase & (quarter - 1)
    flip = rest > quarter // 2
    angle = jnp.where(flip, quarter - rest, rest).astype(jnp.float32) * (
        2.0 * math.pi / longitudes
    )
    z = angle * angle
    sine = angle * (
        1.0 + z * (-1 / 6 + z * (1 / 120 + z * (-1 / 5040 + z * (1 / 362880))))
    )
    cosine = 1.0 + z * (
        -0.5 + z * (1 / 24 + z * (-1 / 720 + z * (1 / 40320 + z * (-1 / 3628800))))
    )
    c, s = jnp.where(flip, sine, cosine), jnp.where(flip, cosine, sine)
    odd = (quadrant & 1) == 1
    c, s = jnp.where(odd, s, c), jnp.where(odd, c, s)
    c = jnp.where((quadrant == 1) | (quadrant == 2), -c, c)
    return c, jnp.where(quadrant >= 2, -s, s)


def table_rows(waves, imaginary, longitudes):
    column = lax.broadcasted_iota(jnp.int32, waves.shape, 1)
    ca, sa = circle((waves * (column * LANES)) & (longitudes - 1), longitudes)
    cb, sb = circle((waves * column) & (longitudes - 1), longitudes)
    scale = float(longitudes) ** -0.5
    ca, sa = ca * scale, sa * scale
    p = jnp.where(imaginary, -sa, ca)
    q = jnp.where(imaginary, -ca, -sa)
    return [
        halves_of(p[:, i : i + 1] * cb + q[:, i : i + 1] * sb)
        for i in range(longitudes // LANES)
    ]


def wave_columns(slot_ref, own):
    for i in range(slot_ref.shape[0]):
        row = jnp.broadcast_to(slot_ref[i : i + 1, :].astype(jnp.float32), (LANES, LANES))
        own[i * LANES : (i + 1) * LANES, :] = row.T.astype(jnp.int32)


def senders(quarter):
    return (
        quarter,
        jnp.bitwise_xor(quarter, 1),
        jnp.where(quarter < 2, 3, 0),
        jnp.where(quarter < 2, 2, 1),
    )


ARRIVALS = (
    ((1, 0), (1, 1), (2, 0), (3, 0)),
    ((0, 0), (0, 1), (0, 2), (2, 1)),
    ((1, 2), (1, 3), (2, 2), (2, 3)),
    ((0, 3), (3, 1), (3, 2)),
)


def forward_kernel(
    dims,
    grid_ref, traj_ref, slot_in, leg_ref, state_ref, rate_in, to_in, from_in,
    spec_out, returned, forced,
    high, low, stage, traj, rows_h, rows_l, outbox, arrived, leg, state, spec,
    into, outof, back, flat_h, flat_l, wave_own, wave_ref, rate_col,
    slot_ref, rate_ref, to_ref, from_ref,
    grid_sem, traj_sem, send_sem, recv_sem, send2_sem, recv2_sem, leg_sem, state_sem, spec_sem,
    pull_sem, tiny_sem,
):
    bands, parts, lats, levels, longitudes, slots, depth, half = dims
    devices = bands * parts
    every = parts * levels
    pairs = levels // PAIR
    unit = 2 * slots
    message = PAIR * unit
    small = 2 * GROUP
    tall = devices * small
    ahead = slots // 2 * devices * 2 * levels
    groups = slots // GROUP
    count_rows = devices * unit
    wide = longitudes // LANES
    band, lev = lax.axis_index("band"), lax.axis_index("lev")
    me = band * parts + lev
    south = band >= bands // 2

    def mesh_id(d):
        return (d // parts, lax.rem(d, parts))

    tiny = [
        pltpu.make_async_copy(source, target, tiny_sem.at[i])
        for i, (source, target) in enumerate(
            ((slot_in, slot_ref), (rate_in, rate_ref), (to_in, to_ref), (from_in, from_ref))
        )
    ]
    for copy in tiny:
        copy.start()
    barrier = pltpu.get_barrier_semaphore()

    def greet(i, carry):
        pl.semaphore_signal(
            barrier, inc=1, device_id=mesh_id(jnp.bitwise_xor(me, i)),
            device_id_type=pl.DeviceIdType.MESH,
        )
        return carry


    span = lats // PIECES
    count = (levels // SUB) * PIECES

    def load_copies(piece):
        block, part = piece // PIECES, lax.rem(piece, PIECES)
        lat = aligned(part * span, span)
        cut = aligned(block * SUB, SUB)
        slot = lax.rem(piece, 2)
        return (
            pltpu.make_async_copy(grid_ref.at[lat, cut, :], stage.at[slot], grid_sem.at[slot]),
            pltpu.make_async_copy(traj_ref.at[lat, cut, :], traj.at[slot], traj_sem.at[slot]),
        )

    def load_piece(piece):
        for copy in load_copies(piece):
            copy.start()

    def finish_piece(piece):
        block, part = piece // PIECES, lax.rem(piece, PIECES)
        slot = lax.rem(piece, 2)
        for copy in load_copies(piece):
            copy.wait()

        def body(i, carry):
            at = part * span + i
            lat = jnp.where(south, lats - 1 - at, at)
            to = aligned((block * lats + lat) * SUB, SUB)
            x = stage[slot, i] * (1.0 + traj[slot, i])
            for j in range(wide):
                forced[j, to, :] = x[:, j * LANES : (j + 1) * LANES]
            return carry

        lax.fori_loop(0, span, body, 0)

        @pl.when(piece + 2 < count)
        def _():
            load_piece(piece + 2)

    load_piece(jnp.int32(0))
    load_piece(jnp.int32(1))
    lax.fori_loop(1, devices, greet, 0)

    def leg_copy(s, slot):
        return pltpu.make_async_copy(leg_ref.at[s], leg.at[slot], leg_sem.at[slot])

    def state_copy(s, slot):
        return pltpu.make_async_copy(state_ref.at[s], state.at[slot], state_sem.at[slot])

    tiny[0].wait()
    wave_columns(slot_ref, wave_own)
    for g in range(groups):
        for i in range(GROUP):
            x = wave_own[pl.ds(g * GROUP + i, devices, stride=slots), :]
            for c in range(2):
                wave_ref[pl.ds(g * tall + 2 * i + c, devices, stride=small), :] = x
    block_rows = 64

    def fill(r, carry):
        at = aligned(r * block_rows, block_rows)
        waves = wave_ref[at, :]
        imaginary = (lax.broadcasted_iota(jnp.int32, waves.shape, 0) & 1) == 1
        for i, (h, l) in enumerate(table_rows(waves, imaginary, longitudes)):
            high[at, i * LANES : (i + 1) * LANES] = h
            low[at, i * LANES : (i + 1) * LANES] = l
        return carry

    def greeted_copy(source, target, d, sem):
        return pltpu.make_async_remote_copy(
            src_ref=outbox.at[source, :],
            dst_ref=arrived.at[target, :],
            send_sem=send_sem,
            recv_sem=recv_sem.at[sem],
            device_id=mesh_id(d),
            device_id_type=pl.DeviceIdType.MESH,
        )

    def partner(i):
        return jnp.bitwise_xor(me, devices - 1 - i)

    def send_pair(q):
        to = aligned((me * pairs + q) * message, message)

        def body(i, carry):
            d = partner(i)
            source = aligned(ahead + (q * devices + d) * message, message)
            greeted_copy(source, to, d, 0).start()
            return carry

        lax.fori_loop(0, devices - 1, body, 0)
        pltpu.make_async_copy(
            outbox.at[aligned(ahead + (q * devices + me) * message, message), :],
            arrived.at[to, :],
            recv_sem.at[0],
        ).start()

    def send_part(q, r, sem):
        def cut(first, h, shift=0):
            return aligned(shift + first * message + h * unit + r * small, small)

        def body(i, carry):
            d = partner(i)
            for h in range(PAIR):
                greeted_copy(
                    cut(q * devices + d, h, ahead), cut(me * pairs + q, h), d, sem
                ).start()
            return carry

        lax.fori_loop(0, devices - 1, body, 0)
        for h in range(PAIR):
            pltpu.make_async_copy(
                outbox.at[cut(q * devices + me, h, ahead), :],
                arrived.at[cut(me * pairs + q, h), :],
                recv_sem.at[sem],
            ).start()

    def extract(q):
        first = q * PAIR
        block, local = first // SUB, lax.rem(first, SUB)
        for h in range(PAIR):
            for i in range(wide):
                x = forced[i, pl.ds(block * lats * SUB + local + h, lats, stride=SUB), :]
                rh, rl = halves_of(x)
                rows_h[h * lats : (h + 1) * lats, i * LANES : (i + 1) * LANES] = rh
                rows_l[h * lats : (h + 1) * lats, i * LANES : (i + 1) * LANES] = rl

    def transform(q, r):
        at = aligned(r * tall, tall)
        got = dot3((high[at, :], low[at, :]), (rows_h[...], rows_l[...]), NT)
        for d in range(devices):
            for h in range(PAIR):
                to = ahead + (q * devices + d) * message + h * unit + r * small
                outbox[aligned(to, small), :] = got[
                    d * small : (d + 1) * small, h * lats : (h + 1) * lats
                ]

    per = SUB // PAIR
    blocks = levels // SUB

    def finish(i, c):
        finish_piece(i)
        return c

    fills = devices * unit // block_rows // PIECES // 2

    def begin(i, c):
        lax.fori_loop(i * fills, (i + 1) * fills, fill, 0)
        return finish(i, c)

    lax.fori_loop(0, PIECES, begin, 0)
    extract(jnp.int32(0))

    def opening(r, carry):
        @pl.when(r >= groups // 2)
        def _():
            lax.fori_loop(r * (tall // block_rows), (r + 1) * (tall // block_rows), fill, 0)

        transform(0, r)

        @pl.when(r == 0)
        def _():
            pl.semaphore_wait(barrier, devices - 1)

        send_part(0, r, 0)
        return carry

    lax.fori_loop(0, groups, opening, 0)

    def middle(q, carry):
        @pl.when(lax.rem(q, per) == 0)
        def _():
            lax.fori_loop(q // per * PIECES, (q // per + 1) * PIECES, finish, 0)

        extract(q)

        def each_group(r, c):
            transform(q, r)
            return c

        lax.fori_loop(0, groups, each_group, 0)
        send_pair(q)
        return carry

    lax.fori_loop(1, pairs - 1, middle, 0)
    extract(jnp.int32(pairs - 1))

    def closing(r, carry):
        transform(pairs - 1, r)
        send_part(pairs - 1, r, r + 1)
        return carry

    lax.fori_loop(0, groups, closing, 0)
    for copy in tiny[1:]:
        copy.wait()
    rate = jnp.concatenate([rate_ref[...], rate_ref[...]], axis=1)
    rate_col[...] = jnp.broadcast_to(rate, (2 * every, 2 * every)).T
    for m in (into, outof, back):
        m[...] = jnp.zeros_like(m)
    for c in range(2):
        cut = slice(c * every, (c + 1) * every)
        into[cut, cut] = to_ref[...]
        outof[cut, cut] = from_ref[...]
        for p in range(parts):
            at = (2 * p + c) * levels
            back[at : at + levels, cut] = from_ref[p * levels : (p + 1) * levels, :]

    leg_copy(0, 0).start()
    state_copy(0, 0).start()
    before = arrived.at[pl.ds(0, (pairs - 1) * devices * message), :]
    pltpu.make_async_copy(before, before, recv_sem.at[0]).wait()
    last_part = arrived.at[pl.ds(0, devices * PAIR * small), :]

    lane = lax.broadcasted_iota(jnp.int32, (2 * every, depth), 1)
    even = lax.rem(lane, 2) == 0
    folds = bands // 2
    each = 2 * levels
    quarter = devices // 4
    order = senders(me // quarter)

    def column(b, s):
        return jnp.concatenate(
            [
                arrived[pl.ds(b * every * unit + 2 * s + c, every, stride=unit), :]
                for c in range(2)
            ],
            axis=0,
        )

    def send2_copy(s, d, sem):
        return pltpu.make_async_remote_copy(
            src_ref=outbox.at[aligned((s * devices + d) * each, each), :],
            dst_ref=returned.at[me, aligned(s * each, each), :],
            send_sem=send2_sem,
            recv_sem=recv2_sem.at[sem],
            device_id=mesh_id(d),
            device_id_type=pl.DeviceIdType.MESH,
        )

    def send2_tail(s, d, sem):
        return pltpu.make_async_remote_copy(
            src_ref=outbox.at[aligned((s * devices + d) * each, each), :],
            dst_ref=forced.at[wide, aligned(lax.rem(me, quarter) * GROUP * each + (s - (slots - GROUP)) * each, each), :],
            send_sem=send2_sem,
            recv_sem=recv2_sem.at[sem],
            device_id=mesh_id(d),
            device_id_type=pl.DeviceIdType.MESH,
        )

    def one_slot(s, carry):
        slot = lax.rem(s, 2)
        sem = me // quarter * groups + s // GROUP

        @pl.when(lax.rem(s, GROUP) == 0)
        def _():
            pltpu.make_async_copy(last_part, last_part, recv_sem.at[s // GROUP + 1]).wait()

        @pl.when(s + 1 < slots)
        def _():
            leg_copy(s + 1, 1 - slot).start()
            state_copy(s + 1, 1 - slot).start()

        leg_copy(s, slot).wait()
        state_copy(s, slot).wait()
        functions = halves_of(leg[slot])
        evens, odds = [], []
        for b in range(folds):
            n, o = column(b, s), column(bands - 1 - b, s)
            evens.append(n + o)
            odds.append(n - o)
        folded = jnp.concatenate(
            [jnp.concatenate(evens, axis=1), jnp.concatenate(odds, axis=1)], axis=0
        )
        both = dot3(halves_of(folded), functions, NT)
        analysed = jnp.where(even, both[: 2 * every], both[2 * every :])
        wave = wave_ref[
            pl.ds((s // GROUP * devices + me) * small + lax.rem(s, GROUP) * 2, 1), :
        ]
        wave = jnp.concatenate([wave] * (depth // LANES), axis=1)
        order = lax.broadcasted_iota(jnp.int32, (1, depth), 1)
        degree = (wave + order).astype(jnp.float32)
        helm = degree * (degree + 1.0) / (depth * (depth - 1.0))
        total = jnp.where(order < depth - wave, analysed + state[slot], 0.0)
        modes = dot3(halves_of(into[...]), halves_of(total), NN)
        scaled = halves_of(modes / (1.0 + helm * rate_col[:, 0:1]))

        @pl.when(s >= 2)
        def _():
            pltpu.make_async_copy(spec.at[slot], spec_out.at[s - 2], spec_sem.at[slot]).wait()

        spec[slot] = dot3(halves_of(outof[...]), scaled, NN)
        pltpu.make_async_copy(spec.at[slot], spec_out.at[s], spec_sem.at[slot]).start()
        coeffs = dot3(halves_of(back[...]), scaled, NN)
        split = jnp.concatenate(
            [jnp.where(even, coeffs, 0.0), jnp.where(even, 0.0, coeffs)], axis=0
        )
        both = dot3(halves_of(split), functions, NN)
        first, second = both[: 2 * every], both[2 * every :]
        north, other = first + second, first - second
        base = s * devices * each

        @pl.when(s == slots // 2)
        def _():
            sent = outbox.at[pl.ds(ahead, pairs * (devices - 1) * message), :]
            pltpu.make_async_copy(sent, sent, send_sem).wait()

        for b in range(folds):
            cut = slice(b * LANES, (b + 1) * LANES)
            outbox[aligned(base + b * 2 * every, 2 * every), :] = north[:, cut]
            outbox[aligned(base + (bands - 1 - b) * 2 * every, 2 * every), :] = other[:, cut]

        def body(i, c):
            d = partner(i)
            near = senders(d // quarter)[3] == me // quarter
            ends = jnp.logical_and(s >= slots - GROUP, near)

            @pl.when(ends)
            def _():
                send2_tail(s, d, sem).start()

            @pl.when(jnp.logical_not(ends))
            def _():
                send2_copy(s, d, sem).start()

            return c

        lax.fori_loop(0, devices - 1, body, 0)
        pltpu.make_async_copy(
            outbox.at[aligned((s * devices + me) * each, each), :],
            returned.at[me, aligned(s * each, each), :],
            recv2_sem.at[sem],
        ).start()
        return carry

    lax.fori_loop(0, slots, one_slot, 0)

    rows = GROUP * each
    staged = devices * rows
    pulled = arrived.reshape(levels * count_rows // rows, rows, lats)
    block = 1024
    piece = quarter * small

    def landed(c, g):
        return returned.at[aligned(order[c] * quarter, quarter), g * rows : (g + 1) * rows, :]

    at = aligned((groups - 1) * tall + order[3] * piece, piece)
    for e, part in enumerate((high, low)):
        for i in range(wide):
            to = slice((e * wide + i) * piece, (e * wide + i + 1) * piece)
            forced[wide + 1, to, :] = part[at, i * LANES : (i + 1) * LANES].astype(jnp.float32)

    for number, units in enumerate(ARRIVALS):
        copies = []
        for u, (c, g) in enumerate(units):
            here = landed(c, g)
            pltpu.make_async_copy(here, here, recv2_sem.at[order[c] * groups + g]).wait()
            copy = pltpu.make_async_copy(
                here, pulled.at[u * quarter : (u + 1) * quarter], pull_sem.at[u]
            )
            copy.start()
            copies.append(copy)
        for copy in copies:
            copy.wait()
        filled = len(units) * piece

        def pull(l, carry):
            x = arrived[pl.ds(l, tall, stride=levels), :]
            if filled < tall:
                x = jnp.where(lax.broadcasted_iota(jnp.int32, x.shape, 0) < filled, x, 0.0)
            x = x.T
            for j in range(tall // LANES):
                arrived[pl.ds(staged + j * lats * levels + l, lats, stride=levels), :] = x[
                    :, j * LANES : (j + 1) * LANES
                ]
            return carry

        lax.fori_loop(0, levels, pull, 0)

        def split(r, carry):
            lat = jnp.where(south, lats - 1 - r, r)
            to = aligned(r * levels, levels)
            for j in range(tall // LANES):
                x = arrived[aligned(staged + (j * lats + lat) * levels, levels), :]
                h, l = halves_of(x)
                flat_h[to, j * LANES : (j + 1) * LANES] = h
                flat_l[to, j * LANES : (j + 1) * LANES] = l
            return carry

        lax.fori_loop(0, lats, split, 0)
        chosen = (units + units[:1])[: tall // piece]

        def multiply(m, carry):
            at = aligned(m * block, block)

            def inner(w, carry2):
                cut = aligned(w * 2 * LANES, 2 * LANES)
                table = [
                    jnp.concatenate(
                        [part[aligned(g * tall + order[c] * piece, piece), cut] for c, g in chosen],
                        axis=0,
                    )
                    for part in (high, low)
                ]
                got = dot3((flat_h[at, :], flat_l[at, :]), table, NN)
                for j in range(2):
                    x = got[:, j * LANES : (j + 1) * LANES]
                    if number > 0:
                        x = x + forced[2 * w + j, at, :]
                    forced[2 * w + j, at, :] = x
                return carry2

            lax.fori_loop(0, wide // 2, inner, 0)
            return carry

        lax.fori_loop(0, lats * levels // block, multiply, 0)

    for s in range(max(slots - 2, 0), slots):
        pltpu.make_async_copy(spec.at[s % 2], spec_out.at[s], spec_sem.at[s % 2]).wait()
    sent = outbox.at[pl.ds(0, slots * (devices - 1) * each), :]
    pltpu.make_async_copy(sent, sent, send2_sem).wait()
    tail = forced.at[wide, pl.ds(0, quarter * rows), :]
    pltpu.make_async_copy(tail, tail, recv2_sem.at[order[3] * groups + groups - 1]).wait()


def finish_kernel(
    dims, partial, spectral, grid_out, spec_out,
    table, turned, stacked, result, spec, out_sem, spec_in, spec_done,
):
    bands, parts, lats, levels, longitudes, slots, depth, half = dims
    devices = bands * parts
    each = 2 * levels
    wide = longitudes // LANES
    south = lax.axis_index("band") >= bands // 2
    block = 1024
    span = block // levels

    def out_copy(w, slot):
        return pltpu.make_async_copy(
            result.at[slot],
            grid_out.at[:, :, aligned(w * 2 * LANES, 2 * LANES)],
            out_sem.at[slot],
        )

    spec_copy = pltpu.make_async_copy(spectral, spec, spec_in)
    spec_copy.start()

    for l in range(levels):
        x = partial[wide, pl.ds(l, LANES // 2, stride=levels), :]
        turned[pl.ds(l, lats, stride=levels), :] = jnp.concatenate([x, x], axis=0).T
    keep = lax.broadcasted_iota(jnp.int32, (levels, LANES), 1) < LANES // 2
    piece = LANES // 2
    for i in range(wide):
        cut = slice(i * LANES, (i + 1) * LANES)
        h, l = [
            partial[wide + 1, (e * wide + i) * piece : (e * wide + i + 1) * piece, :].astype(
                jnp.bfloat16
            )
            for e in range(2)
        ]
        for e, part in enumerate((h, l, h, jnp.zeros_like(h))):
            table[e * piece : (e + 1) * piece, cut] = part

    spec_copy.wait()
    done = pltpu.make_async_copy(spec, spec_out, spec_done)
    done.start()
    burst = 8

    def split(i, carry):
        for e in range(burst):
            r = i * burst + e
            lat = jnp.where(south, lats - 1 - r, r)
            h, l = halves_of(turned[aligned(lat * levels, levels), :])
            to = aligned(r * levels, levels)
            stacked[to, 0:LANES] = h
            stacked[to, LANES : 2 * LANES] = jnp.where(keep, l, jnp.zeros_like(l))
        return carry

    lax.fori_loop(0, lats // burst, split, 0)

    def outer(w, carry):
        slot = lax.rem(w, 2)

        @pl.when(w >= 2)
        def _():
            out_copy(w - 2, slot).wait()

        cut = aligned(w * 2 * LANES, 2 * LANES)
        for m in range(lats // span):
            at = slice(m * block, (m + 1) * block)
            got = dot1(stacked[at, :], table[:, cut], NN)
            for j in range(2):
                x = got[:, j * LANES : (j + 1) * LANES] + partial[2 * w + j, at, :]
                result[slot, m * span : (m + 1) * span, :, j * LANES : (j + 1) * LANES] = (
                    x.reshape(span, levels, LANES)
                )
        out_copy(w, slot).start()
        return carry

    turns = wide // 2
    lax.fori_loop(0, turns, outer, 0)
    for w in range(turns - 2, turns):
        out_copy(w, w % 2).wait()
    done.wait()


def shards(
    grid_adjoint, trajectory, legendre_north, slot_wavenumber, spectral_state,
    to_modes, from_modes, rates,
):
    lats, levels, longitudes = grid_adjoint.shape
    slots, depth, half = legendre_north.shape
    bands = lax.axis_size("band")
    parts = lax.axis_size("lev")
    devices = bands * parts
    every = parts * levels
    fits = (
        lats == LANES and levels == 2 * SUB and 4 * devices == LANES
        and longitudes % (2 * LANES) == 0 and longitudes & (longitudes - 1) == 0
        and bands % 2 == 0 and half == bands // 2 * lats and depth % LANES == 0
        and slots == 4 * GROUP and devices * slots % LANES == 0 and levels // PAIR >= 3 and longitudes <= lats * levels and 2 * every == LANES and to_modes.shape[0] == every
    )
    if not fits:
        return plain_shards(
            grid_adjoint, trajectory, legendre_north, slot_wavenumber, spectral_state,
            to_modes, from_modes, rates,
        )
    dims = (bands, parts, lats, levels, longitudes, slots, depth, half)
    count = devices * slots * 2
    hbm = pl.BlockSpec(memory_space=pl.ANY)
    vmem = pl.BlockSpec(memory_space=pltpu.VMEM)
    f32, bf16 = jnp.float32, jnp.bfloat16
    dma = pltpu.SemaphoreType.DMA
    wide = longitudes // LANES
    numbers = slot_wavenumber.reshape(-1, LANES)
    state = spectral_state.transpose(0, 2, 3, 1).reshape(slots, 2 * every, depth)
    square = pltpu.VMEM((2 * every, 2 * every), f32)
    spectral, _, partial = pl.pallas_call(
        functools.partial(forward_kernel, dims),
        out_shape=(
            jax.ShapeDtypeStruct((slots, 2 * every, depth), f32),
            jax.ShapeDtypeStruct((devices, slots * 2 * levels, lats), f32),
            pltpu.VMEM((wide + 2, lats * levels, LANES), f32),
        ),
        in_specs=[hbm] * 8,
        out_specs=(hbm, hbm, vmem),
        scratch_shapes=[
            pltpu.VMEM((count, longitudes), bf16),
            pltpu.VMEM((count, longitudes), bf16),
            pltpu.VMEM((2, lats // PIECES, SUB, longitudes), f32),
            pltpu.VMEM((2, lats // PIECES, SUB, longitudes), f32),
            pltpu.VMEM((PAIR * lats, longitudes), bf16),
            pltpu.VMEM((PAIR * lats, longitudes), bf16),
            pltpu.VMEM((levels * count * 3 // 2, lats), f32),
            pltpu.VMEM((levels * count, lats), f32),
            pltpu.VMEM((2, depth, half), f32),
            pltpu.VMEM((2, 2 * every, depth), f32),
            pltpu.VMEM((2, 2 * every, depth), f32),
            square, square, square,
            pltpu.VMEM((lats * levels, devices * 2 * GROUP), bf16),
            pltpu.VMEM((lats * levels, devices * 2 * GROUP), bf16),
            pltpu.VMEM((devices * slots, LANES), jnp.int32),
            pltpu.VMEM((count, LANES), jnp.int32),
            square,
            pltpu.VMEM(numbers.shape, jnp.int32),
            pltpu.VMEM((1, every), f32),
            pltpu.VMEM(to_modes.shape, f32),
            pltpu.VMEM(from_modes.shape, f32),
            dma((2,)), dma((2,)), dma, dma((slots // GROUP + 1,)), dma,
            dma((slots,)),
            dma((2,)), dma((2,)), dma((2,)), dma((4,)), dma((4,)),
        ],
        compiler_params=pltpu.CompilerParams(
            collective_id=0, has_side_effects=True, vmem_limit_bytes=GRANT
        ),
        name="spectral",
    )(
        grid_adjoint, trajectory, numbers, legendre_north, state, rates.reshape(1, every),
        to_modes, from_modes,
    )
    grid, spectral = pl.pallas_call(
        functools.partial(finish_kernel, dims),
        out_shape=(
            jax.ShapeDtypeStruct(grid_adjoint.shape, f32),
            jax.ShapeDtypeStruct(spectral.shape, f32),
        ),
        in_specs=[vmem, hbm],
        out_specs=(hbm, hbm),
        scratch_shapes=[
            pltpu.VMEM((2 * LANES, longitudes), bf16),
            pltpu.VMEM((lats * levels, LANES), f32),
            pltpu.VMEM((lats * levels, 2 * LANES), bf16),
            pltpu.VMEM((2, lats, levels, 2 * LANES), f32),
            pltpu.VMEM(spectral.shape, f32),
            dma((2,)), dma, dma,
        ],
        compiler_params=pltpu.CompilerParams(vmem_limit_bytes=LAST_GRANT),
        name="finish",
    )(pltpu.with_memory_space_constraint(partial, pltpu.VMEM), spectral)
    return spectral.reshape(slots, 2, every, depth).transpose(0, 3, 1, 2), grid


def solution(mesh):
    return jax.shard_map(
        shards,
        mesh=mesh,
        in_specs=(
            P("band", "lev", None),
            P("band", "lev", None),
            P(("band", "lev"), None, None),
            P(),
            P(("band", "lev"), None, None, None),
            P(),
            P(),
            P(),
        ),
        out_specs=(P(("band", "lev"), None, None, None), P("band", "lev", None)),
        check_vma=False,
    )
```
